32 devices in a mesh: az: 4 (over y, x), rng: 8 (over z, core).
Axes of the slice: x: 2, y: 2, z: 4, core: 2. Of those that a mesh axis runs over, the one named last changes fastest.
Arguments:
- echoes: bfloat16 [2, 256, 32, 1024], P(None, 'az', None, 'rng'), may hold values from -12 to 12
- arc_start: int32 [64], replicated, may hold values from 0 to 255, as said below
- arc_offsets: int32 [64, 16], replicated, may hold values from 0 to 63, as said below
- doppler_bins: int32 [64, 16], replicated, may hold values from 0 to 31
- steer_angles: float32 [64, 16], replicated, may hold values from -3.140625 to 3.140625
- train_mask: int32 [64, 8], P('az', 'rng'), may hold values from 0 to 1, as said below
Outputs:
- smoothed: float32 [64, 16, 1024], P('az', None, 'rng')
The draws below stay inside these ranges and needn't reach their ends.
Inputs may be any that keep to these rules, and one draw needn't show every extreme that they name: `arc_start`: beam b's arc begins at column (b * 4 - 64 / 2 + j) mod 256 for some j with 0 <= j < 4. `arc_offsets`: each row holds 16 distinct offsets, ascending. `train_mask`: the last block of every beam is a training block.
All inputs are finite; a program needn't handle non-finite values.
Results may differ from the reference program's by a relative error of at most 0.0035.
Values may be sent and summed in bfloat16 or wider, within the bound.
A program may use at most 64 MiB of HBM per device.

```python
import jax
import jax.numpy as jnp
from jax import lax

COLS = 256
PULSES = 32
ARC = 64
SEL = 16
BINS = 3
BEAMS = 64
DBINS = 16
BLK = 128
RANGE = 1024
NBLK = 8


PATCHES = 128


CLUTTER_LEVEL = 2.0


def clutter_steering(patch_key):
    jitter = jax.random.uniform(patch_key, (PATCHES,), jnp.float32, 0.0, 1.0)
    azimuth = 2.0 * jnp.pi * (jnp.arange(PATCHES, dtype=jnp.float32) + jitter) / PATCHES
    col_angle = 2.0 * jnp.pi * jnp.arange(COLS, dtype=jnp.float32) / COLS
    pulse_ids = jnp.arange(PULSES, dtype=jnp.float32)
    spatial = COLS / 2.0 * jnp.cos(col_angle[:, None, None] - azimuth[None, None, :])
    temporal = jnp.pi * jnp.cos(azimuth)[None, None, :] * pulse_ids[None, :, None]
    phase = (spatial + temporal).reshape(COLS * PULSES, PATCHES)
    return (jnp.cos(phase), jnp.sin(phase))


def clutter_field(steer_re, steer_im, amp_re, amp_im):
    real_part = jnp.dot(steer_re, amp_re, precision=lax.Precision.HIGHEST) - jnp.dot(steer_im, amp_im, precision=lax.Precision.HIGHEST)
    imag_part = jnp.dot(steer_re, amp_im, precision=lax.Precision.HIGHEST) + jnp.dot(steer_im, amp_re, precision=lax.Precision.HIGHEST)
    return jnp.stack([real_part, imag_part], 0).reshape(2, COLS, PULSES, RANGE)


def draw_echoes(key, part):
    base_key = jax.random.fold_in(key, 11)
    noise_key = jax.random.fold_in(base_key, 0)
    patch_key = jax.random.fold_in(base_key, 2)
    amp_key = jax.random.fold_in(base_key, 3)
    array_shape = (2, COLS, PULSES, RANGE)
    position = jnp.arange(RANGE, dtype=jnp.float32) / RANGE
    steer_re, steer_im = clutter_steering(patch_key)
    amp_scale = CLUTTER_LEVEL / PATCHES ** 0.5
    amplitudes = jax.random.normal(amp_key, (2, PATCHES, RANGE), jnp.float32) * amp_scale
    noise = jnp.clip(jax.random.normal(noise_key, array_shape, jnp.float32), -5.0, 5.0)
    values = noise + clutter_field(steer_re, steer_im, amplitudes[0], amplitudes[1])
    values = values * jnp.exp(0.6 * position)
    return jnp.clip(values, -12.0, 12.0).astype(jnp.bfloat16)


def draw_arc_start(key, part):
    spacing = COLS // BEAMS
    jitter = jax.random.randint(jax.random.fold_in(key, 12), (BEAMS,), 0, spacing)
    centre = jnp.arange(BEAMS, dtype=jnp.int32) * spacing
    return ((centre - ARC // 2 + jitter) % COLS).astype(jnp.int32)


def draw_arc_offsets(key, part):
    beam_keys = jax.random.split(jax.random.fold_in(key, 13), BEAMS)
    orders = jax.vmap(lambda single: jax.random.permutation(single, ARC))(beam_keys)
    return jnp.sort(orders[:, :SEL], axis=1).astype(jnp.int32)


def draw_train_mask(key, part):
    block_ids = jnp.arange(NBLK, dtype=jnp.int32)
    chance = 25 + 70 * block_ids // max(NBLK - 1, 1)
    rolls = jax.random.randint(jax.random.fold_in(key, 14), (BEAMS, NBLK), 0, 100)
    kept = jnp.where(block_ids[None, :] == NBLK - 1, 1, (rolls < chance[None, :]).astype(jnp.int32))
    return kept.astype(jnp.int32)


def plant(drawn, own_key, low, high):
    extent = drawn.shape
    spot = [jax.random.randint(jax.random.fold_in(own_key, axis), (), 0, extent[axis]) for axis in range(len(extent))]
    drawn = drawn.at[tuple(spot)].set(low)
    longest = extent.index(max(extent))
    spot[longest] = (spot[longest] + 1) % extent[longest]
    return drawn.at[tuple(spot)].set(high)


def setup_inputs(seed: int = 0) -> dict:
    arg_keys = jax.random.split(jax.random.key(seed), 7)
    return {
        "echoes": draw_echoes(jax.random.fold_in(arg_keys[6], 71), 0),
        "arc_start": draw_arc_start(jax.random.fold_in(arg_keys[6], 71), 0),
        "arc_offsets": draw_arc_offsets(jax.random.fold_in(arg_keys[6], 71), 0),
        "doppler_bins": plant(jax.random.randint(arg_keys[3], (BEAMS, DBINS), 0, PULSES), jax.random.fold_in(arg_keys[3], 1), 0, PULSES - 1).astype(jnp.int32),
        "steer_angles": jnp.clip(jax.random.uniform(arg_keys[4], (BEAMS, SEL), jnp.float32, -3.140625, 3.140625), -3.140625, 3.140625),
        "train_mask": draw_train_mask(jax.random.fold_in(arg_keys[6], 71), 0),
    }


LOADING = 0.1

def doppler_table():
    freq_ids = jnp.arange(PULSES, dtype=jnp.int32)
    phase_steps = freq_ids[:, None] * freq_ids[None, :] % PULSES
    phase_angle = -2.0 * jnp.pi / PULSES * phase_steps.astype(jnp.float32)
    return (jnp.cos(phase_angle).astype(jnp.bfloat16), jnp.sin(phase_angle).astype(jnp.bfloat16))

def snapshot(beam_cols, centers, beam_angle, table_re, table_im):
    num_sel = beam_cols.shape[1]
    num_pulses = beam_cols.shape[2]
    num_cells = beam_cols.shape[3]
    num_chan = centers.shape[0]
    bin_ids = ((centers[:, None] + jnp.arange(BINS, dtype=jnp.int32)[None, :] - BINS // 2) % num_pulses).reshape(-1)
    bin_pick = (jnp.arange(num_pulses, dtype=jnp.int32)[None, :] == bin_ids[:, None]).astype(jnp.bfloat16)
    wt_real = jnp.dot(bin_pick.astype(jnp.float32), table_re.astype(jnp.float32), preferred_element_type=jnp.float32).astype(jnp.bfloat16)
    wt_imag = jnp.dot(bin_pick.astype(jnp.float32), table_im.astype(jnp.float32), preferred_element_type=jnp.float32).astype(jnp.bfloat16)
    stacked_table = jnp.concatenate([jnp.concatenate([wt_real, -wt_imag], 1), jnp.concatenate([wt_imag, wt_real], 1)], 0)
    flat_cols = jnp.transpose(beam_cols, (0, 2, 1, 3)).reshape(2 * num_pulses, num_sel * num_cells)
    spectrum = jnp.dot(stacked_table.astype(jnp.float32), flat_cols.astype(jnp.float32), preferred_element_type=jnp.float32).reshape(2, num_chan, BINS, num_sel, num_cells)
    cosine = jnp.cos(beam_angle)[None, None, :, None]
    sine_part = jnp.sin(beam_angle)[None, None, :, None]
    part_real = cosine * spectrum[0] - sine_part * spectrum[1]
    part_imag = sine_part * spectrum[0] + cosine * spectrum[1]
    joined = jnp.concatenate([part_real.reshape(num_chan, BINS * num_sel, num_cells), part_imag.reshape(num_chan, BINS * num_sel, num_cells)], 1)
    return joined.astype(jnp.bfloat16)

def weights_from_blocks(block_a, block_b, train_count):
    dof_size = block_a.shape[0]
    embedded = jnp.concatenate([jnp.concatenate([block_a, -block_b], 1), jnp.concatenate([block_b, block_a], 1)], 0) / train_count
    loading_level = LOADING * jnp.trace(block_a) / (train_count * dof_size)
    embedded = embedded + loading_level * jnp.eye(2 * dof_size, dtype=jnp.float32)
    factor = jnp.linalg.cholesky(embedded)
    steering = (jnp.arange(2 * dof_size, dtype=jnp.int32)[:, None] // dof_size == jnp.arange(2, dtype=jnp.int32)[None, :]).astype(jnp.float32)
    solved = jax.scipy.linalg.cho_solve((factor, True), steering)
    quiescent = jnp.sum(solved[:dof_size, 0])
    return (solved.T.astype(jnp.bfloat16), quiescent)

def reference(echoes, arc_start, arc_offsets, doppler_bins, steer_angles, train_mask):
    table_re, table_im = doppler_table()

    def per_beam(packed):
        start, offsets, centers, beam_angle, mask_row = packed
        col_index = ((start + offsets) % COLS).astype(jnp.int32)
        beam_cols = jnp.take(echoes, col_index, axis=1)
        snapshots = snapshot(beam_cols, centers, beam_angle, table_re, table_im)
        cell_mask = jnp.repeat(mask_row, BLK).astype(jnp.bfloat16)
        train_count = (BLK * jnp.sum(mask_row)).astype(jnp.float32)

        def per_channel(single):
            gram_sum = jnp.dot((single * cell_mask[None, :]).astype(jnp.float32), single.T.astype(jnp.float32), preferred_element_type=jnp.float32)
            dof_size = gram_sum.shape[0] // 2
            block_a = gram_sum[:dof_size, :dof_size] + gram_sum[dof_size:, dof_size:]
            block_b = gram_sum[dof_size:, :dof_size] - gram_sum[:dof_size, dof_size:]
            adapted, quiescent = weights_from_blocks(block_a, block_b, train_count)
            projected = jnp.dot(adapted.astype(jnp.float32), single.astype(jnp.float32), preferred_element_type=jnp.float32)
            return (projected[0] * projected[0] + projected[1] * projected[1]) / quiescent
        return lax.map(per_channel, snapshots)
    power_map = lax.map(per_beam, (arc_start, arc_offsets, doppler_bins, steer_angles, train_mask))
    padded = jnp.pad(power_map, ((0, 0), (0, 0), (1, 1)))
    row_sums = padded[:, :, :-2] + padded[:, :, 1:-1] + padded[:, :, 2:]
    return (jnp.roll(row_sums, 1, 0) + row_sums + jnp.roll(row_sums, -1, 0)) / 9.0
```

```python
import functools

import jax
import jax.numpy as jnp
from jax import lax
from jax.experimental import pallas as pl
from jax.experimental.pallas import tpu as pltpu
from jax.sharding import PartitionSpec as P


COLS = 256
ARC = 64
BINS = 3
BEAMS = 64
BLK = 128
LOADING = 0.1
VMEM_LIMIT = 48 << 20
CHAIN_VMEM = 66_200_000


def doppler_table(num_pulses):
    freq_ids = jnp.arange(num_pulses, dtype=jnp.int32)
    phase_steps = freq_ids[:, None] * freq_ids[None, :] % num_pulses
    phase_angle = -2.0 * jnp.pi / num_pulses * phase_steps.astype(jnp.float32)
    return (jnp.cos(phase_angle).astype(jnp.bfloat16), jnp.sin(phase_angle).astype(jnp.bfloat16))


def snap_gram_kernel(
    col_ref, bins_ref, cos_ref, sin_ref, ext_ref, table_ref, mask_ref, v_ref, gram_ref
):
    beam = pl.program_id(0)
    pulses = ext_ref.shape[2]
    num_sel = col_ref.shape[1]
    num_chan = bins_ref.shape[1]
    table = table_ref[...]
    parts_re, parts_im = [], []
    for j in range(num_sel):
        col = col_ref[beam, j]
        data = jnp.concatenate([ext_ref[0, col], ext_ref[1, col]], axis=0)
        spec = jnp.dot(table, data, preferred_element_type=jnp.float32)
        cosine = cos_ref[beam, j]
        sine = sin_ref[beam, j]
        spec_re = spec[:pulses]
        spec_im = spec[pulses:]
        parts_re.append(cosine * spec_re - sine * spec_im)
        parts_im.append(sine * spec_re + cosine * spec_im)
    for part, pieces in enumerate((parts_re, parts_im)):
        stacked = jnp.swapaxes(jnp.stack(pieces, 0), 0, 1)
        v_ref[0, part] = stacked.astype(jnp.bfloat16)
    dof = BINS * num_sel
    mask_row = mask_ref[0]
    row = lax.broadcasted_iota(jnp.int32, (dof, dof), 0)
    colm = lax.broadcasted_iota(jnp.int32, (dof, dof), 1)
    lower = row >= colm
    packed = []
    for k in range(num_chan):
        centre = bins_ref[beam, k]
        ids = [(centre + (q - BINS // 2 + pulses)) % pulses for q in range(BINS)]
        u_re = jnp.concatenate([v_ref[0, 0, f] for f in ids], 0)
        u_im = jnp.concatenate([v_ref[0, 1, f] for f in ids], 0)
        right = jnp.concatenate([u_re, u_im], 1)
        m_re = u_re * mask_row
        m_im = u_im * mask_row
        left = jnp.concatenate(
            [jnp.concatenate([m_re, m_im], 1), jnp.concatenate([m_im, -m_re], 1)], 0
        )
        both = lax.dot_general(
            left, right, (((1,), (1,)), ((), ())), preferred_element_type=jnp.float32
        )
        packed.append(jnp.where(lower, both[:dof], both[dof:]))
    gram_ref[0] = jnp.concatenate(packed, 1)


def solve_kernel(part_ref, out_ref, stack, turned, hr, hi, xr, xi):
    lead, dof, wide = part_ref.shape
    width = wide // dof
    lanes = lead * width
    nb = dof // 8
    group = min(8, lanes)
    for g in range(0, lanes, group):
        pieces = []
        for item in range(g, g + group):
            k = item % width
            pieces.append(part_ref[item // width, :, k * dof : (k + 1) * dof])
        stack[:, g : g + group, :] = jnp.swapaxes(jnp.stack(pieces, 0), 0, 1)
    for i in range(dof):
        turned[i] = stack[i].T
    trace = jnp.zeros((1, lanes), jnp.float32)
    for i in range(dof):
        trace = trace + turned[i, i : i + 1, :]
    load = (LOADING / dof) * trace
    cube = (8, 8, lanes)
    row = lax.broadcasted_iota(jnp.int32, cube, 0)
    col = lax.broadcasted_iota(jnp.int32, cube, 1)
    for ib in range(nb):
        rows = slice(8 * ib, 8 * ib + 8)
        for jb in range(ib, nb):
            cols = slice(8 * jb, 8 * jb + 8)
            imag = turned[rows, cols, :]
            real = jnp.swapaxes(turned[cols, rows, :], 0, 1)
            if ib == jb:
                straight, flip = imag, real
                real = jnp.where(row >= col, straight, flip)
                real = jnp.where(row == col, real + load[None], real)
                imag = jnp.where(row < col, straight, jnp.where(row > col, -flip, 0.0))
            hr[rows, cols, :] = real
            hi[rows, cols, :] = imag
    hr[:, dof:, :] = jnp.ones((dof, 8, lanes), jnp.float32)
    hi[:, dof:, :] = jnp.zeros((dof, 8, lanes), jnp.float32)
    xr[...] = jnp.zeros_like(xr)
    xi[...] = jnp.zeros_like(xi)
    sub = lax.broadcasted_iota(jnp.int32, (8, lanes), 0)

    for kb in range(nb):

        def step(k, carry, kb=kb):
            pivot = 1.0 / hr[k, pl.ds(k, 1), :]
            rr = [hr[k, 8 * b : 8 * b + 8, :] for b in range(kb, nb + 1)]
            ri = [hi[k, 8 * b : 8 * b + 8, :] for b in range(kb, nb + 1)]
            for ib in range(kb, nb):
                fr = rr[ib - kb] * pivot
                fi = -ri[ib - kb] * pivot
                if ib == kb:
                    live = sub + 8 * kb > k
                    fr = jnp.where(live, fr, 0.0)
                    fi = jnp.where(live, fi, 0.0)
                for s in range(8):
                    i = 8 * ib + s
                    cr = jnp.broadcast_to(fr[s : s + 1], (8, lanes))
                    ci = jnp.broadcast_to(fi[s : s + 1], (8, lanes))
                    for b in range(ib, nb + 1):
                        pr, pi = rr[b - kb], ri[b - kb]
                        sl = slice(8 * b, 8 * b + 8)
                        hr[i, sl, :] = hr[i, sl, :] - (cr * pr - ci * pi)
                        hi[i, sl, :] = hi[i, sl, :] - (cr * pi + ci * pr)
            return carry

        lax.fori_loop(8 * kb, 8 * kb + 8, step, 0)

    for ib in reversed(range(nb)):

        def back(t, carry, ib=ib):
            i = 8 * ib + 7 - t
            sr = jnp.zeros((8, lanes), jnp.float32)
            si = jnp.zeros((8, lanes), jnp.float32)
            for b in range(ib, nb):
                sl = slice(8 * b, 8 * b + 8)
                ar, ai = hr[i, sl, :], hi[i, sl, :]
                br, bi = xr[sl, :], xi[sl, :]
                sr = sr + (ar * br - ai * bi)
                si = si + (ar * bi + ai * br)
            pivot = 1.0 / hr[i, pl.ds(i, 1), :]
            top_r = hr[i, dof : dof + 1, :]
            top_i = hi[i, dof : dof + 1, :]
            xr[pl.ds(i, 1), :] = (top_r - jnp.sum(sr, 0, keepdims=True)) * pivot
            xi[pl.ds(i, 1), :] = (top_i - jnp.sum(si, 0, keepdims=True)) * pivot
            return carry

        lax.fori_loop(0, 8, back, 0)
    out_ref[:dof, :lanes] = xr[...]
    out_ref[dof : 2 * dof, :lanes] = xi[...]
    out_ref[2 * dof : 2 * dof + 8, :lanes] = jnp.broadcast_to(
        jnp.sum(xr[...], 0, keepdims=True), (8, lanes)
    )


MESH = pl.DeviceIdType.MESH


def scatter_kernel(n, halves, *refs):
    g_refs = refs[:halves]
    out_ref, pair, acc, right, left, psend, precv, rsend, rrecv, lsend, lrecv = refs[halves:]
    share = n // halves

    def own(t, core):
        return g_refs[t // share].at[2 * (t % share) + core]

    me = lax.axis_index("rng")
    z = me // 2
    c = me % 2
    mate = 2 * z + 1 - c
    ahead = lax.rem(me + 2, 2 * n)
    behind = lax.rem(me + 2 * n - 2, 2 * n)
    barrier = pltpu.get_barrier_semaphore()
    pl.semaphore_signal(barrier, inc=1, device_id={"rng": mate}, device_id_type=MESH)
    pl.semaphore_signal(barrier, inc=1, device_id={"rng": ahead}, device_id_type=MESH)
    pl.semaphore_signal(barrier, inc=1, device_id={"rng": behind}, device_id_type=MESH)
    pl.semaphore_wait(barrier, 3)

    order = []
    for t in range((n + 1) // 2):
        order.append(n - 1 - t)
        if t != n - 1 - t:
            order.append(t)

    def pair_copy(t):
        return pltpu.make_async_remote_copy(
            src_ref=own(t, 1 - c),
            dst_ref=pair.at[t],
            send_sem=psend.at[t],
            recv_sem=precv.at[t],
            device_id={"rng": mate},
            device_id_type=MESH,
        )

    def right_copy(t):
        return pltpu.make_async_remote_copy(
            src_ref=acc.at[t],
            dst_ref=right.at[t],
            send_sem=rsend.at[t],
            recv_sem=rrecv.at[t],
            device_id={"rng": ahead},
            device_id_type=MESH,
        )

    def left_copy(t):
        return pltpu.make_async_remote_copy(
            src_ref=acc.at[t],
            dst_ref=left.at[t],
            send_sem=lsend.at[t],
            recv_sem=lrecv.at[t],
            device_id={"rng": behind},
            device_id_type=MESH,
        )

    for t in order:
        pair_copy(t).start()
    for t in order:
        pair_copy(t).wait_recv()
        acc[t] = own(t, c)[...] + pair[t]

        @pl.when(jnp.logical_and(z == 0, t > 0))
        def _(t=t):
            right_copy(t).start()

        @pl.when(jnp.logical_and(z == n - 1, t < n - 1))
        def _(t=t):
            left_copy(t).start()

    for place in range(n):
        events = [(place + n - 1 - t, 0, t) for t in range(place + 1, n) if place > 0]
        events += [(n - 1 - place + t, 1, t) for t in range(place) if place < n - 1]

        @pl.when(z == place)
        def _(place=place, events=sorted(events)):
            for _, side, t in events:
                copy = left_copy(t) if side else right_copy(t)
                source = left if side else right
                copy.wait_recv()
                acc[t] = acc[t] + source[t]
                copy.start()
            total = acc[place]
            if place > 0:
                right_copy(place).wait_recv()
                total = total + right[place]
            if place < n - 1:
                left_copy(place).wait_recv()
                total = total + left[place]
            out_ref[...] = total

    for t in range(n):
        pair_copy(t).wait_send()

        @pl.when(z < t)
        def _(t=t):
            right_copy(t).wait_send()

        @pl.when(z > t)
        def _(t=t):
            left_copy(t).wait_send()


def apply_kernel(
    halves,
    per,
    dof,
    pay_ref,
    bins_ref,
    *refs,
):
    v_refs = refs[:halves]
    (out_ref, v_all, gat, power, edge, halo, sums, az_lo, az_hi) = refs[halves : halves + 9]
    (vsem, gsend, grecv, esend, erecv, asend, arecv) = refs[halves + 9 :]
    me = lax.axis_index("rng")
    az = lax.axis_index("az")
    n = lax.axis_size("rng")
    m = lax.axis_size("az")
    beams, num_chan, cells = out_ref.shape
    pulses, num_sel = v_all.shape[2], v_all.shape[3]
    taps = pulses * num_sel
    az_next = lax.rem(az + 1, m)
    az_prev = lax.rem(az + m - 1, m)
    barrier = pltpu.get_barrier_semaphore()
    for d in range(1, n):
        peer = lax.rem(me + d, n)
        pl.semaphore_signal(barrier, inc=1, device_id={"rng": peer}, device_id_type=MESH)
    for other in (az_next, az_prev):
        pl.semaphore_signal(barrier, inc=1, device_id={"az": other}, device_id_type=MESH)
    share = beams // halves
    loads = []
    for h in range(halves):
        load = pltpu.make_async_copy(v_refs[h], v_all.at[pl.ds(h * share, share)], vsem.at[h])
        load.start()
        loads.append(load)
    pl.semaphore_wait(barrier, n + 1)

    copies = []
    for d in range(1, n):
        peer = lax.rem(me + d, n)
        copy = pltpu.make_async_remote_copy(
            src_ref=pay_ref,
            dst_ref=gat.at[me],
            send_sem=gsend.at[d],
            recv_sem=grecv.at[d],
            device_id={"rng": peer},
            device_id_type=MESH,
        )
        copy.start()
        copies.append(copy)
    gat[me] = pay_ref[...]
    for load in loads:
        load.wait()
    for copy in copies:
        copy.wait_recv()
    rows = gat.shape[1] - beams
    count = jnp.zeros((beams, gat.shape[2]), jnp.float32)
    for r in range(n):
        count = count + gat[r, rows:, :]
    sums[0] = jnp.zeros(sums.shape[1:], jnp.float32)
    for b in range(beams):
        sums[b, :1, :] = count[b : b + 1]
    freq = lax.broadcasted_iota(jnp.int32, (num_chan, taps), 1) // num_sel
    lanes = gat.shape[2]
    lane = lax.broadcasted_iota(jnp.int32, (num_chan, lanes), 1)

    def one(b, carry):
        if per >= num_chan:
            ratio = per // num_chan
            start = pl.multiple_of((b % ratio) * num_chan, 8)
            w = gat[b // ratio, pl.ds(start, num_chan), :]
        else:
            split = num_chan // per
            w = jnp.concatenate([gat[b * split + t, :per, :] for t in range(split)], 0)
        w = w * sums[b, :1, :]
        quiet = w[:, 2 * dof : 2 * dof + 1]
        centre = bins_ref[b]
        planes = []
        hits = []
        for q in range(BINS):
            f = lax.rem(centre + (q - BINS // 2 + pulses), pulses)
            hits.append(freq == f)
        for part in range(2):
            plane = jnp.zeros((num_chan, taps), jnp.float32)
            for q in range(BINS):
                start = part * dof + q * num_sel
                piece = pltpu.roll(w, (lanes - start) % lanes, 1) if start else w
                piece = jnp.where(lane < num_sel, piece, 0.0)
                span = num_sel
                while span < lanes:
                    piece = piece + pltpu.roll(piece, span, 1)
                    span *= 2
                tiled = jnp.concatenate([piece] * (taps // lanes), 1)
                plane = jnp.where(hits[q], tiled, plane)
            planes.append(plane)
        top = jnp.concatenate([planes[0], planes[1]], 1)
        low = jnp.concatenate([-planes[1], planes[0]], 1)
        lhs = jnp.concatenate([top, low], 0).astype(jnp.bfloat16)
        flat = v_all[b].reshape(2 * taps, cells)
        proj = jnp.dot(lhs, flat, preferred_element_type=jnp.float32)
        p0 = proj[:num_chan]
        p1 = proj[num_chan:]
        power[b] = (p0 * p0 + p1 * p1) / quiet
        return carry

    lax.fori_loop(0, beams, one, 0)
    items = beams * num_chan
    turned = power[...].reshape(items, cells).T
    edge[0] = turned[:8]
    edge[1] = turned[cells - 8 :]

    def edge_copy(side):
        target = lax.rem(me + 1, n) if side else lax.rem(me + n - 1, n)
        return pltpu.make_async_remote_copy(
            src_ref=edge.at[side],
            dst_ref=halo.at[side],
            send_sem=esend.at[side],
            recv_sem=erecv.at[side],
            device_id={"rng": target},
            device_id_type=MESH,
        )

    for side in range(2):
        edge_copy(side).start()
    for side in range(2):
        edge_copy(side).wait()
    before = jnp.where(me > 0, halo[1, 7:8], 0.0)
    after = jnp.where(me < n - 1, halo[0, 0:1], 0.0)
    turned = (
        jnp.concatenate([before, turned[:-1]], 0)
        + turned
        + jnp.concatenate([turned[1:], after], 0)
    )
    sums[...] = turned.T.reshape(beams, num_chan, cells)
    up = pltpu.make_async_remote_copy(
        src_ref=sums.at[beams - 1],
        dst_ref=az_lo,
        send_sem=asend.at[0],
        recv_sem=arecv.at[0],
        device_id={"az": az_next},
        device_id_type=MESH,
    )
    down = pltpu.make_async_remote_copy(
        src_ref=sums.at[0],
        dst_ref=az_hi,
        send_sem=asend.at[1],
        recv_sem=arecv.at[1],
        device_id={"az": az_prev},
        device_id_type=MESH,
    )
    up.start()
    down.start()
    for b in range(1, beams - 1):
        out_ref[b] = (sums[b - 1] + sums[b] + sums[b + 1]) / 9.0
    up.wait_recv()
    down.wait_recv()
    out_ref[0] = (az_lo[...] + sums[0] + sums[1]) / 9.0
    out_ref[beams - 1] = (sums[beams - 2] + sums[beams - 1] + az_hi[...]) / 9.0
    up.wait_send()
    down.wait_send()
    for copy in copies:
        copy.wait_send()


def gram_of(v_ref, beam, bins, mask_row):
    pulses = v_ref.shape[2]
    num_sel = v_ref.shape[3]
    dof = BINS * num_sel
    row = lax.broadcasted_iota(jnp.int32, (dof, dof), 0)
    colm = lax.broadcasted_iota(jnp.int32, (dof, dof), 1)
    lower = row >= colm
    packed = []
    for centre in bins:
        ids = [lax.rem(centre + (q - BINS // 2 + pulses), pulses) for q in range(BINS)]
        u_re = jnp.concatenate([v_ref[beam, 0, f] for f in ids], 0)
        u_im = jnp.concatenate([v_ref[beam, 1, f] for f in ids], 0)
        right = jnp.concatenate([u_re, u_im], 1)
        m_re = u_re * mask_row
        m_im = u_im * mask_row
        left = jnp.concatenate(
            [jnp.concatenate([m_re, m_im], 1), jnp.concatenate([m_im, -m_re], 1)], 0
        )
        both = lax.dot_general(
            left, right, (((1,), (1,)), ((), ())), preferred_element_type=jnp.float32
        )
        packed.append(jnp.where(lower, both[:dof], both[dof:]))
    return packed


def chain_kernel(
    early,
    start_ref,
    offs_ref,
    bins_ref,
    cos_ref,
    sin_ref,
    echoes,
    table_ref,
    mask_ref,
    chan_ref,
    out_ref,
    ext,
    low,
    high,
    v_all,
    gram,
    pair,
    acc,
    ring,
    direct,
    part,
    solved,
    stack,
    turned,
    hr,
    hi,
    xr,
    xi,
    masks,
    counts,
    pay,
    gat_e,
    gat_l,
    wts_e,
    wts_l,
    pw,
    pl_left,
    pl_right,
    rows,
    esem,
    hsend,
    hrecv,
    psend,
    precv,
    rsend,
    rrecv,
    dsend,
    drecv,
    msend,
    mrecv,
    gsend,
    grecv_e,
    grecv_l,
    lsend,
    lrecv,
    tsend,
    trecv,
    asend,
    arecv,
):
    me = lax.axis_index("rng")
    az = lax.axis_index("az")
    size = lax.axis_size("rng")
    m = lax.axis_size("az")
    n = size // 2
    z = me // 2
    c = lax.rem(me, 2)
    beams, num_chan, cells = out_ref.shape
    columns = echoes.shape[1]
    pulses = echoes.shape[2]
    num_sel = offs_ref.shape[0]
    dof = BINS * num_sel
    taps = pulses * num_sel
    steps = beams // 2
    late = steps - early
    width = ARC // 2
    w = width // steps
    side_chan = num_chan // 2
    az_next = lax.rem(az + 1, m)
    az_prev = lax.rem(az + m - 1, m)
    ahead = lax.rem(me + 1, size)
    behind = lax.rem(me + size - 1, size)
    mid_l = n // 2 - 1
    mid_r = n // 2
    is_end = jnp.logical_or(z == 0, z == n - 1)
    is_mid = jnp.logical_or(z == mid_l, z == mid_r)

    own_cols = pltpu.make_async_copy(echoes, ext.at[:, width : width + columns], esem)
    own_cols.start()
    pl_left[...] = jnp.zeros(pl_left.shape, jnp.float32)
    pl_right[...] = jnp.zeros(pl_right.shape, jnp.float32)
    barrier = pltpu.get_barrier_semaphore()
    for d in range(1, size):
        peer = lax.rem(me + d, size)
        pl.semaphore_signal(barrier, inc=1, device_id={"rng": peer}, device_id_type=MESH)
    for other in (az_next, az_prev):
        pl.semaphore_signal(barrier, inc=1, device_id={"az": other}, device_id_type=MESH)
        for r in (ahead, behind):
            pl.semaphore_signal(
                barrier, inc=1, device_id={"az": other, "rng": r}, device_id_type=MESH
            )
    pl.semaphore_wait(barrier, size + 5)

    def low_copy(i):
        return pltpu.make_async_remote_copy(
            src_ref=echoes.at[:, pl.ds(columns - w * (i + 1), w)],
            dst_ref=low.at[i],
            send_sem=hsend.at[0, i],
            recv_sem=hrecv.at[0, i],
            device_id={"az": az_next},
            device_id_type=MESH,
        )

    def high_copy(i):
        return pltpu.make_async_remote_copy(
            src_ref=echoes.at[:, pl.ds(w * i, w)],
            dst_ref=high.at[i],
            send_sem=hsend.at[1, i],
            recv_sem=hrecv.at[1, i],
            device_id={"az": az_prev},
            device_id_type=MESH,
        )

    for i in range(steps):
        low_copy(i).start()
        high_copy(i).start()

    def mask_copy(d):
        return pltpu.make_async_remote_copy(
            src_ref=mask_ref,
            dst_ref=masks.at[me],
            send_sem=msend.at[d],
            recv_sem=mrecv.at[me],
            device_id={"rng": lax.rem(me + d, size)},
            device_id_type=MESH,
        )

    for d in range(1, size):
        mask_copy(d).start()
    masks[me] = mask_ref[...]

    part[...] = jnp.zeros(part.shape, jnp.float32)
    solved[...] = jnp.zeros(solved.shape, jnp.float32)
    own_cols.wait()

    def mine(t):
        return jnp.where(c == 0, steps - 1 - t, steps + t)

    def pair_copy(t):
        return pltpu.make_async_remote_copy(
            src_ref=gram.at[jnp.where(c == 0, steps + t, steps - 1 - t)],
            dst_ref=pair.at[t],
            send_sem=psend.at[t],
            recv_sem=precv.at[t],
            device_id={"rng": 2 * z + 1 - c},
            device_id_type=MESH,
        )

    def ring_copy(side, t):
        target = lax.rem(me + 2, size) if side else lax.rem(me + size - 2, size)
        return pltpu.make_async_remote_copy(
            src_ref=acc.at[t, side],
            dst_ref=ring.at[side, t],
            send_sem=rsend.at[side, t],
            recv_sem=rrecv.at[side, t],
            device_id={"rng": target},
            device_id_type=MESH,
        )

    def direct_copy(side, t, source):
        owner = 2 * (mid_r if side else mid_l) + c
        return pltpu.make_async_remote_copy(
            src_ref=acc.at[t, side],
            dst_ref=direct.at[t - early, source],
            send_sem=dsend.at[t - early, side],
            recv_sem=drecv.at[t - early, source],
            device_id={"rng": owner},
            device_id_type=MESH,
        )

    table = table_ref[...]

    def one_beam(b):
        bg = az * beams + b
        first = lax.rem(start_ref[bg] - az * columns + (width + COLS), COLS)
        first = jnp.minimum(first, ext.shape[1] - ARC)
        parts_re, parts_im = [], []
        for j in range(num_sel):
            col = first + offs_ref[j, bg]
            data = jnp.concatenate([ext[0, col], ext[1, col]], axis=0)
            spec = jnp.dot(table, data, preferred_element_type=jnp.float32)
            cosine = cos_ref[j, bg]
            sine = sin_ref[j, bg]
            spec_re = spec[:pulses]
            spec_im = spec[pulses:]
            parts_re.append(cosine * spec_re - sine * spec_im)
            parts_im.append(sine * spec_re + cosine * spec_im)
        for p, pieces in enumerate((parts_re, parts_im)):
            stacked = jnp.swapaxes(jnp.stack(pieces, 0), 0, 1)
            v_all[b, p] = stacked.astype(jnp.bfloat16)
        mask_row = mask_ref[pl.ds(b, 1), :].astype(jnp.bfloat16)
        bins = [bins_ref[k, bg] for k in range(num_chan)]
        packed = gram_of(v_all, b, bins, mask_row)
        gram[b, 0] = jnp.concatenate(packed[:side_chan], 1)
        gram[b, 1] = jnp.concatenate(packed[side_chan:], 1)

    def slot(s, carry):
        @pl.when(s < steps)
        def _():
            low_copy(s).wait_recv()
            high_copy(s).wait_recv()
            ext[:, pl.ds(width - w * (s + 1), w)] = low[s]
            ext[:, pl.ds(width + columns + w * s, w)] = high[s]

            def two(i, carry):
                one_beam(jnp.where(i == 0, steps - 1 - s, steps + s))
                return carry

            lax.fori_loop(0, 2, two, 0)
            pair_copy(s).start()

        t = s - 1

        @pl.when(jnp.logical_and(t >= 0, t < steps))
        def _():
            pair_copy(t).wait_recv()
            own = mine(t)
            acc[t] = gram[own] + pair[t]

            @pl.when(t < early)
            def _():
                @pl.when(z == 0)
                def _():
                    ring_copy(1, t).start()

                @pl.when(z == n - 1)
                def _():
                    ring_copy(0, t).start()

            @pl.when(t >= early)
            def _():
                for side, owner in ((0, mid_l), (1, mid_r)):

                    @pl.when(z != owner)
                    def _(side=side):
                        direct_copy(side, t, z).start()

        for side in range(2):
            place = z if side else n - 1 - z
            tt = s - 1 - place

            @pl.when(jnp.logical_and(place > 0, jnp.logical_and(tt >= 0, tt < early)))
            def _(side=side, place=place, tt=tt):
                ring_copy(side, tt).wait_recv()
                total = acc[tt, side] + ring[side, tt]

                @pl.when(place < n - 1)
                def _():
                    acc[tt, side] = total
                    ring_copy(side, tt).start()

                @pl.when(place == n - 1)
                def _():
                    part[tt] = total

        return carry

    lax.fori_loop(0, max(steps + 1, early + n), slot, 0)

    for side, owner in ((0, mid_l), (1, mid_r)):

        @pl.when(z == owner)
        def _(side=side, owner=owner):
            for i in range(late):
                total = acc[early + i, side]
                for source in range(n):
                    if source != owner:
                        direct_copy(side, early + i, source).wait_recv()
                        total = total + direct[i, source]
                part[i] = total

    for d in range(1, size):
        src = lax.rem(me + d, size)
        pltpu.make_async_remote_copy(
            src_ref=mask_ref,
            dst_ref=masks.at[src],
            send_sem=msend.at[d],
            recv_sem=mrecv.at[src],
            device_id={"rng": src},
            device_id_type=MESH,
        ).wait_recv()
    all_masks = masks[0]
    for r in range(1, size):
        all_masks = all_masks + masks[r]
    counts[...] = jnp.broadcast_to(jnp.sum(all_masks, 1, keepdims=True), counts.shape)

    solve_kernel(part, solved, stack, turned, hr, hi, xr, xi)
    lanes = pay.shape[1]
    flipped = solved[...].T
    items = early * side_chan
    scaled = []
    for t in range(early):
        tt = jnp.where(is_mid, early + jnp.minimum(t, late - 1), t)
        scaled.append(
            flipped[side_chan * t : side_chan * (t + 1)] * counts[pl.ds(mine(tt), 1), :]
        )
    full = jnp.concatenate(scaled, 0)
    lane = lax.broadcasted_iota(jnp.int32, (items, lanes), 1)
    hi_part = full.astype(jnp.bfloat16).astype(jnp.float32)
    rest = full - hi_part
    mid_part = rest.astype(jnp.bfloat16).astype(jnp.float32)
    lo_part = rest - mid_part
    coded = jnp.where(
        lane == 2 * dof + 1, mid_part, jnp.where(lane == 2 * dof + 2, lo_part, hi_part)
    )
    pay[...] = coded.astype(jnp.bfloat16)

    def end_copy(d, side):
        return pltpu.make_async_remote_copy(
            src_ref=pay,
            dst_ref=gat_e.at[side, c],
            send_sem=gsend.at[d],
            recv_sem=grecv_e.at[side, c],
            device_id={"rng": lax.rem(me + d, size)},
            device_id_type=MESH,
        )

    def mid_copy(d, side):
        return pltpu.make_async_remote_copy(
            src_ref=pay.at[: late * side_chan],
            dst_ref=gat_l.at[side, c],
            send_sem=gsend.at[d],
            recv_sem=grecv_l.at[side, c],
            device_id={"rng": lax.rem(me + d, size)},
            device_id_type=MESH,
        )

    for side, owner in ((0, 0), (1, n - 1)):

        @pl.when(z == owner)
        def _(side=side):
            for d in range(1, size):
                end_copy(d, side).start()
            gat_e[side, c] = pay[...]

    for side, owner in ((0, mid_l), (1, mid_r)):

        @pl.when(z == owner)
        def _(side=side):
            for d in range(1, size):
                mid_copy(d, side).start()
            gat_l[side, c] = pay[: late * side_chan]

    freq = (lax.broadcasted_iota(jnp.int32, (num_chan, taps), 1) // num_sel).astype(jnp.float32)
    blane = lax.broadcasted_iota(jnp.int32, chan_ref.shape, 1)
    wlane = lax.broadcasted_iota(jnp.int32, (num_chan, lanes), 1)

    def tile_copy(side, b):
        target = ahead if side else behind
        buf = pl_left if side else pl_right
        return pltpu.make_async_remote_copy(
            src_ref=pw.at[b + 1],
            dst_ref=buf.at[b + 1],
            send_sem=lsend.at[side, b],
            recv_sem=lrecv.at[side, b],
            device_id={"rng": target},
            device_id_type=MESH,
        )

    def az_copy(up):
        return pltpu.make_async_remote_copy(
            src_ref=pw.at[beams if up else 1],
            dst_ref=pw.at[0 if up else beams + 1],
            send_sem=tsend.at[up],
            recv_sem=trecv.at[up],
            device_id={"az": az_next if up else az_prev},
            device_id_type=MESH,
        )

    def corner_copy(up, side):
        buf = pl_left if side else pl_right
        return pltpu.make_async_remote_copy(
            src_ref=pw.at[beams if up else 1],
            dst_ref=buf.at[0 if up else beams + 1],
            send_sem=asend.at[up, side],
            recv_sem=arecv.at[up, side],
            device_id={
                "az": az_next if up else az_prev,
                "rng": ahead if side else behind,
            },
            device_id_type=MESH,
        )

    def one_power(b, wt):
        quiet = wt[:, 2 * dof : 2 * dof + 1]
        quiet = quiet + wt[:, 2 * dof + 1 : 2 * dof + 2] + wt[:, 2 * dof + 2 : 2 * dof + 3]
        centre = jnp.sum(
            jnp.where(blane == az * beams + b, chan_ref[...], 0.0), 1, keepdims=True
        )
        hits = []
        for q in range(BINS):
            f = centre + (q - BINS // 2)
            f = jnp.where(f < 0.0, f + pulses, jnp.where(f >= pulses, f - pulses, f))
            hits.append(freq == f)
        planes = []
        for p in range(2):
            plane = jnp.zeros((num_chan, taps), jnp.float32)
            for q in range(BINS):
                start = p * dof + q * num_sel
                piece = pltpu.roll(wt, (lanes - start) % lanes, 1) if start else wt
                piece = jnp.where(wlane < num_sel, piece, 0.0)
                span = num_sel
                while span < lanes:
                    piece = piece + pltpu.roll(piece, span, 1)
                    span *= 2
                tiled = jnp.concatenate([piece] * (taps // lanes), 1)
                plane = jnp.where(hits[q], tiled, plane)
            planes.append(plane)
        top = jnp.concatenate([planes[0], planes[1]], 1)
        bottom = jnp.concatenate([-planes[1], planes[0]], 1)
        lhs = jnp.concatenate([top, bottom], 0).astype(jnp.bfloat16)
        flat = v_all[b].reshape(2 * taps, cells)
        proj = jnp.dot(lhs, flat, preferred_element_type=jnp.float32)
        p0 = proj[:num_chan]
        p1 = proj[num_chan:]
        pw[b + 1] = (p0 * p0 + p1 * p1) / quiet

        @pl.when(me < size - 1)
        def _():
            tile_copy(1, b).start()

        @pl.when(me > 0)
        def _():
            tile_copy(0, b).start()

    def gathered(sem, buf, side, owner, copy):
        for core in range(2):

            @pl.when(me != 2 * owner + core)
            def _(core=core):
                pltpu.make_async_remote_copy(
                    src_ref=copy,
                    dst_ref=buf.at[side, core],
                    send_sem=gsend.at[0],
                    recv_sem=sem.at[side, core],
                    device_id={"rng": ahead},
                    device_id_type=MESH,
                ).wait_recv()

    gathered(grecv_e, gat_e, 0, 0, pay)
    gathered(grecv_e, gat_e, 1, n - 1, pay)
    wts_e[...] = gat_e[...].astype(jnp.float32)

    def weights(buf, i, core):
        start = pl.multiple_of(i * side_chan, side_chan)
        return jnp.concatenate(
            [buf[0, core, pl.ds(start, side_chan), :], buf[1, core, pl.ds(start, side_chan), :]], 0
        )

    def early_power(i, carry):
        t = i // 2
        core = lax.rem(i, 2)
        one_power(jnp.where(core == 0, steps - 1 - t, steps + t), weights(wts_e, t, core))
        return carry

    lax.fori_loop(0, 2 * early, early_power, 0)
    short = pay.at[: late * side_chan]
    gathered(grecv_l, gat_l, 0, mid_l, short)
    gathered(grecv_l, gat_l, 1, mid_r, short)
    wts_l[...] = gat_l[...].astype(jnp.float32)

    def late_power(i, carry):
        t = late - 1 - i // 2
        core = lax.rem(i, 2)
        one_power(
            jnp.where(core == 0, late - 1 - t, steps + early + t), weights(wts_l, t, core)
        )

        @pl.when(i == 0)
        def _():
            az_copy(0).start()

            @pl.when(me < size - 1)
            def _():
                corner_copy(0, 1).start()

            @pl.when(me > 0)
            def _():
                corner_copy(0, 0).start()

        @pl.when(i == 1)
        def _():
            az_copy(1).start()

            @pl.when(me < size - 1)
            def _():
                corner_copy(1, 1).start()

            @pl.when(me > 0)
            def _():
                corner_copy(1, 0).start()

        return carry

    lax.fori_loop(0, 2 * late, late_power, 0)

    lane = lax.broadcasted_iota(jnp.int32, (num_chan, cells), 1)

    def row_sum(i):
        mid = pw[i]
        back = pltpu.roll(jnp.where(lane == cells - 1, pl_left[i], mid), 1, 1)
        fore = pltpu.roll(jnp.where(lane == 0, pl_right[i], mid), cells - 1, 1)
        return back + mid + fore

    for b in range(beams):

        @pl.when(me > 0)
        def _(b=b):
            tile_copy(1, b).wait_recv()

        @pl.when(me < size - 1)
        def _(b=b):
            tile_copy(0, b).wait_recv()

    for b in range(beams):
        rows[b + 1] = row_sum(b + 1)
    for b in range(1, beams - 1):
        out_ref[b] = (rows[b] + rows[b + 1] + rows[b + 2]) / 9.0
    for up in range(2):
        az_copy(up).wait_recv()

        @pl.when(me > 0)
        def _(up=up):
            corner_copy(up, 1).wait_recv()

        @pl.when(me < size - 1)
        def _(up=up):
            corner_copy(up, 0).wait_recv()

    out_ref[0] = (row_sum(0) + rows[1] + rows[2]) / 9.0
    out_ref[beams - 1] = (rows[beams - 1] + rows[beams] + row_sum(beams + 1)) / 9.0

    for i in range(steps):
        low_copy(i).wait_send()
        high_copy(i).wait_send()
        pair_copy(i).wait_send()
    for i in range(early):

        @pl.when(z < n - 1)
        def _(i=i):
            ring_copy(1, i).wait_send()

        @pl.when(z > 0)
        def _(i=i):
            ring_copy(0, i).wait_send()

    for i in range(late):
        for side, owner in ((0, mid_l), (1, mid_r)):

            @pl.when(z != owner)
            def _(side=side, i=i):
                direct_copy(side, early + i, z).wait_send()

    for d in range(1, size):
        mask_copy(d).wait_send()

        @pl.when(is_end)
        def _(d=d):
            end_copy(d, 0).wait_send()

        @pl.when(is_mid)
        def _(d=d):
            mid_copy(d, 0).wait_send()

    for up in range(2):
        az_copy(up).wait_send()

    for side in range(2):

        @pl.when(me < size - 1 if side else me > 0)
        def _(side=side):
            for b in range(beams):
                tile_copy(side, b).wait_send()
            for up in range(2):
                corner_copy(up, side).wait_send()


def chain(echoes, arc_start, arc_offsets, doppler_bins, steer_angles, train_mask, early):
    columns, num_pulses, cells = echoes.shape[1:]
    num_sel = arc_offsets.shape[1]
    num_chan = doppler_bins.shape[1]
    size = lax.axis_size("rng")
    beams = BEAMS // lax.axis_size("az")
    dof = BINS * num_sel
    steps = beams // 2
    late = steps - early
    n = size // 2
    width = ARC // 2
    w = width // steps
    side_chan = num_chan // 2
    half = side_chan * dof
    items = early * side_chan
    lanes = 128
    table_re, table_im = doppler_table(num_pulses)
    table = jnp.concatenate(
        [jnp.concatenate([table_re, -table_im], 1), jnp.concatenate([table_im, table_re], 1)], 0
    )
    blocks = train_mask.shape[1]
    cell_mask = (
        jnp.broadcast_to(train_mask[:, :, None], (beams, blocks, BLK))
        .reshape(beams, blocks * BLK)
        .astype(jnp.float32)
    )
    vm = pltpu.VMEM
    dma = pltpu.SemaphoreType.DMA
    f32 = jnp.float32
    bf16 = jnp.bfloat16
    smem = pl.BlockSpec(memory_space=pltpu.SMEM)
    vmem = pl.BlockSpec(memory_space=vm)
    tile = (num_chan, cells)
    scratch = [
        vm((2, columns + 2 * width, num_pulses, cells), bf16),
        vm((steps, 2, w, num_pulses, cells), bf16),
        vm((steps, 2, w, num_pulses, cells), bf16),
        vm((beams, 2, num_pulses, num_sel, cells), bf16),
        vm((beams, 2, dof, half), f32),
        vm((steps, 2, dof, half), f32),
        vm((steps, 2, dof, half), f32),
        vm((2, early, dof, half), f32),
        vm((late, n, dof, half), f32),
        vm((early, dof, half), f32),
        vm((lanes, lanes), f32),
        vm((dof, items, dof), f32),
        vm((dof, dof, items), f32),
        vm((dof, dof + 8, items), f32),
        vm((dof, dof + 8, items), f32),
        vm((dof, items), f32),
        vm((dof, items), f32),
        vm((size, beams, cells), f32),
        vm((beams, lanes), f32),
        vm((items, lanes), bf16),
        vm((2, 2, items, lanes), bf16),
        vm((2, 2, late * side_chan, lanes), bf16),
        vm((2, 2, items, lanes), f32),
        vm((2, 2, late * side_chan, lanes), f32),
        vm((beams + 2,) + tile, f32),
        vm((beams + 2,) + tile, f32),
        vm((beams + 2,) + tile, f32),
        vm((beams + 2,) + tile, f32),
        dma,
        dma((2, steps)),
        dma((2, steps)),
        dma((steps,)),
        dma((steps,)),
        dma((2, early)),
        dma((2, early)),
        dma((late, 2)),
        dma((late, n)),
        dma((size,)),
        dma((size,)),
        dma((size,)),
        dma((2, 2)),
        dma((2, 2)),
        dma((2, beams)),
        dma((2, beams)),
        dma((2,)),
        dma((2,)),
        dma((2, 2)),
        dma((2, 2)),
    ]
    return pl.pallas_call(
        functools.partial(chain_kernel, early),
        in_specs=[smem] * 5 + [pl.BlockSpec(memory_space=pl.ANY)] + [vmem] * 3,
        out_specs=vmem,
        out_shape=jax.ShapeDtypeStruct((beams,) + tile, f32),
        scratch_shapes=scratch,
        compiler_params=pltpu.CompilerParams(
            collective_id=2, has_side_effects=True, vmem_limit_bytes=CHAIN_VMEM
        ),
        name="chain",
    )(
        arc_start,
        arc_offsets.T,
        doppler_bins.T,
        jnp.cos(steer_angles.T),
        jnp.sin(steer_angles.T),
        echoes,
        table,
        cell_mask,
        doppler_bins.T.astype(f32),
    )


EARLY_PARTS = (3, 4)


def body(echoes, arc_start, arc_offsets, doppler_bins, steer_angles, train_mask):
    columns = echoes.shape[1]
    num_pulses = echoes.shape[2]
    cells = echoes.shape[3]
    num_sel = arc_offsets.shape[1]
    chan_count = doppler_bins.shape[1]
    cycle_size = lax.axis_size("az")
    cycle_pos = lax.axis_index("az")
    rng_size = lax.axis_size("rng")
    beam_count = BEAMS // cycle_size
    item_count = beam_count * chan_count
    dof = BINS * num_sel
    pairs = beam_count // 2
    early = pairs * EARLY_PARTS[0] // EARLY_PARTS[1]
    if (
        columns == ARC
        and beam_count % 2 == 0
        and pairs * (COLS // BEAMS) == ARC // 2
        and rng_size == 8
        and cycle_size > 2
        and cells == 128
        and chan_count % 16 == 0
        and chan_count // 2 * dof % 128 == 0
        and 2 * dof + 8 <= 128
        and pairs >= 4
        and early * (chan_count // 2) <= 128
    ):
        return chain(
            echoes, arc_start, arc_offsets, doppler_bins, steer_angles, train_mask, early
        )
    table_re, table_im = doppler_table(num_pulses)
    table = jnp.concatenate(
        [jnp.concatenate([table_re, -table_im], 1), jnp.concatenate([table_im, table_re], 1)], 0
    )

    def own(x):
        return lax.dynamic_slice_in_dim(x, cycle_pos * beam_count, beam_count, axis=0)

    arc_first = (own(arc_start) - cycle_pos * columns + ARC // 2) % COLS
    col_index = arc_first[:, None] + own(arc_offsets)
    bins_own = own(doppler_bins)
    angles = own(steer_angles)
    block_count = train_mask.shape[1]
    cell_mask = (
        jnp.broadcast_to(train_mask[:, :, None], (beam_count, block_count, BLK))
        .reshape(beam_count, 1, block_count * BLK)
        .astype(jnp.bfloat16)
    )
    smem = pl.BlockSpec(memory_space=pltpu.SMEM)

    def snap_gram(extended, first, last, base):
        share = last - first
        ext_cols = extended.shape[1]
        return pl.pallas_call(
            snap_gram_kernel,
            grid=(share,),
            in_specs=[
                smem,
                smem,
                smem,
                smem,
                pl.BlockSpec((2, ext_cols, num_pulses, cells), lambda b: (0, 0, 0, 0)),
                pl.BlockSpec(table.shape, lambda b: (0, 0)),
                pl.BlockSpec((1, 1, cells), lambda b: (b, 0, 0)),
            ],
            out_specs=[
                pl.BlockSpec((1, 2, num_pulses, num_sel, cells), lambda b: (b, 0, 0, 0, 0)),
                pl.BlockSpec((1, dof, chan_count * dof), lambda b: (b, 0, 0)),
            ],
            out_shape=[
                jax.ShapeDtypeStruct((share, 2, num_pulses, num_sel, cells), jnp.bfloat16),
                jax.ShapeDtypeStruct((share, dof, chan_count * dof), jnp.float32),
            ],
            compiler_params=pltpu.CompilerParams(vmem_limit_bytes=VMEM_LIMIT),
            cost_estimate=pl.CostEstimate(
                flops=share * 600_000_000, bytes_accessed=share * 1_500_000, transcendentals=0
            ),
            name="snap_gram",
        )(
            col_index[first:last] - base,
            bins_own[first:last],
            jnp.cos(angles)[first:last],
            jnp.sin(angles)[first:last],
            extended,
            table,
            cell_mask[first:last],
        )

    width = ARC // 2
    forward = [(i, (i + 1) % cycle_size) for i in range(cycle_size)]
    backward = [(target, source) for source, target in forward]
    low = lax.ppermute(echoes[:, columns - width :], "az", forward)
    high = lax.ppermute(echoes[:, :width], "az", backward)
    step = COLS // BEAMS
    half = beam_count // 2
    if (half - 1) * step + step - 1 + ARC - 1 < width + columns and half * step >= width:
        v_lo, gram_lo = snap_gram(jnp.concatenate([low, echoes], 1), 0, half, 0)
        high, v_lo, gram_lo = lax.optimization_barrier((high, v_lo, gram_lo))
        v_hi, gram_hi = snap_gram(jnp.concatenate([echoes, high], 1), half, beam_count, width)
        v_parts = (v_lo, v_hi)
        grams = (gram_lo, gram_hi)
        if rng_size % 4 or item_count // rng_size < chan_count:
            grams = (jnp.concatenate(grams, 0),)
    else:
        v_one, gram_one = snap_gram(jnp.concatenate([low, echoes, high], 1), 0, beam_count, 0)
        v_parts = (v_one,)
        grams = (gram_one,)

    per = item_count // rng_size
    if per < chan_count:
        split = chan_count // per
        gram = grams[0].reshape(beam_count, dof, split, per * dof)
        grams = (jnp.swapaxes(gram, 1, 2).reshape(beam_count * split, dof, per * dof),)
        width = per
    else:
        width = chan_count
    vm = pltpu.VMEM
    dma = pltpu.SemaphoreType.DMA
    line = rng_size // 2
    chunk = (grams[0].shape[0] * len(grams) // rng_size, dof, grams[0].shape[2])
    part = pl.pallas_call(
        functools.partial(scatter_kernel, line, len(grams)),
        in_specs=[pl.BlockSpec(memory_space=vm)] * len(grams),
        out_specs=pl.BlockSpec(memory_space=vm),
        out_shape=jax.ShapeDtypeStruct(chunk, jnp.float32),
        scratch_shapes=[vm((line,) + chunk, jnp.float32)] * 4 + [dma((line,))] * 6,
        compiler_params=pltpu.CompilerParams(
            collective_id=0, has_side_effects=True, vmem_limit_bytes=VMEM_LIMIT
        ),
        name="scatter",
    )(*[g.reshape((rng_size // len(grams),) + chunk) for g in grams])
    solved = pl.pallas_call(
        solve_kernel,
        out_shape=jax.ShapeDtypeStruct((2 * dof + 8, per), jnp.float32),
        scratch_shapes=[
            vm((dof, per, dof), jnp.float32),
            vm((dof, dof, per), jnp.float32),
            vm((dof, dof + 8, per), jnp.float32),
            vm((dof, dof + 8, per), jnp.float32),
            vm((dof, per), jnp.float32),
            vm((dof, per), jnp.float32),
        ],
        compiler_params=pltpu.CompilerParams(vmem_limit_bytes=VMEM_LIMIT),
        name="solve",
    )(part)
    lanes = 128
    local_count = (BLK * jnp.sum(train_mask, axis=1)).astype(jnp.float32)
    pad_rows = -per % 8
    payload = jnp.concatenate(
        [
            jnp.pad(solved.T, ((0, pad_rows), (0, lanes - solved.shape[0]))),
            jnp.broadcast_to(local_count[:, None], (beam_count, lanes)),
        ],
        0,
    )
    halves = len(v_parts)
    any_spec = pl.BlockSpec(memory_space=pl.ANY)
    block = (chan_count, cells)
    out = pl.pallas_call(
        functools.partial(apply_kernel, halves, per, dof),
        in_specs=[pl.BlockSpec(memory_space=vm)] * 2 + [any_spec] * halves,
        out_specs=pl.BlockSpec(memory_space=vm),
        out_shape=jax.ShapeDtypeStruct((beam_count,) + block, jnp.float32),
        scratch_shapes=[
            vm((beam_count, 2, num_pulses, num_sel, cells), jnp.bfloat16),
            vm((rng_size,) + payload.shape, jnp.float32),
            vm((beam_count,) + block, jnp.float32),
            vm((2, 8, item_count), jnp.float32),
            vm((2, 8, item_count), jnp.float32),
            vm((beam_count,) + block, jnp.float32),
            vm(block, jnp.float32),
            vm(block, jnp.float32),
            dma((halves,)),
            dma((rng_size,)),
            dma((rng_size,)),
            dma((2,)),
            dma((2,)),
            dma((2,)),
            dma((2,)),
        ],
        compiler_params=pltpu.CompilerParams(
            collective_id=1, has_side_effects=True, vmem_limit_bytes=VMEM_LIMIT
        ),
        name="apply",
    )(payload, bins_own[:, :, None], *v_parts)
    return out


def solution(mesh):
    return jax.shard_map(
        body,
        mesh=mesh,
        in_specs=(P(None, "az", None, "rng"), P(), P(), P(), P(), P("az", "rng")),
        out_specs=P("az", None, "rng"),
        check_vma=False,
    )
```

```python
import functools

import jax
import numpy as np
import jax.numpy as jnp
from jax import lax
from jax.experimental import pallas as pl
from jax.experimental.pallas import tpu as pltpu
from jax.sharding import PartitionSpec as P


COLS = 256
ARC = 64
BINS = 3
BEAMS = 64
BLK = 128
LOADING = 0.1
VMEM_LIMIT = 48 << 20
CHAIN_VMEM = 66_200_000
CODE_TOP = 32000.0
LAG = 3


def doppler_table(num_pulses):
    freq_ids = jnp.arange(num_pulses, dtype=jnp.int32)
    phase_steps = freq_ids[:, None] * freq_ids[None, :] % num_pulses
    phase_angle = -2.0 * jnp.pi / num_pulses * phase_steps.astype(jnp.float32)
    return (jnp.cos(phase_angle).astype(jnp.bfloat16), jnp.sin(phase_angle).astype(jnp.bfloat16))


def snap_gram_kernel(
    col_ref, bins_ref, cos_ref, sin_ref, ext_ref, table_ref, mask_ref, v_ref, gram_ref
):
    beam = pl.program_id(0)
    pulses = ext_ref.shape[2]
    num_sel = col_ref.shape[1]
    num_chan = bins_ref.shape[1]
    table = table_ref[...]
    parts_re, parts_im = [], []
    for j in range(num_sel):
        col = col_ref[beam, j]
        data = jnp.concatenate([ext_ref[0, col], ext_ref[1, col]], axis=0)
        spec = jnp.dot(table, data, preferred_element_type=jnp.float32)
        cosine = cos_ref[beam, j]
        sine = sin_ref[beam, j]
        spec_re = spec[:pulses]
        spec_im = spec[pulses:]
        parts_re.append(cosine * spec_re - sine * spec_im)
        parts_im.append(sine * spec_re + cosine * spec_im)
    for part, pieces in enumerate((parts_re, parts_im)):
        stacked = jnp.swapaxes(jnp.stack(pieces, 0), 0, 1)
        v_ref[0, part] = stacked.astype(jnp.bfloat16)
    dof = BINS * num_sel
    mask_row = mask_ref[0]
    row = lax.broadcasted_iota(jnp.int32, (dof, dof), 0)
    colm = lax.broadcasted_iota(jnp.int32, (dof, dof), 1)
    lower = row >= colm
    packed = []
    for k in range(num_chan):
        centre = bins_ref[beam, k]
        ids = [(centre + (q - BINS // 2 + pulses)) % pulses for q in range(BINS)]
        u_re = jnp.concatenate([v_ref[0, 0, f] for f in ids], 0)
        u_im = jnp.concatenate([v_ref[0, 1, f] for f in ids], 0)
        right = jnp.concatenate([u_re, u_im], 1)
        m_re = u_re * mask_row
        m_im = u_im * mask_row
        left = jnp.concatenate(
            [jnp.concatenate([m_re, m_im], 1), jnp.concatenate([m_im, -m_re], 1)], 0
        )
        both = lax.dot_general(
            left, right, (((1,), (1,)), ((), ())), preferred_element_type=jnp.float32
        )
        packed.append(jnp.where(lower, both[:dof], both[dof:]))
    gram_ref[0] = jnp.concatenate(packed, 1)


def solve_kernel(part_ref, out_ref, stack, turned, hr, hi, xr, xi, yr, yi):
    lead, dof, wide = part_ref.shape
    width = wide // dof
    lanes = lead * width
    nb = dof // 8
    group = min(8, lanes)
    for g in range(0, lanes, group):
        pieces = []
        for item in range(g, g + group):
            k = item % width
            pieces.append(part_ref[item // width, :, k * dof : (k + 1) * dof])
        stack[:, g : g + group, :] = jnp.swapaxes(jnp.stack(pieces, 0), 0, 1)
    for i in range(dof):
        turned[i] = stack[i].T
    trace = jnp.zeros((1, lanes), jnp.float32)
    for i in range(dof):
        trace = trace + turned[i, i : i + 1, :]
    load = (LOADING / dof) * trace
    cube = (8, 8, lanes)
    row = lax.broadcasted_iota(jnp.int32, cube, 0)
    col = lax.broadcasted_iota(jnp.int32, cube, 1)
    for ib in range(nb):
        rows = slice(8 * ib, 8 * ib + 8)
        for jb in range(ib, nb):
            cols = slice(8 * jb, 8 * jb + 8)
            imag = turned[rows, cols, :]
            real = jnp.swapaxes(turned[cols, rows, :], 0, 1)
            if ib == jb:
                straight, flip = imag, real
                real = jnp.where(row >= col, straight, flip)
                real = jnp.where(row == col, real + load[None], real)
                imag = jnp.where(row < col, straight, jnp.where(row > col, -flip, 0.0))
            hr[rows, cols, :] = real
            hi[rows, cols, :] = imag
    yr[...] = jnp.ones_like(yr)
    yi[...] = jnp.zeros_like(yi)
    xr[...] = jnp.zeros_like(xr)
    xi[...] = jnp.zeros_like(xi)
    sub = lax.broadcasted_iota(jnp.int32, (8, lanes), 0)

    for kb in range(nb):

        def step(k, carry, kb=kb):
            pivot = 1.0 / hr[k, pl.ds(k, 1), :]
            rr = [hr[k, 8 * b : 8 * b + 8, :] for b in range(kb, nb)]
            ri = [hi[k, 8 * b : 8 * b + 8, :] for b in range(kb, nb)]
            gr = jnp.broadcast_to(yr[pl.ds(k, 1), :], (8, lanes))
            gi = jnp.broadcast_to(yi[pl.ds(k, 1), :], (8, lanes))
            for ib in range(kb, nb):
                fr = rr[ib - kb] * pivot
                fi = -ri[ib - kb] * pivot
                if ib == kb:
                    live = sub + 8 * kb > k
                    fr = jnp.where(live, fr, 0.0)
                    fi = jnp.where(live, fi, 0.0)
                own = slice(8 * ib, 8 * ib + 8)
                yr[own, :] = yr[own, :] - (fr * gr - fi * gi)
                yi[own, :] = yi[own, :] - (fr * gi + fi * gr)
                for s in range(8):
                    i = 8 * ib + s
                    cr = jnp.broadcast_to(fr[s : s + 1], (8, lanes))
                    ci = jnp.broadcast_to(fi[s : s + 1], (8, lanes))
                    for b in range(ib, nb):
                        pr, pi = rr[b - kb], ri[b - kb]
                        sl = slice(8 * b, 8 * b + 8)
                        hr[i, sl, :] = hr[i, sl, :] - (cr * pr - ci * pi)
                        hi[i, sl, :] = hi[i, sl, :] - (cr * pi + ci * pr)
            return carry

        lax.fori_loop(8 * kb, 8 * kb + 8, step, 0)

    for ib in reversed(range(nb)):

        def back(t, carry, ib=ib):
            i = 8 * ib + 7 - t
            sr = jnp.zeros((8, lanes), jnp.float32)
            si = jnp.zeros((8, lanes), jnp.float32)
            for b in range(ib, nb):
                sl = slice(8 * b, 8 * b + 8)
                ar, ai = hr[i, sl, :], hi[i, sl, :]
                br, bi = xr[sl, :], xi[sl, :]
                sr = sr + (ar * br - ai * bi)
                si = si + (ar * bi + ai * br)
            pivot = 1.0 / hr[i, pl.ds(i, 1), :]
            top_r = yr[pl.ds(i, 1), :]
            top_i = yi[pl.ds(i, 1), :]
            xr[pl.ds(i, 1), :] = (top_r - jnp.sum(sr, 0, keepdims=True)) * pivot
            xi[pl.ds(i, 1), :] = (top_i - jnp.sum(si, 0, keepdims=True)) * pivot
            return carry

        lax.fori_loop(0, 8, back, 0)
    out_ref[:dof, :lanes] = xr[...]
    out_ref[dof : 2 * dof, :lanes] = xi[...]
    out_ref[2 * dof : 2 * dof + 8, :lanes] = jnp.broadcast_to(
        jnp.sum(xr[...], 0, keepdims=True), (8, lanes)
    )


MESH = pl.DeviceIdType.MESH


def scatter_kernel(n, halves, *refs):
    g_refs = refs[:halves]
    out_ref, pair, acc, right, left, psend, precv, rsend, rrecv, lsend, lrecv = refs[halves:]
    share = n // halves

    def own(t, core):
        return g_refs[t // share].at[2 * (t % share) + core]

    me = lax.axis_index("rng")
    z = me // 2
    c = me % 2
    mate = 2 * z + 1 - c
    ahead = lax.rem(me + 2, 2 * n)
    behind = lax.rem(me + 2 * n - 2, 2 * n)
    barrier = pltpu.get_barrier_semaphore()
    pl.semaphore_signal(barrier, inc=1, device_id={"rng": mate}, device_id_type=MESH)
    pl.semaphore_signal(barrier, inc=1, device_id={"rng": ahead}, device_id_type=MESH)
    pl.semaphore_signal(barrier, inc=1, device_id={"rng": behind}, device_id_type=MESH)
    pl.semaphore_wait(barrier, 3)

    order = []
    for t in range((n + 1) // 2):
        order.append(n - 1 - t)
        if t != n - 1 - t:
            order.append(t)

    def pair_copy(t):
        return pltpu.make_async_remote_copy(
            src_ref=own(t, 1 - c),
            dst_ref=pair.at[t],
            send_sem=psend.at[t],
            recv_sem=precv.at[t],
            device_id={"rng": mate},
            device_id_type=MESH,
        )

    def right_copy(t):
        return pltpu.make_async_remote_copy(
            src_ref=acc.at[t],
            dst_ref=right.at[t],
            send_sem=rsend.at[t],
            recv_sem=rrecv.at[t],
            device_id={"rng": ahead},
            device_id_type=MESH,
        )

    def left_copy(t):
        return pltpu.make_async_remote_copy(
            src_ref=acc.at[t],
            dst_ref=left.at[t],
            send_sem=lsend.at[t],
            recv_sem=lrecv.at[t],
            device_id={"rng": behind},
            device_id_type=MESH,
        )

    for t in order:
        pair_copy(t).start()
    for t in order:
        pair_copy(t).wait_recv()
        acc[t] = own(t, c)[...] + pair[t]

        @pl.when(jnp.logical_and(z == 0, t > 0))
        def _(t=t):
            right_copy(t).start()

        @pl.when(jnp.logical_and(z == n - 1, t < n - 1))
        def _(t=t):
            left_copy(t).start()

    for place in range(n):
        events = [(place + n - 1 - t, 0, t) for t in range(place + 1, n) if place > 0]
        events += [(n - 1 - place + t, 1, t) for t in range(place) if place < n - 1]

        @pl.when(z == place)
        def _(place=place, events=sorted(events)):
            for _, side, t in events:
                copy = left_copy(t) if side else right_copy(t)
                source = left if side else right
                copy.wait_recv()
                acc[t] = acc[t] + source[t]
                copy.start()
            total = acc[place]
            if place > 0:
                right_copy(place).wait_recv()
                total = total + right[place]
            if place < n - 1:
                left_copy(place).wait_recv()
                total = total + left[place]
            out_ref[...] = total

    for t in range(n):
        pair_copy(t).wait_send()

        @pl.when(z < t)
        def _(t=t):
            right_copy(t).wait_send()

        @pl.when(z > t)
        def _(t=t):
            left_copy(t).wait_send()


def apply_kernel(
    halves,
    per,
    dof,
    pay_ref,
    bins_ref,
    *refs,
):
    v_refs = refs[:halves]
    (out_ref, v_all, gat, power, edge, halo, sums, az_lo, az_hi) = refs[halves : halves + 9]
    (vsem, gsend, grecv, esend, erecv, asend, arecv) = refs[halves + 9 :]
    me = lax.axis_index("rng")
    az = lax.axis_index("az")
    n = lax.axis_size("rng")
    m = lax.axis_size("az")
    beams, num_chan, cells = out_ref.shape
    pulses, num_sel = v_all.shape[2], v_all.shape[3]
    taps = pulses * num_sel
    az_next = lax.rem(az + 1, m)
    az_prev = lax.rem(az + m - 1, m)
    barrier = pltpu.get_barrier_semaphore()
    for d in range(1, n):
        peer = lax.rem(me + d, n)
        pl.semaphore_signal(barrier, inc=1, device_id={"rng": peer}, device_id_type=MESH)
    for other in (az_next, az_prev):
        pl.semaphore_signal(barrier, inc=1, device_id={"az": other}, device_id_type=MESH)
    share = beams // halves
    loads = []
    for h in range(halves):
        load = pltpu.make_async_copy(v_refs[h], v_all.at[pl.ds(h * share, share)], vsem.at[h])
        load.start()
        loads.append(load)
    pl.semaphore_wait(barrier, n + 1)

    copies = []
    for d in range(1, n):
        peer = lax.rem(me + d, n)
        copy = pltpu.make_async_remote_copy(
            src_ref=pay_ref,
            dst_ref=gat.at[me],
            send_sem=gsend.at[d],
            recv_sem=grecv.at[d],
            device_id={"rng": peer},
            device_id_type=MESH,
        )
        copy.start()
        copies.append(copy)
    gat[me] = pay_ref[...]
    for load in loads:
        load.wait()
    for copy in copies:
        copy.wait_recv()
    rows = gat.shape[1] - beams
    count = jnp.zeros((beams, gat.shape[2]), jnp.float32)
    for r in range(n):
        count = count + gat[r, rows:, :]
    sums[0] = jnp.zeros(sums.shape[1:], jnp.float32)
    for b in range(beams):
        sums[b, :1, :] = count[b : b + 1]
    freq = lax.broadcasted_iota(jnp.int32, (num_chan, taps), 1) // num_sel
    lanes = gat.shape[2]
    lane = lax.broadcasted_iota(jnp.int32, (num_chan, lanes), 1)

    def one(b, carry):
        if per >= num_chan:
            ratio = per // num_chan
            start = pl.multiple_of((b % ratio) * num_chan, 8)
            w = gat[b // ratio, pl.ds(start, num_chan), :]
        else:
            split = num_chan // per
            w = jnp.concatenate([gat[b * split + t, :per, :] for t in range(split)], 0)
        w = w * sums[b, :1, :]
        quiet = w[:, 2 * dof : 2 * dof + 1]
        centre = bins_ref[b]
        planes = []
        hits = []
        for q in range(BINS):
            f = lax.rem(centre + (q - BINS // 2 + pulses), pulses)
            hits.append(freq == f)
        for part in range(2):
            plane = jnp.zeros((num_chan, taps), jnp.float32)
            for q in range(BINS):
                start = part * dof + q * num_sel
                piece = pltpu.roll(w, (lanes - start) % lanes, 1) if start else w
                piece = jnp.where(lane < num_sel, piece, 0.0)
                span = num_sel
                while span < lanes:
                    piece = piece + pltpu.roll(piece, span, 1)
                    span *= 2
                tiled = jnp.concatenate([piece] * (taps // lanes), 1)
                plane = jnp.where(hits[q], tiled, plane)
            planes.append(plane)
        top = jnp.concatenate([planes[0], planes[1]], 1)
        low = jnp.concatenate([-planes[1], planes[0]], 1)
        lhs = jnp.concatenate([top, low], 0).astype(jnp.bfloat16)
        flat = v_all[b].reshape(2 * taps, cells)
        proj = jnp.dot(lhs, flat, preferred_element_type=jnp.float32)
        p0 = proj[:num_chan]
        p1 = proj[num_chan:]
        power[b] = (p0 * p0 + p1 * p1) / quiet
        return carry

    lax.fori_loop(0, beams, one, 0)
    items = beams * num_chan
    turned = power[...].reshape(items, cells).T
    edge[0] = turned[:8]
    edge[1] = turned[cells - 8 :]

    def edge_copy(side):
        target = lax.rem(me + 1, n) if side else lax.rem(me + n - 1, n)
        return pltpu.make_async_remote_copy(
            src_ref=edge.at[side],
            dst_ref=halo.at[side],
            send_sem=esend.at[side],
            recv_sem=erecv.at[side],
            device_id={"rng": target},
            device_id_type=MESH,
        )

    for side in range(2):
        edge_copy(side).start()
    for side in range(2):
        edge_copy(side).wait()
    before = jnp.where(me > 0, halo[1, 7:8], 0.0)
    after = jnp.where(me < n - 1, halo[0, 0:1], 0.0)
    turned = (
        jnp.concatenate([before, turned[:-1]], 0)
        + turned
        + jnp.concatenate([turned[1:], after], 0)
    )
    sums[...] = turned.T.reshape(beams, num_chan, cells)
    up = pltpu.make_async_remote_copy(
        src_ref=sums.at[beams - 1],
        dst_ref=az_lo,
        send_sem=asend.at[0],
        recv_sem=arecv.at[0],
        device_id={"az": az_next},
        device_id_type=MESH,
    )
    down = pltpu.make_async_remote_copy(
        src_ref=sums.at[0],
        dst_ref=az_hi,
        send_sem=asend.at[1],
        recv_sem=arecv.at[1],
        device_id={"az": az_prev},
        device_id_type=MESH,
    )
    up.start()
    down.start()
    for b in range(1, beams - 1):
        out_ref[b] = (sums[b - 1] + sums[b] + sums[b + 1]) / 9.0
    up.wait_recv()
    down.wait_recv()
    out_ref[0] = (az_lo[...] + sums[0] + sums[1]) / 9.0
    out_ref[beams - 1] = (sums[beams - 2] + sums[beams - 1] + az_hi[...]) / 9.0
    up.wait_send()
    down.wait_send()
    for copy in copies:
        copy.wait_send()


def gram_of(v_ref, beam, bins, mask_row):
    pulses = v_ref.shape[2]
    num_sel = v_ref.shape[3]
    dof = BINS * num_sel
    row = lax.broadcasted_iota(jnp.int32, (dof, dof), 0)
    colm = lax.broadcasted_iota(jnp.int32, (dof, dof), 1)
    lower = row >= colm
    packed = []
    for centre in bins:
        ids = [lax.rem(centre + (q - BINS // 2 + pulses), pulses) for q in range(BINS)]
        u_re = jnp.concatenate([v_ref[beam, 0, f] for f in ids], 0)
        u_im = jnp.concatenate([v_ref[beam, 1, f] for f in ids], 0)
        right = jnp.concatenate([u_re, u_im], 1)
        m_re = u_re * mask_row
        m_im = u_im * mask_row
        left = jnp.concatenate(
            [jnp.concatenate([m_re, m_im], 1), jnp.concatenate([m_im, -m_re], 1)], 0
        )
        both = lax.dot_general(
            left, right, (((1,), (1,)), ((), ())), preferred_element_type=jnp.float32
        )
        packed.append(jnp.where(lower, both[:dof], both[dof:]))
    return packed


def chain_kernel(
    start_hbm,
    offs_hbm,
    bins_hbm,
    train_hbm,
    angle_hbm,
    echoes,
    table_hbm,
    spread_hbm,
    out_ref,
    start_ref,
    offs_ref,
    bins_ref,
    train_ref,
    angle_ref,
    chan_ref,
    table_ref,
    spread_ref,
    turn,
    ext,
    low,
    high,
    v_all,
    gram,
    pair,
    coded,
    scale,
    code_in,
    scale_in,
    part,
    solved,
    stack,
    turned,
    hr,
    hi,
    xr,
    xi,
    yr,
    yi,
    masks,
    totals,
    counts,
    pay,
    gat,
    tiles,
    pw,
    pl_left,
    pl_right,
    rows,
    esem,
    hsend,
    hrecv,
    psend,
    precv,
    dsend,
    drecv,
    msend,
    mrecv,
    gsend,
    grecv,
    lsend,
    lrecv,
    tsend,
    trecv,
    asend,
    arecv,
):
    me = lax.axis_index("rng")
    az = lax.axis_index("az")
    size = lax.axis_size("rng")
    m = lax.axis_size("az")
    n = size // 2
    z = me // 2
    c = lax.rem(me, 2)
    beams, num_chan, cells = out_ref.shape
    columns = echoes.shape[1]
    pulses = echoes.shape[2]
    num_sel = offs_ref.shape[0]
    blocks = train_ref.shape[0]
    dof = BINS * num_sel
    taps = pulses * num_sel
    steps = beams // 2
    width = ARC // 2
    w = width // steps
    side_chan = num_chan // 2
    half = side_chan * dof
    lanes = pay.shape[1]
    az_next = lax.rem(az + 1, m)
    az_prev = lax.rem(az + m - 1, m)
    ahead = lax.rem(me + 1, size)
    behind = lax.rem(me + size - 1, size)
    mate = 2 * z + 1 - c
    mid_l = n // 2 - 1
    mid_r = n // 2
    owners = ((0, mid_l), (1, mid_r))
    is_mid = jnp.logical_or(z == mid_l, z == mid_r)

    loads = [
        pltpu.make_async_copy(src, dst, esem.at[i])
        for i, (src, dst) in enumerate(
            (
                (start_hbm, start_ref),
                (offs_hbm, offs_ref),
                (bins_hbm, bins_ref),
                (train_hbm, train_ref),
                (angle_hbm, angle_ref),
                (bins_hbm, chan_ref),
                (table_hbm, table_ref),
                (spread_hbm, spread_ref),
                (echoes, ext.at[:, width : width + columns]),
            )
        )
    ]
    barrier = pltpu.get_barrier_semaphore()
    for other in (az_next, az_prev):
        pl.semaphore_signal(barrier, inc=1, device_id={"az": other}, device_id_type=MESH)
    pl.semaphore_signal(barrier, inc=1, device_id={"rng": mate}, device_id_type=MESH)
    for place in range(n):
        near = jnp.logical_or(is_mid, place in (mid_l, mid_r))

        @pl.when(jnp.logical_and(z != place, near))
        def _(place=place):
            pl.semaphore_signal(
                barrier, inc=1, device_id={"rng": 2 * place + c}, device_id_type=MESH
            )

    for load in loads:
        load.start()
    pl_left[...] = jnp.zeros(pl_left.shape, jnp.float32)
    pl_right[...] = jnp.zeros(pl_right.shape, jnp.float32)
    solved[...] = jnp.zeros(solved.shape, jnp.float32)
    pl.semaphore_wait(barrier, 3 + jnp.where(is_mid, n - 1, 2))

    def low_copy(i):
        return pltpu.make_async_remote_copy(
            src_ref=echoes.at[:, pl.ds(columns - w * (i + 1), w)],
            dst_ref=low.at[i],
            send_sem=hsend.at[0, i],
            recv_sem=hrecv.at[0, i],
            device_id={"az": az_next},
            device_id_type=MESH,
        )

    def high_copy(i):
        return pltpu.make_async_remote_copy(
            src_ref=echoes.at[:, pl.ds(w * i, w)],
            dst_ref=high.at[i],
            send_sem=hsend.at[1, i],
            recv_sem=hrecv.at[1, i],
            device_id={"az": az_prev},
            device_id_type=MESH,
        )

    for i in range(steps):
        low_copy(i).start()
        high_copy(i).start()
    for load in loads:
        load.wait()

    cell = lax.broadcasted_iota(jnp.int32, (1, cells), 1) // BLK
    for b in range(beams):
        row = jnp.zeros((1, cells), jnp.float32)
        for blk in range(blocks):
            row = jnp.where(cell == blk, train_ref[blk, b].astype(jnp.float32), row)
        masks[0, b : b + 1, :] = row

    mask_copy = pltpu.make_async_remote_copy(
        src_ref=masks.at[0],
        dst_ref=masks.at[1],
        send_sem=msend,
        recv_sem=mrecv,
        device_id={"rng": mate},
        device_id_type=MESH,
    )
    mask_copy.start()
    turn[0] = jnp.cos(angle_ref[...])
    turn[1] = jnp.sin(angle_ref[...])
    mask_copy.wait_recv()
    totals[...] = jnp.broadcast_to(
        jnp.sum(masks[0] + masks[1], 1, keepdims=True), totals.shape
    )

    def mine(t):
        return jnp.where(c == 0, steps - 1 - t, steps + t)

    def pair_copy(t):
        return pltpu.make_async_remote_copy(
            src_ref=gram.at[jnp.where(c == 0, steps + t, steps - 1 - t)],
            dst_ref=pair.at[t],
            send_sem=psend.at[t],
            recv_sem=precv.at[t],
            device_id={"rng": mate},
            device_id_type=MESH,
        )

    def code_copies(side, t, source):
        owner = 2 * (mid_r if side else mid_l) + c
        return [
            pltpu.make_async_remote_copy(
                src_ref=src.at[t, side],
                dst_ref=dst.at[t, source],
                send_sem=dsend.at[i, t, side],
                recv_sem=drecv.at[i, t, source],
                device_id={"rng": owner},
                device_id_type=MESH,
            )
            for i, (src, dst) in enumerate(((coded, code_in), (scale, scale_in)))
        ]

    table = table_ref[...]
    blane = lax.broadcasted_iota(jnp.int32, angle_ref.shape, 1)

    def one_beam(b):
        bg = az * beams + b
        first = lax.rem(start_ref[bg] - az * columns + (width + COLS), COLS)
        first = jnp.minimum(first, ext.shape[1] - ARC)
        here = blane == bg
        cosine = jnp.sum(jnp.where(here, turn[0], 0.0), 1, keepdims=True)
        sine = jnp.sum(jnp.where(here, turn[1], 0.0), 1, keepdims=True)
        cosine = jnp.broadcast_to(cosine, (num_sel, cells))[None]
        sine = jnp.broadcast_to(sine, (num_sel, cells))[None]
        parts_re, parts_im = [], []
        for j in range(num_sel):
            col = first + offs_ref[j, bg]
            data = jnp.concatenate([ext[0, col], ext[1, col]], axis=0)
            spec = jnp.dot(table, data, preferred_element_type=jnp.float32)
            parts_re.append(spec[:pulses])
            parts_im.append(spec[pulses:])
        spec_re = jnp.swapaxes(jnp.stack(parts_re, 0), 0, 1)
        spec_im = jnp.swapaxes(jnp.stack(parts_im, 0), 0, 1)
        v_all[b, 0] = (cosine * spec_re - sine * spec_im).astype(jnp.bfloat16)
        v_all[b, 1] = (sine * spec_re + cosine * spec_im).astype(jnp.bfloat16)
        mask_row = masks[0, pl.ds(b, 1), :].astype(jnp.bfloat16)
        bins = [bins_ref[k, bg] for k in range(num_chan)]
        packed = gram_of(v_all, b, bins, mask_row)
        gram[b, 0] = jnp.concatenate(packed[:side_chan], 1)
        gram[b, 1] = jnp.concatenate(packed[side_chan:], 1)

    def slot(s, carry):
        @pl.when(s < steps)
        def _():
            low_copy(s).wait_recv()
            high_copy(s).wait_recv()
            ext[:, pl.ds(width - w * (s + 1), w)] = low[s]
            ext[:, pl.ds(width + columns + w * s, w)] = high[s]
            one_beam(steps - 1 - s)

        t = s - 1

        @pl.when(jnp.logical_and(t >= 0, t < steps))
        def _():
            pair_copy(t).wait_recv()
            own = mine(t)
            number = totals[pl.ds(own, 1), :]
            for side, owner in owners:
                total = gram[own, side] + pair[t, side]

                @pl.when(z == owner)
                def _(side=side, total=total):
                    part[t] = total
                    counts[t] = number

                @pl.when(z != owner)
                def _(side=side, total=total):
                    top = jnp.max(jnp.abs(total), 0, keepdims=True)
                    top = jnp.maximum(top, 1e-30)
                    code = jnp.round(total * (CODE_TOP / top))
                    coded[t, side] = code.astype(jnp.int32).astype(jnp.int16)
                    scale[t, side, :, :half] = top * (1.0 / CODE_TOP)
                    scale[t, side, :, half:] = number
                    for copy in code_copies(side, t, z):
                        copy.start()

        tt = s - LAG

        @pl.when(jnp.logical_and(tt >= 0, tt < steps))
        def _():
            for side, owner in owners:

                @pl.when(z == owner)
                def _(side=side, owner=owner):
                    total = part[tt]
                    number = counts[tt]
                    for source in range(n):
                        if source != owner:
                            for copy in code_copies(side, tt, source):
                                copy.wait_recv()
                            code = code_in[tt, source].astype(jnp.int32).astype(jnp.float32)
                            total = total + code * scale_in[tt, source, :, :half]
                            number = number + scale_in[tt, source, :, half:]
                    part[tt] = total
                    counts[tt] = number

        @pl.when(s < steps)
        def _():
            one_beam(steps + s)
            pair_copy(s).start()

        return carry

    lax.fori_loop(0, steps + LAG, slot, 0)

    items = steps * side_chan

    def send_copy(d, side):
        return pltpu.make_async_remote_copy(
            src_ref=pay,
            dst_ref=gat.at[side, c],
            send_sem=gsend.at[d],
            recv_sem=grecv.at[side, c],
            device_id={"rng": lax.rem(me + d, size)},
            device_id_type=MESH,
        )

    @pl.when(is_mid)
    def _():
        solve_kernel(part, solved, stack, turned, hr, hi, xr, xi, yr, yi)
        flipped = solved[...].T
        scaled = []
        for t in range(steps):
            scaled.append(flipped[side_chan * t : side_chan * (t + 1)] * counts[t])
        full = jnp.concatenate(scaled, 0)
        lane = lax.broadcasted_iota(jnp.int32, (items, lanes), 1)
        hi_part = full.astype(jnp.bfloat16).astype(jnp.float32)
        rest = full - hi_part
        mid_part = rest.astype(jnp.bfloat16).astype(jnp.float32)
        lo_part = rest - mid_part
        split = jnp.where(
            lane == 2 * dof + 1, mid_part, jnp.where(lane == 2 * dof + 2, lo_part, hi_part)
        )
        pay[...] = split.astype(jnp.bfloat16)
        for side, owner in owners:

            @pl.when(z == owner)
            def _(side=side):
                for d in range(1, size):
                    send_copy(d, side).start()
                gat[side, c] = pay[...]

    freq = (lax.broadcasted_iota(jnp.int32, (num_chan, taps), 1) // num_sel).astype(jnp.float32)
    centres = chan_ref[...].astype(jnp.float32)

    def tile_copy(side, b):
        target = ahead if side else behind
        buf = pl_left if side else pl_right
        return pltpu.make_async_remote_copy(
            src_ref=pw.at[b + 1],
            dst_ref=buf.at[b + 1],
            send_sem=lsend.at[side, b],
            recv_sem=lrecv.at[side, b],
            device_id={"rng": target},
            device_id_type=MESH,
        )

    def az_copy(up):
        return pltpu.make_async_remote_copy(
            src_ref=pw.at[beams if up else 1],
            dst_ref=pw.at[0 if up else beams + 1],
            send_sem=tsend.at[up],
            recv_sem=trecv.at[up],
            device_id={"az": az_next if up else az_prev},
            device_id_type=MESH,
        )

    def corner_copy(up, side):
        buf = pl_left if side else pl_right
        return pltpu.make_async_remote_copy(
            src_ref=pw.at[beams if up else 1],
            dst_ref=buf.at[0 if up else beams + 1],
            send_sem=asend.at[up, side],
            recv_sem=arecv.at[up, side],
            device_id={
                "az": az_next if up else az_prev,
                "rng": ahead if side else behind,
            },
            device_id_type=MESH,
        )

    def one_power(b, t, core):
        start = pl.multiple_of(t * side_chan, side_chan)
        both = [tiles[side, core, pl.ds(start, side_chan), :] for side in range(2)]
        wide = jnp.concatenate(both, 0)
        tail = wide[:, 2 * BINS * lanes :]
        quiet = tail[:, :1] + tail[:, 1:2] + tail[:, 2:3]
        centre = jnp.sum(jnp.where(blane == az * beams + b, centres, 0.0), 1, keepdims=True)
        hits = []
        for q in range(BINS):
            f = centre + (q - BINS // 2)
            f = jnp.where(f < 0.0, f + pulses, jnp.where(f >= pulses, f - pulses, f))
            hits.append(freq == f)
        planes = []
        for p in range(2):
            plane = jnp.zeros((num_chan, taps), jnp.float32)
            for q in range(BINS):
                at = (p * BINS + q) * lanes
                piece = wide[:, at : at + lanes]
                tiled = jnp.concatenate([piece] * (taps // lanes), 1)
                plane = jnp.where(hits[q], tiled, plane)
            planes.append(plane)
        top = jnp.concatenate([planes[0], planes[1]], 1)
        bottom = jnp.concatenate([-planes[1], planes[0]], 1)
        lhs = jnp.concatenate([top, bottom], 0).astype(jnp.bfloat16)
        flat = v_all[b].reshape(2 * taps, cells)
        proj = jnp.dot(lhs, flat, preferred_element_type=jnp.float32)
        p0 = proj[:num_chan]
        p1 = proj[num_chan:]
        pw[b + 1] = (p0 * p0 + p1 * p1) / quiet

        @pl.when(me < size - 1)
        def _():
            tile_copy(1, b).start()

        @pl.when(me > 0)
        def _():
            tile_copy(0, b).start()

    for side, owner in owners:
        for core in range(2):

            @pl.when(me != 2 * owner + core)
            def _(side=side, core=core):
                pltpu.make_async_remote_copy(
                    src_ref=pay,
                    dst_ref=gat.at[side, core],
                    send_sem=gsend.at[0],
                    recv_sem=grecv.at[side, core],
                    device_id={"rng": ahead},
                    device_id_type=MESH,
                ).wait_recv()

            tiles[side, core] = jnp.dot(
                gat[side, core], spread_ref[...], preferred_element_type=jnp.float32
            )

    def power(i, carry):
        one_power(i, steps - 1 - i, 0)
        one_power(beams - 1 - i, steps - 1 - i, 1)

        @pl.when(i == 0)
        def _():
            for up in range(2):
                az_copy(up).start()

                @pl.when(me < size - 1)
                def _(up=up):
                    corner_copy(up, 1).start()

                @pl.when(me > 0)
                def _(up=up):
                    corner_copy(up, 0).start()

        return carry

    lax.fori_loop(0, steps, power, 0)

    lane = lax.broadcasted_iota(jnp.int32, (num_chan, cells), 1)

    def row_sum(i):
        mid = pw[i]
        back = pltpu.roll(jnp.where(lane == cells - 1, pl_left[i], mid), 1, 1)
        fore = pltpu.roll(jnp.where(lane == 0, pl_right[i], mid), cells - 1, 1)
        return back + mid + fore

    for b in range(beams):

        @pl.when(me > 0)
        def _(b=b):
            tile_copy(1, b).wait_recv()

        @pl.when(me < size - 1)
        def _(b=b):
            tile_copy(0, b).wait_recv()

    for b in range(beams):
        rows[b + 1] = row_sum(b + 1)
    for b in range(1, beams - 1):
        out_ref[b] = (rows[b] + rows[b + 1] + rows[b + 2]) / 9.0
    for up in range(2):
        az_copy(up).wait_recv()

        @pl.when(me > 0)
        def _(up=up):
            corner_copy(up, 1).wait_recv()

        @pl.when(me < size - 1)
        def _(up=up):
            corner_copy(up, 0).wait_recv()

    out_ref[0] = (row_sum(0) + rows[1] + rows[2]) / 9.0
    out_ref[beams - 1] = (rows[beams - 1] + rows[beams] + row_sum(beams + 1)) / 9.0

    for i in range(steps):
        low_copy(i).wait_send()
        high_copy(i).wait_send()
        pair_copy(i).wait_send()
        for side, owner in owners:

            @pl.when(z != owner)
            def _(side=side, i=i):
                for copy in code_copies(side, i, z):
                    copy.wait_send()

    mask_copy.wait_send()

    @pl.when(is_mid)
    def _():
        for d in range(1, size):
            send_copy(d, 0).wait_send()

    for up in range(2):
        az_copy(up).wait_send()

    for side in range(2):

        @pl.when(me < size - 1 if side else me > 0)
        def _(side=side):
            for b in range(beams):
                tile_copy(side, b).wait_send()
            for up in range(2):
                corner_copy(up, side).wait_send()


def chain(echoes, arc_start, arc_offsets, doppler_bins, steer_angles, train_mask):
    columns, num_pulses, cells = echoes.shape[1:]
    num_sel = arc_offsets.shape[1]
    num_chan = doppler_bins.shape[1]
    size = lax.axis_size("rng")
    beams = BEAMS // lax.axis_size("az")
    dof = BINS * num_sel
    steps = beams // 2
    n = size // 2
    width = ARC // 2
    w = width // steps
    side_chan = num_chan // 2
    half = side_chan * dof
    items = steps * side_chan
    lanes = 128
    with jax.ensure_compile_time_eval():
        table_re, table_im = doppler_table(num_pulses)
        table = np.block([[table_re, -table_im], [table_im, table_re]])
    source = np.arange(lanes)[:, None]
    target = np.arange((2 * BINS + 1) * lanes)[None, :]
    block, place = target // lanes, target % lanes
    wanted = np.where(
        block < 2 * BINS, block * num_sel + place % num_sel, 2 * dof + np.minimum(place, 3)
    )
    spread = jnp.asarray(source == wanted, jnp.bfloat16)
    vm = pltpu.VMEM
    sm = pltpu.SMEM
    dma = pltpu.SemaphoreType.DMA
    f32 = jnp.float32
    bf16 = jnp.bfloat16
    i32 = jnp.int32
    i16 = jnp.int16
    tile = (num_chan, cells)
    scratch = [
        sm(arc_start.shape, i32),
        sm(arc_offsets.T.shape, i32),
        sm(doppler_bins.T.shape, i32),
        sm(train_mask.T.shape, i32),
        vm(steer_angles.T.shape, f32),
        vm(doppler_bins.T.shape, i32),
        vm(table.shape, bf16),
        vm(spread.shape, bf16),
        vm((2,) + steer_angles.T.shape, f32),
        vm((2, columns + 2 * width, num_pulses, cells), bf16),
        vm((steps, 2, w, num_pulses, cells), bf16),
        vm((steps, 2, w, num_pulses, cells), bf16),
        vm((beams, 2, num_pulses, num_sel, cells), bf16),
        vm((beams, 2, dof, half), f32),
        vm((steps, 2, dof, half), f32),
        vm((steps, 2, dof, half), i16),
        vm((steps, 2, 1, half + lanes), f32),
        vm((steps, n, dof, half), i16),
        vm((steps, n, 1, half + lanes), f32),
        vm((steps, dof, half), f32),
        vm((lanes, lanes), f32),
        vm((dof, items, dof), f32),
        vm((dof, dof, items), f32),
        vm((dof, dof, items), f32),
        vm((dof, dof, items), f32),
        vm((dof, items), f32),
        vm((dof, items), f32),
        vm((dof, items), f32),
        vm((dof, items), f32),
        vm((2, beams, cells), f32),
        vm((beams, lanes), f32),
        vm((steps, 1, lanes), f32),
        vm((items, lanes), bf16),
        vm((2, 2, items, lanes), bf16),
        vm((2, 2, items, spread.shape[1]), f32),
        vm((beams + 2,) + tile, f32),
        vm((beams + 2,) + tile, f32),
        vm((beams + 2,) + tile, f32),
        vm((beams + 2,) + tile, f32),
        dma((9,)),
        dma((2, steps)),
        dma((2, steps)),
        dma((steps,)),
        dma((steps,)),
        dma((2, steps, 2)),
        dma((2, steps, n)),
        dma,
        dma,
        dma((size,)),
        dma((2, 2)),
        dma((2, beams)),
        dma((2, beams)),
        dma((2,)),
        dma((2,)),
        dma((2, 2)),
        dma((2, 2)),
    ]
    return pl.pallas_call(
        chain_kernel,
        in_specs=[pl.BlockSpec(memory_space=pl.ANY)] * 8,
        out_specs=pl.BlockSpec(memory_space=vm),
        out_shape=jax.ShapeDtypeStruct((beams,) + tile, f32),
        scratch_shapes=scratch,
        compiler_params=pltpu.CompilerParams(
            collective_id=2, has_side_effects=True, vmem_limit_bytes=CHAIN_VMEM
        ),
        name="chain",
    )(
        arc_start,
        arc_offsets.T,
        doppler_bins.T,
        train_mask.T,
        steer_angles.T,
        echoes,
        jnp.asarray(table),
        spread,
    )


def body(echoes, arc_start, arc_offsets, doppler_bins, steer_angles, train_mask):
    columns = echoes.shape[1]
    num_pulses = echoes.shape[2]
    cells = echoes.shape[3]
    num_sel = arc_offsets.shape[1]
    chan_count = doppler_bins.shape[1]
    cycle_size = lax.axis_size("az")
    cycle_pos = lax.axis_index("az")
    rng_size = lax.axis_size("rng")
    beam_count = BEAMS // cycle_size
    item_count = beam_count * chan_count
    dof = BINS * num_sel
    pairs = beam_count // 2
    if (
        columns == ARC
        and beam_count % 2 == 0
        and pairs * (COLS // BEAMS) == ARC // 2
        and rng_size == 8
        and cycle_size > 2
        and cells == 128
        and chan_count % 16 == 0
        and chan_count // 2 * dof % 128 == 0
        and 2 * dof + 8 <= 128
        and dof % 16 == 0
        and pairs * (chan_count // 2) <= 128
    ):
        return chain(echoes, arc_start, arc_offsets, doppler_bins, steer_angles, train_mask)
    table_re, table_im = doppler_table(num_pulses)
    table = jnp.concatenate(
        [jnp.concatenate([table_re, -table_im], 1), jnp.concatenate([table_im, table_re], 1)], 0
    )

    def own(x):
        return lax.dynamic_slice_in_dim(x, cycle_pos * beam_count, beam_count, axis=0)

    arc_first = (own(arc_start) - cycle_pos * columns + ARC // 2) % COLS
    col_index = arc_first[:, None] + own(arc_offsets)
    bins_own = own(doppler_bins)
    angles = own(steer_angles)
    block_count = train_mask.shape[1]
    cell_mask = (
        jnp.broadcast_to(train_mask[:, :, None], (beam_count, block_count, BLK))
        .reshape(beam_count, 1, block_count * BLK)
        .astype(jnp.bfloat16)
    )
    smem = pl.BlockSpec(memory_space=pltpu.SMEM)

    def snap_gram(extended, first, last, base):
        share = last - first
        ext_cols = extended.shape[1]
        return pl.pallas_call(
            snap_gram_kernel,
            grid=(share,),
            in_specs=[
                smem,
                smem,
                smem,
                smem,
                pl.BlockSpec((2, ext_cols, num_pulses, cells), lambda b: (0, 0, 0, 0)),
                pl.BlockSpec(table.shape, lambda b: (0, 0)),
                pl.BlockSpec((1, 1, cells), lambda b: (b, 0, 0)),
            ],
            out_specs=[
                pl.BlockSpec((1, 2, num_pulses, num_sel, cells), lambda b: (b, 0, 0, 0, 0)),
                pl.BlockSpec((1, dof, chan_count * dof), lambda b: (b, 0, 0)),
            ],
            out_shape=[
                jax.ShapeDtypeStruct((share, 2, num_pulses, num_sel, cells), jnp.bfloat16),
                jax.ShapeDtypeStruct((share, dof, chan_count * dof), jnp.float32),
            ],
            compiler_params=pltpu.CompilerParams(vmem_limit_bytes=VMEM_LIMIT),
            cost_estimate=pl.CostEstimate(
                flops=share * 600_000_000, bytes_accessed=share * 1_500_000, transcendentals=0
            ),
            name="snap_gram",
        )(
            col_index[first:last] - base,
            bins_own[first:last],
            jnp.cos(angles)[first:last],
            jnp.sin(angles)[first:last],
            extended,
            table,
            cell_mask[first:last],
        )

    width = ARC // 2
    forward = [(i, (i + 1) % cycle_size) for i in range(cycle_size)]
    backward = [(target, source) for source, target in forward]
    low = lax.ppermute(echoes[:, columns - width :], "az", forward)
    high = lax.ppermute(echoes[:, :width], "az", backward)
    step = COLS // BEAMS
    half = beam_count // 2
    if (half - 1) * step + step - 1 + ARC - 1 < width + columns and half * step >= width:
        v_lo, gram_lo = snap_gram(jnp.concatenate([low, echoes], 1), 0, half, 0)
        high, v_lo, gram_lo = lax.optimization_barrier((high, v_lo, gram_lo))
        v_hi, gram_hi = snap_gram(jnp.concatenate([echoes, high], 1), half, beam_count, width)
        v_parts = (v_lo, v_hi)
        grams = (gram_lo, gram_hi)
        if rng_size % 4 or item_count // rng_size < chan_count:
            grams = (jnp.concatenate(grams, 0),)
    else:
        v_one, gram_one = snap_gram(jnp.concatenate([low, echoes, high], 1), 0, beam_count, 0)
        v_parts = (v_one,)
        grams = (gram_one,)

    per = item_count // rng_size
    if per < chan_count:
        split = chan_count // per
        gram = grams[0].reshape(beam_count, dof, split, per * dof)
        grams = (jnp.swapaxes(gram, 1, 2).reshape(beam_count * split, dof, per * dof),)
        width = per
    else:
        width = chan_count
    vm = pltpu.VMEM
    dma = pltpu.SemaphoreType.DMA
    line = rng_size // 2
    chunk = (grams[0].shape[0] * len(grams) // rng_size, dof, grams[0].shape[2])
    part = pl.pallas_call(
        functools.partial(scatter_kernel, line, len(grams)),
        in_specs=[pl.BlockSpec(memory_space=vm)] * len(grams),
        out_specs=pl.BlockSpec(memory_space=vm),
        out_shape=jax.ShapeDtypeStruct(chunk, jnp.float32),
        scratch_shapes=[vm((line,) + chunk, jnp.float32)] * 4 + [dma((line,))] * 6,
        compiler_params=pltpu.CompilerParams(
            collective_id=0, has_side_effects=True, vmem_limit_bytes=VMEM_LIMIT
        ),
        name="scatter",
    )(*[g.reshape((rng_size // len(grams),) + chunk) for g in grams])
    solved = pl.pallas_call(
        solve_kernel,
        out_shape=jax.ShapeDtypeStruct((2 * dof + 8, per), jnp.float32),
        scratch_shapes=[
            vm((dof, per, dof), jnp.float32),
            vm((dof, dof, per), jnp.float32),
            vm((dof, dof, per), jnp.float32),
            vm((dof, dof, per), jnp.float32),
            vm((dof, per), jnp.float32),
            vm((dof, per), jnp.float32),
            vm((dof, per), jnp.float32),
            vm((dof, per), jnp.float32),
        ],
        compiler_params=pltpu.CompilerParams(vmem_limit_bytes=VMEM_LIMIT),
        name="solve",
    )(part)
    lanes = 128
    local_count = (BLK * jnp.sum(train_mask, axis=1)).astype(jnp.float32)
    pad_rows = -per % 8
    payload = jnp.concatenate(
        [
            jnp.pad(solved.T, ((0, pad_rows), (0, lanes - solved.shape[0]))),
            jnp.broadcast_to(local_count[:, None], (beam_count, lanes)),
        ],
        0,
    )
    halves = len(v_parts)
    any_spec = pl.BlockSpec(memory_space=pl.ANY)
    block = (chan_count, cells)
    out = pl.pallas_call(
        functools.partial(apply_kernel, halves, per, dof),
        in_specs=[pl.BlockSpec(memory_space=vm)] * 2 + [any_spec] * halves,
        out_specs=pl.BlockSpec(memory_space=vm),
        out_shape=jax.ShapeDtypeStruct((beam_count,) + block, jnp.float32),
        scratch_shapes=[
            vm((beam_count, 2, num_pulses, num_sel, cells), jnp.bfloat16),
            vm((rng_size,) + payload.shape, jnp.float32),
            vm((beam_count,) + block, jnp.float32),
            vm((2, 8, item_count), jnp.float32),
            vm((2, 8, item_count), jnp.float32),
            vm((beam_count,) + block, jnp.float32),
            vm(block, jnp.float32),
            vm(block, jnp.float32),
            dma((halves,)),
            dma((rng_size,)),
            dma((rng_size,)),
            dma((2,)),
            dma((2,)),
            dma((2,)),
            dma((2,)),
        ],
        compiler_params=pltpu.CompilerParams(
            collective_id=1, has_side_effects=True, vmem_limit_bytes=VMEM_LIMIT
        ),
        name="apply",
    )(payload, bins_own[:, :, None], *v_parts)
    return out


def solution(mesh):
    return jax.shard_map(
        body,
        mesh=mesh,
        in_specs=(P(None, "az", None, "rng"), P(), P(), P(), P(), P("az", "rng")),
        out_specs=P("az", None, "rng"),
        check_vma=False,
    )
```

```python
import functools

import jax
import numpy as np
import jax.numpy as jnp
from jax import lax
from jax.experimental import pallas as pl
from jax.experimental.pallas import tpu as pltpu
from jax.sharding import PartitionSpec as P


COLS = 256
ARC = 64
BINS = 3
BEAMS = 64
BLK = 128
LOADING = 0.1
VMEM_LIMIT = 48 << 20
CHAIN_VMEM = 66_200_000
CODE_TOP = 32000.0
LAG = 3
LATE = 2


def doppler_table(num_pulses):
    freq_ids = jnp.arange(num_pulses, dtype=jnp.int32)
    phase_steps = freq_ids[:, None] * freq_ids[None, :] % num_pulses
    phase_angle = -2.0 * jnp.pi / num_pulses * phase_steps.astype(jnp.float32)
    return (jnp.cos(phase_angle).astype(jnp.bfloat16), jnp.sin(phase_angle).astype(jnp.bfloat16))


def snap_gram_kernel(
    col_ref, bins_ref, cos_ref, sin_ref, ext_ref, table_ref, mask_ref, v_ref, gram_ref
):
    beam = pl.program_id(0)
    pulses = ext_ref.shape[2]
    num_sel = col_ref.shape[1]
    num_chan = bins_ref.shape[1]
    table = table_ref[...]
    parts_re, parts_im = [], []
    for j in range(num_sel):
        col = col_ref[beam, j]
        data = jnp.concatenate([ext_ref[0, col], ext_ref[1, col]], axis=0)
        spec = jnp.dot(table, data, preferred_element_type=jnp.float32)
        cosine = cos_ref[beam, j]
        sine = sin_ref[beam, j]
        spec_re = spec[:pulses]
        spec_im = spec[pulses:]
        parts_re.append(cosine * spec_re - sine * spec_im)
        parts_im.append(sine * spec_re + cosine * spec_im)
    for part, pieces in enumerate((parts_re, parts_im)):
        stacked = jnp.swapaxes(jnp.stack(pieces, 0), 0, 1)
        v_ref[0, part] = stacked.astype(jnp.bfloat16)
    dof = BINS * num_sel
    mask_row = mask_ref[0]
    row = lax.broadcasted_iota(jnp.int32, (dof, dof), 0)
    colm = lax.broadcasted_iota(jnp.int32, (dof, dof), 1)
    lower = row >= colm
    packed = []
    for k in range(num_chan):
        centre = bins_ref[beam, k]
        ids = [(centre + (q - BINS // 2 + pulses)) % pulses for q in range(BINS)]
        u_re = jnp.concatenate([v_ref[0, 0, f] for f in ids], 0)
        u_im = jnp.concatenate([v_ref[0, 1, f] for f in ids], 0)
        right = jnp.concatenate([u_re, u_im], 1)
        m_re = u_re * mask_row
        m_im = u_im * mask_row
        left = jnp.concatenate(
            [jnp.concatenate([m_re, m_im], 1), jnp.concatenate([m_im, -m_re], 1)], 0
        )
        both = lax.dot_general(
            left, right, (((1,), (1,)), ((), ())), preferred_element_type=jnp.float32
        )
        packed.append(jnp.where(lower, both[:dof], both[dof:]))
    gram_ref[0] = jnp.concatenate(packed, 1)


def solve_kernel(part_ref, out_ref, stack, turned, hr, hi, xr, xi, yr, yi):
    lead, dof, wide = part_ref.shape
    width = wide // dof
    lanes = lead * width
    nb = dof // 8
    group = min(8, lanes)
    for g in range(0, lanes, group):
        pieces = []
        for item in range(g, g + group):
            k = item % width
            pieces.append(part_ref[item // width, :, k * dof : (k + 1) * dof])
        stack[:, g : g + group, :] = jnp.swapaxes(jnp.stack(pieces, 0), 0, 1)
    for i in range(dof):
        turned[i] = stack[i].T
    trace = jnp.zeros((1, lanes), jnp.float32)
    for i in range(dof):
        trace = trace + turned[i, i : i + 1, :]
    load = (LOADING / dof) * trace
    cube = (8, 8, lanes)
    row = lax.broadcasted_iota(jnp.int32, cube, 0)
    col = lax.broadcasted_iota(jnp.int32, cube, 1)
    for ib in range(nb):
        rows = slice(8 * ib, 8 * ib + 8)
        for jb in range(ib, nb):
            cols = slice(8 * jb, 8 * jb + 8)
            imag = turned[rows, cols, :]
            real = jnp.swapaxes(turned[cols, rows, :], 0, 1)
            if ib == jb:
                straight, flip = imag, real
                real = jnp.where(row >= col, straight, flip)
                real = jnp.where(row == col, real + load[None], real)
                imag = jnp.where(row < col, straight, jnp.where(row > col, -flip, 0.0))
            hr[rows, cols, :] = real
            hi[rows, cols, :] = imag
    yr[...] = jnp.ones_like(yr)
    yi[...] = jnp.zeros_like(yi)
    xr[...] = jnp.zeros_like(xr)
    xi[...] = jnp.zeros_like(xi)
    sub = lax.broadcasted_iota(jnp.int32, (8, lanes), 0)

    for kb in range(nb):

        def step(k, carry, kb=kb):
            pivot = 1.0 / hr[k, pl.ds(k, 1), :]
            rr = [hr[k, 8 * b : 8 * b + 8, :] for b in range(kb, nb)]
            ri = [hi[k, 8 * b : 8 * b + 8, :] for b in range(kb, nb)]
            gr = jnp.broadcast_to(yr[pl.ds(k, 1), :], (8, lanes))
            gi = jnp.broadcast_to(yi[pl.ds(k, 1), :], (8, lanes))
            for ib in range(kb, nb):
                fr = rr[ib - kb] * pivot
                fi = -ri[ib - kb] * pivot
                if ib == kb:
                    live = sub + 8 * kb > k
                    fr = jnp.where(live, fr, 0.0)
                    fi = jnp.where(live, fi, 0.0)
                own = slice(8 * ib, 8 * ib + 8)
                yr[own, :] = yr[own, :] - (fr * gr - fi * gi)
                yi[own, :] = yi[own, :] - (fr * gi + fi * gr)
                for s in range(8):
                    i = 8 * ib + s
                    cr = jnp.broadcast_to(fr[s : s + 1], (8, lanes))
                    ci = jnp.broadcast_to(fi[s : s + 1], (8, lanes))
                    for b in range(ib, nb):
                        pr, pi = rr[b - kb], ri[b - kb]
                        sl = slice(8 * b, 8 * b + 8)
                        hr[i, sl, :] = hr[i, sl, :] - (cr * pr - ci * pi)
                        hi[i, sl, :] = hi[i, sl, :] - (cr * pi + ci * pr)
            return carry

        lax.fori_loop(8 * kb, 8 * kb + 8, step, 0)

    for ib in reversed(range(nb)):

        def back(t, carry, ib=ib):
            i = 8 * ib + 7 - t
            sr = jnp.zeros((8, lanes), jnp.float32)
            si = jnp.zeros((8, lanes), jnp.float32)
            for b in range(ib, nb):
                sl = slice(8 * b, 8 * b + 8)
                ar, ai = hr[i, sl, :], hi[i, sl, :]
                br, bi = xr[sl, :], xi[sl, :]
                sr = sr + (ar * br - ai * bi)
                si = si + (ar * bi + ai * br)
            pivot = 1.0 / hr[i, pl.ds(i, 1), :]
            top_r = yr[pl.ds(i, 1), :]
            top_i = yi[pl.ds(i, 1), :]
            xr[pl.ds(i, 1), :] = (top_r - jnp.sum(sr, 0, keepdims=True)) * pivot
            xi[pl.ds(i, 1), :] = (top_i - jnp.sum(si, 0, keepdims=True)) * pivot
            return carry

        lax.fori_loop(0, 8, back, 0)
    out_ref[:dof, :lanes] = xr[...]
    out_ref[dof : 2 * dof, :lanes] = xi[...]
    out_ref[2 * dof : 2 * dof + 8, :lanes] = jnp.broadcast_to(
        jnp.sum(xr[...], 0, keepdims=True), (8, lanes)
    )


MESH = pl.DeviceIdType.MESH


def scatter_kernel(n, halves, *refs):
    g_refs = refs[:halves]
    out_ref, pair, acc, right, left, psend, precv, rsend, rrecv, lsend, lrecv = refs[halves:]
    share = n // halves

    def own(t, core):
        return g_refs[t // share].at[2 * (t % share) + core]

    me = lax.axis_index("rng")
    z = me // 2
    c = me % 2
    mate = 2 * z + 1 - c
    ahead = lax.rem(me + 2, 2 * n)
    behind = lax.rem(me + 2 * n - 2, 2 * n)
    barrier = pltpu.get_barrier_semaphore()
    pl.semaphore_signal(barrier, inc=1, device_id={"rng": mate}, device_id_type=MESH)
    pl.semaphore_signal(barrier, inc=1, device_id={"rng": ahead}, device_id_type=MESH)
    pl.semaphore_signal(barrier, inc=1, device_id={"rng": behind}, device_id_type=MESH)
    pl.semaphore_wait(barrier, 3)

    order = []
    for t in range((n + 1) // 2):
        order.append(n - 1 - t)
        if t != n - 1 - t:
            order.append(t)

    def pair_copy(t):
        return pltpu.make_async_remote_copy(
            src_ref=own(t, 1 - c),
            dst_ref=pair.at[t],
            send_sem=psend.at[t],
            recv_sem=precv.at[t],
            device_id={"rng": mate},
            device_id_type=MESH,
        )

    def right_copy(t):
        return pltpu.make_async_remote_copy(
            src_ref=acc.at[t],
            dst_ref=right.at[t],
            send_sem=rsend.at[t],
            recv_sem=rrecv.at[t],
            device_id={"rng": ahead},
            device_id_type=MESH,
        )

    def left_copy(t):
        return pltpu.make_async_remote_copy(
            src_ref=acc.at[t],
            dst_ref=left.at[t],
            send_sem=lsend.at[t],
            recv_sem=lrecv.at[t],
            device_id={"rng": behind},
            device_id_type=MESH,
        )

    for t in order:
        pair_copy(t).start()
    for t in order:
        pair_copy(t).wait_recv()
        acc[t] = own(t, c)[...] + pair[t]

        @pl.when(jnp.logical_and(z == 0, t > 0))
        def _(t=t):
            right_copy(t).start()

        @pl.when(jnp.logical_and(z == n - 1, t < n - 1))
        def _(t=t):
            left_copy(t).start()

    for place in range(n):
        events = [(place + n - 1 - t, 0, t) for t in range(place + 1, n) if place > 0]
        events += [(n - 1 - place + t, 1, t) for t in range(place) if place < n - 1]

        @pl.when(z == place)
        def _(place=place, events=sorted(events)):
            for _, side, t in events:
                copy = left_copy(t) if side else right_copy(t)
                source = left if side else right
                copy.wait_recv()
                acc[t] = acc[t] + source[t]
                copy.start()
            total = acc[place]
            if place > 0:
                right_copy(place).wait_recv()
                total = total + right[place]
            if place < n - 1:
                left_copy(place).wait_recv()
                total = total + left[place]
            out_ref[...] = total

    for t in range(n):
        pair_copy(t).wait_send()

        @pl.when(z < t)
        def _(t=t):
            right_copy(t).wait_send()

        @pl.when(z > t)
        def _(t=t):
            left_copy(t).wait_send()


def apply_kernel(
    halves,
    per,
    dof,
    pay_ref,
    bins_ref,
    *refs,
):
    v_refs = refs[:halves]
    (out_ref, v_all, gat, power, edge, halo, sums, az_lo, az_hi) = refs[halves : halves + 9]
    (vsem, gsend, grecv, esend, erecv, asend, arecv) = refs[halves + 9 :]
    me = lax.axis_index("rng")
    az = lax.axis_index("az")
    n = lax.axis_size("rng")
    m = lax.axis_size("az")
    beams, num_chan, cells = out_ref.shape
    pulses, num_sel = v_all.shape[2], v_all.shape[3]
    taps = pulses * num_sel
    az_next = lax.rem(az + 1, m)
    az_prev = lax.rem(az + m - 1, m)
    barrier = pltpu.get_barrier_semaphore()
    for d in range(1, n):
        peer = lax.rem(me + d, n)
        pl.semaphore_signal(barrier, inc=1, device_id={"rng": peer}, device_id_type=MESH)
    for other in (az_next, az_prev):
        pl.semaphore_signal(barrier, inc=1, device_id={"az": other}, device_id_type=MESH)
    share = beams // halves
    loads = []
    for h in range(halves):
        load = pltpu.make_async_copy(v_refs[h], v_all.at[pl.ds(h * share, share)], vsem.at[h])
        load.start()
        loads.append(load)
    pl.semaphore_wait(barrier, n + 1)

    copies = []
    for d in range(1, n):
        peer = lax.rem(me + d, n)
        copy = pltpu.make_async_remote_copy(
            src_ref=pay_ref,
            dst_ref=gat.at[me],
            send_sem=gsend.at[d],
            recv_sem=grecv.at[d],
            device_id={"rng": peer},
            device_id_type=MESH,
        )
        copy.start()
        copies.append(copy)
    gat[me] = pay_ref[...]
    for load in loads:
        load.wait()
    for copy in copies:
        copy.wait_recv()
    rows = gat.shape[1] - beams
    count = jnp.zeros((beams, gat.shape[2]), jnp.float32)
    for r in range(n):
        count = count + gat[r, rows:, :]
    sums[0] = jnp.zeros(sums.shape[1:], jnp.float32)
    for b in range(beams):
        sums[b, :1, :] = count[b : b + 1]
    freq = lax.broadcasted_iota(jnp.int32, (num_chan, taps), 1) // num_sel
    lanes = gat.shape[2]
    lane = lax.broadcasted_iota(jnp.int32, (num_chan, lanes), 1)

    def one(b, carry):
        if per >= num_chan:
            ratio = per // num_chan
            start = pl.multiple_of((b % ratio) * num_chan, 8)
            w = gat[b // ratio, pl.ds(start, num_chan), :]
        else:
            split = num_chan // per
            w = jnp.concatenate([gat[b * split + t, :per, :] for t in range(split)], 0)
        w = w * sums[b, :1, :]
        quiet = w[:, 2 * dof : 2 * dof + 1]
        centre = bins_ref[b]
        planes = []
        hits = []
        for q in range(BINS):
            f = lax.rem(centre + (q - BINS // 2 + pulses), pulses)
            hits.append(freq == f)
        for part in range(2):
            plane = jnp.zeros((num_chan, taps), jnp.float32)
            for q in range(BINS):
                start = part * dof + q * num_sel
                piece = pltpu.roll(w, (lanes - start) % lanes, 1) if start else w
                piece = jnp.where(lane < num_sel, piece, 0.0)
                span = num_sel
                while span < lanes:
                    piece = piece + pltpu.roll(piece, span, 1)
                    span *= 2
                tiled = jnp.concatenate([piece] * (taps // lanes), 1)
                plane = jnp.where(hits[q], tiled, plane)
            planes.append(plane)
        top = jnp.concatenate([planes[0], planes[1]], 1)
        low = jnp.concatenate([-planes[1], planes[0]], 1)
        lhs = jnp.concatenate([top, low], 0).astype(jnp.bfloat16)
        flat = v_all[b].reshape(2 * taps, cells)
        proj = jnp.dot(lhs, flat, preferred_element_type=jnp.float32)
        p0 = proj[:num_chan]
        p1 = proj[num_chan:]
        power[b] = (p0 * p0 + p1 * p1) / quiet
        return carry

    lax.fori_loop(0, beams, one, 0)
    items = beams * num_chan
    turned = power[...].reshape(items, cells).T
    edge[0] = turned[:8]
    edge[1] = turned[cells - 8 :]

    def edge_copy(side):
        target = lax.rem(me + 1, n) if side else lax.rem(me + n - 1, n)
        return pltpu.make_async_remote_copy(
            src_ref=edge.at[side],
            dst_ref=halo.at[side],
            send_sem=esend.at[side],
            recv_sem=erecv.at[side],
            device_id={"rng": target},
            device_id_type=MESH,
        )

    for side in range(2):
        edge_copy(side).start()
    for side in range(2):
        edge_copy(side).wait()
    before = jnp.where(me > 0, halo[1, 7:8], 0.0)
    after = jnp.where(me < n - 1, halo[0, 0:1], 0.0)
    turned = (
        jnp.concatenate([before, turned[:-1]], 0)
        + turned
        + jnp.concatenate([turned[1:], after], 0)
    )
    sums[...] = turned.T.reshape(beams, num_chan, cells)
    up = pltpu.make_async_remote_copy(
        src_ref=sums.at[beams - 1],
        dst_ref=az_lo,
        send_sem=asend.at[0],
        recv_sem=arecv.at[0],
        device_id={"az": az_next},
        device_id_type=MESH,
    )
    down = pltpu.make_async_remote_copy(
        src_ref=sums.at[0],
        dst_ref=az_hi,
        send_sem=asend.at[1],
        recv_sem=arecv.at[1],
        device_id={"az": az_prev},
        device_id_type=MESH,
    )
    up.start()
    down.start()
    for b in range(1, beams - 1):
        out_ref[b] = (sums[b - 1] + sums[b] + sums[b + 1]) / 9.0
    up.wait_recv()
    down.wait_recv()
    out_ref[0] = (az_lo[...] + sums[0] + sums[1]) / 9.0
    out_ref[beams - 1] = (sums[beams - 2] + sums[beams - 1] + az_hi[...]) / 9.0
    up.wait_send()
    down.wait_send()
    for copy in copies:
        copy.wait_send()


def gram_of(v_ref, beam, bins, mask_row):
    pulses = v_ref.shape[2]
    num_sel = v_ref.shape[3]
    dof = BINS * num_sel
    row = lax.broadcasted_iota(jnp.int32, (dof, dof), 0)
    colm = lax.broadcasted_iota(jnp.int32, (dof, dof), 1)
    lower = row >= colm
    packed = []
    for centre in bins:
        ids = [lax.rem(centre + (q - BINS // 2 + pulses), pulses) for q in range(BINS)]
        u_re = jnp.concatenate([v_ref[beam, 0, f] for f in ids], 0)
        u_im = jnp.concatenate([v_ref[beam, 1, f] for f in ids], 0)
        right = jnp.concatenate([u_re, u_im], 1)
        m_re = u_re * mask_row
        m_im = u_im * mask_row
        left = jnp.concatenate(
            [jnp.concatenate([m_re, m_im], 1), jnp.concatenate([m_im, -m_re], 1)], 0
        )
        both = lax.dot_general(
            left, right, (((1,), (1,)), ((), ())), preferred_element_type=jnp.float32
        )
        packed.append(jnp.where(lower, both[:dof], both[dof:]))
    return packed


def chain_kernel(
    early,
    start_hbm,
    offs_hbm,
    bins_hbm,
    train_hbm,
    angle_hbm,
    echoes,
    table_hbm,
    spread_hbm,
    out_ref,
    start_ref,
    offs_ref,
    bins_ref,
    train_ref,
    angle_ref,
    chan_ref,
    table_ref,
    spread_ref,
    turn,
    ext,
    low,
    high,
    v_all,
    gram,
    pair,
    coded,
    scale,
    code_in,
    scale_in,
    part,
    solved,
    stack,
    turned,
    hr,
    hi,
    xr,
    xi,
    yr,
    yi,
    masks,
    totals,
    counts,
    pay,
    gat_e,
    gat_l,
    tiles_e,
    tiles_l,
    pw,
    pl_left,
    pl_right,
    rows,
    esem,
    hsend,
    hrecv,
    psend,
    precv,
    dsend,
    drecv,
    msend,
    mrecv,
    gsend,
    grecv,
    hello,
    lsend,
    lrecv,
    tsend,
    trecv,
    asend,
    arecv,
):
    me = lax.axis_index("rng")
    az = lax.axis_index("az")
    size = lax.axis_size("rng")
    m = lax.axis_size("az")
    n = size // 2
    z = me // 2
    c = lax.rem(me, 2)
    beams, num_chan, cells = out_ref.shape
    columns = echoes.shape[1]
    pulses = echoes.shape[2]
    num_sel = offs_ref.shape[0]
    blocks = train_ref.shape[0]
    dof = BINS * num_sel
    taps = pulses * num_sel
    steps = beams // 2
    width = ARC // 2
    w = width // steps
    side_chan = num_chan // 2
    half = side_chan * dof
    lanes = pay.shape[1]
    az_next = lax.rem(az + 1, m)
    az_prev = lax.rem(az + m - 1, m)
    ahead = lax.rem(me + 1, size)
    behind = lax.rem(me + size - 1, size)
    mate = 2 * z + 1 - c
    mid_l = n // 2 - 1
    mid_r = n // 2
    late = steps - early
    middles = ((0, mid_l), (1, mid_r))
    ends = ((0, 0), (1, n - 1))
    is_mid = jnp.logical_or(z == mid_l, z == mid_r)

    loads = [
        pltpu.make_async_copy(src, dst, esem.at[i])
        for i, (src, dst) in enumerate(
            (
                (start_hbm, start_ref),
                (offs_hbm, offs_ref),
                (bins_hbm, bins_ref),
                (train_hbm, train_ref),
                (angle_hbm, angle_ref),
                (bins_hbm, chan_ref),
                (table_hbm, table_ref),
                (spread_hbm, spread_ref),
                (echoes, ext.at[:, width : width + columns]),
            )
        )
    ]
    barrier = pltpu.get_barrier_semaphore()
    for other in (az_next, az_prev):
        pl.semaphore_signal(barrier, inc=1, device_id={"az": other}, device_id_type=MESH)
    pl.semaphore_signal(barrier, inc=1, device_id={"rng": mate}, device_id_type=MESH)
    for place in range(n):
        near = jnp.logical_or(is_mid, place in (mid_l, mid_r))

        @pl.when(jnp.logical_and(z != place, near))
        def _(place=place):
            pl.semaphore_signal(
                barrier, inc=1, device_id={"rng": 2 * place + c}, device_id_type=MESH
            )

    for load in loads:
        load.start()
    pl_left[...] = jnp.zeros(pl_left.shape, jnp.float32)
    pl_right[...] = jnp.zeros(pl_right.shape, jnp.float32)
    solved[...] = jnp.zeros(solved.shape, jnp.float32)
    part[...] = jnp.zeros(part.shape, jnp.float32)
    pl.semaphore_wait(barrier, 3 + jnp.where(is_mid, n - 1, 2))

    def low_copy(i):
        return pltpu.make_async_remote_copy(
            src_ref=echoes.at[:, pl.ds(columns - w * (i + 1), w)],
            dst_ref=low.at[i],
            send_sem=hsend.at[0, i],
            recv_sem=hrecv.at[0, i],
            device_id={"az": az_next},
            device_id_type=MESH,
        )

    def high_copy(i):
        return pltpu.make_async_remote_copy(
            src_ref=echoes.at[:, pl.ds(w * i, w)],
            dst_ref=high.at[i],
            send_sem=hsend.at[1, i],
            recv_sem=hrecv.at[1, i],
            device_id={"az": az_prev},
            device_id_type=MESH,
        )

    for i in range(steps):
        low_copy(i).start()
        high_copy(i).start()
    for side, middle in middles:

        @pl.when(z == middle)
        def _(side=side):
            end = 2 * (n - 1 if side else 0) + c
            pl.semaphore_signal(hello, inc=1, device_id={"rng": end}, device_id_type=MESH)

    for load in loads:
        load.wait()

    cell = lax.broadcasted_iota(jnp.int32, (1, cells), 1) // BLK
    for b in range(beams):
        row = jnp.zeros((1, cells), jnp.float32)
        for blk in range(blocks):
            row = jnp.where(cell == blk, train_ref[blk, b].astype(jnp.float32), row)
        masks[0, b : b + 1, :] = row

    mask_copy = pltpu.make_async_remote_copy(
        src_ref=masks.at[0],
        dst_ref=masks.at[1],
        send_sem=msend,
        recv_sem=mrecv,
        device_id={"rng": mate},
        device_id_type=MESH,
    )
    mask_copy.start()
    turn[0] = jnp.cos(angle_ref[...])
    turn[1] = jnp.sin(angle_ref[...])
    mask_copy.wait_recv()
    totals[...] = jnp.broadcast_to(
        jnp.sum(masks[0] + masks[1], 1, keepdims=True), totals.shape
    )

    def mine(t):
        return jnp.where(c == 0, steps - 1 - t, steps + t)

    def theirs(t):
        return jnp.where(c == 0, steps + t, steps - 1 - t)

    def owner_of(side, t):
        far, near = (n - 1, mid_r) if side else (0, mid_l)
        return jnp.where(t < early, far, near)

    def pair_copy(t):
        return pltpu.make_async_remote_copy(
            src_ref=gram.at[theirs(t)],
            dst_ref=pair.at[t],
            send_sem=psend.at[t],
            recv_sem=precv.at[t],
            device_id={"rng": mate},
            device_id_type=MESH,
        )

    def code_copies(side, t, source):
        owner = 2 * owner_of(side, t) + c
        return [
            pltpu.make_async_remote_copy(
                src_ref=src.at[t, side],
                dst_ref=dst.at[t, source],
                send_sem=dsend.at[i, t, side],
                recv_sem=drecv.at[i, t, source],
                device_id={"rng": owner},
                device_id_type=MESH,
            )
            for i, (src, dst) in enumerate(((coded, code_in), (scale, scale_in)))
        ]

    table = table_ref[...]
    blane = lax.broadcasted_iota(jnp.int32, angle_ref.shape, 1)

    def one_beam(b):
        bg = az * beams + b
        first = lax.rem(start_ref[bg] - az * columns + (width + COLS), COLS)
        first = jnp.minimum(first, ext.shape[1] - ARC)
        here = blane == bg
        cosine = jnp.sum(jnp.where(here, turn[0], 0.0), 1, keepdims=True)
        sine = jnp.sum(jnp.where(here, turn[1], 0.0), 1, keepdims=True)
        cosine = jnp.broadcast_to(cosine, (num_sel, cells))[None]
        sine = jnp.broadcast_to(sine, (num_sel, cells))[None]
        parts_re, parts_im = [], []
        for j in range(num_sel):
            col = first + offs_ref[j, bg]
            data = jnp.concatenate([ext[0, col], ext[1, col]], axis=0)
            spec = jnp.dot(table, data, preferred_element_type=jnp.float32)
            parts_re.append(spec[:pulses])
            parts_im.append(spec[pulses:])
        spec_re = jnp.swapaxes(jnp.stack(parts_re, 0), 0, 1)
        spec_im = jnp.swapaxes(jnp.stack(parts_im, 0), 0, 1)
        v_all[b, 0] = (cosine * spec_re - sine * spec_im).astype(jnp.bfloat16)
        v_all[b, 1] = (sine * spec_re + cosine * spec_im).astype(jnp.bfloat16)
        mask_row = masks[0, pl.ds(b, 1), :].astype(jnp.bfloat16)
        bins = [bins_ref[k, bg] for k in range(num_chan)]
        packed = gram_of(v_all, b, bins, mask_row)
        gram[b, 0] = jnp.concatenate(packed[:side_chan], 1)
        gram[b, 1] = jnp.concatenate(packed[side_chan:], 1)

    def slot(s, carry):
        @pl.when(s < steps)
        def _():
            low_copy(s).wait_recv()
            high_copy(s).wait_recv()
            ext[:, pl.ds(width - w * (s + 1), w)] = low[s]
            ext[:, pl.ds(width + columns + w * s, w)] = high[s]
            one_beam(theirs(s))
            pair_copy(s).start()

        t = s - 1

        @pl.when(jnp.logical_and(t >= 0, t < steps))
        def _():
            pair_copy(t).wait_recv()
            own = mine(t)
            number = totals[pl.ds(own, 1), :]
            row = jnp.where(t < early, t, t - early)
            for side in range(2):
                total = gram[own, side] + pair[t, side]
                owner = owner_of(side, t)

                @pl.when(z == owner)
                def _(total=total):
                    part[row] = total
                    counts[row] = number

                @pl.when(z != owner)
                def _(side=side, total=total):
                    top = jnp.max(jnp.abs(total), 0, keepdims=True)
                    top = jnp.maximum(top, 1e-30)
                    code = jnp.round(total * (CODE_TOP / top))
                    coded[t, side] = code.astype(jnp.int32).astype(jnp.int16)
                    scale[t, side, :, :half] = top * (1.0 / CODE_TOP)
                    scale[t, side, :, half:] = number
                    for copy in code_copies(side, t, z):
                        copy.start()

        tt = s - LAG

        @pl.when(jnp.logical_and(tt >= 0, tt < steps))
        def _():
            row = jnp.where(tt < early, tt, tt - early)
            for side in range(2):
                for owner, is_early in ((ends[side][1], True), (middles[side][1], False)):
                    right_time = tt < early if is_early else tt >= early

                    @pl.when(jnp.logical_and(z == owner, right_time))
                    def _(side=side, owner=owner):
                        total = part[row]
                        number = counts[row]
                        for source in range(n):
                            if source != owner:
                                for copy in code_copies(side, tt, source):
                                    copy.wait_recv()
                                code = code_in[tt, source].astype(jnp.int32)
                                code = code.astype(jnp.float32)
                                total = total + code * scale_in[tt, source, :, :half]
                                number = number + scale_in[tt, source, :, half:]
                        part[row] = total
                        counts[row] = number

        @pl.when(s < steps)
        def _():
            one_beam(mine(s))

        return carry

    @pl.when(jnp.logical_not(is_mid))
    def _():
        pl.semaphore_wait(hello, 1)

    lax.fori_loop(0, steps + LAG, slot, 0)

    items = pay.shape[0]

    def send_copy(d, side, buf, which):
        return pltpu.make_async_remote_copy(
            src_ref=pay.at[: buf.shape[2]],
            dst_ref=buf.at[side, c],
            send_sem=gsend.at[d],
            recv_sem=grecv.at[which, side, c],
            device_id={"rng": lax.rem(me + d, size)},
            device_id_type=MESH,
        )

    solve_kernel(part, solved, stack, turned, hr, hi, xr, xi, yr, yi)
    flipped = solved[...].T
    scaled = []
    for t in range(items // side_chan):
        scaled.append(flipped[side_chan * t : side_chan * (t + 1)] * counts[t])
    full = jnp.concatenate(scaled, 0)
    lane = lax.broadcasted_iota(jnp.int32, (items, lanes), 1)
    hi_part = full.astype(jnp.bfloat16).astype(jnp.float32)
    rest = full - hi_part
    mid_part = rest.astype(jnp.bfloat16).astype(jnp.float32)
    lo_part = rest - mid_part
    split = jnp.where(
        lane == 2 * dof + 1, mid_part, jnp.where(lane == 2 * dof + 2, lo_part, hi_part)
    )
    pay[...] = split.astype(jnp.bfloat16)
    for which, (places, buf) in enumerate(((ends, gat_e), (middles, gat_l))):
        for side, owner in places:

            @pl.when(z == owner)
            def _(side=side, buf=buf, which=which):
                for d in range(1, size):
                    send_copy(d, side, buf, which).start()
                buf[side, c] = pay[: buf.shape[2]]

    freq = (lax.broadcasted_iota(jnp.int32, (num_chan, taps), 1) // num_sel).astype(jnp.float32)
    centres = chan_ref[...].astype(jnp.float32)

    def tile_copy(side, b):
        target = ahead if side else behind
        buf = pl_left if side else pl_right
        return pltpu.make_async_remote_copy(
            src_ref=pw.at[b + 1],
            dst_ref=buf.at[b + 1],
            send_sem=lsend.at[side, b],
            recv_sem=lrecv.at[side, b],
            device_id={"rng": target},
            device_id_type=MESH,
        )

    def az_copy(up):
        return pltpu.make_async_remote_copy(
            src_ref=pw.at[beams if up else 1],
            dst_ref=pw.at[0 if up else beams + 1],
            send_sem=tsend.at[up],
            recv_sem=trecv.at[up],
            device_id={"az": az_next if up else az_prev},
            device_id_type=MESH,
        )

    def corner_copy(up, side):
        buf = pl_left if side else pl_right
        return pltpu.make_async_remote_copy(
            src_ref=pw.at[beams if up else 1],
            dst_ref=buf.at[0 if up else beams + 1],
            send_sem=asend.at[up, side],
            recv_sem=arecv.at[up, side],
            device_id={
                "az": az_next if up else az_prev,
                "rng": ahead if side else behind,
            },
            device_id_type=MESH,
        )

    def one_power(b, tiles, t, core):
        start = pl.multiple_of(t * side_chan, side_chan)
        both = [tiles[side, core, pl.ds(start, side_chan), :] for side in range(2)]
        wide = jnp.concatenate(both, 0)
        tail = wide[:, 2 * BINS * lanes :]
        quiet = tail[:, :1] + tail[:, 1:2] + tail[:, 2:3]
        centre = jnp.sum(jnp.where(blane == az * beams + b, centres, 0.0), 1, keepdims=True)
        hits = []
        for q in range(BINS):
            f = centre + (q - BINS // 2)
            f = jnp.where(f < 0.0, f + pulses, jnp.where(f >= pulses, f - pulses, f))
            hits.append(freq == f)
        planes = []
        for p in range(2):
            plane = jnp.zeros((num_chan, taps), jnp.float32)
            for q in range(BINS):
                at = (p * BINS + q) * lanes
                piece = wide[:, at : at + lanes]
                tiled = jnp.concatenate([piece] * (taps // lanes), 1)
                plane = jnp.where(hits[q], tiled, plane)
            planes.append(plane)
        top = jnp.concatenate([planes[0], planes[1]], 1)
        bottom = jnp.concatenate([-planes[1], planes[0]], 1)
        lhs = jnp.concatenate([top, bottom], 0).astype(jnp.bfloat16)
        flat = v_all[b].reshape(2 * taps, cells)
        proj = jnp.dot(lhs, flat, preferred_element_type=jnp.float32)
        p0 = proj[:num_chan]
        p1 = proj[num_chan:]
        pw[b + 1] = (p0 * p0 + p1 * p1) / quiet

        @pl.when(me < size - 1)
        def _():
            tile_copy(1, b).start()

        @pl.when(me > 0)
        def _():
            tile_copy(0, b).start()

    def spread_weights(which, places, buf, tiles):
        for side, owner in places:
            for core in range(2):

                @pl.when(me != 2 * owner + core)
                def _(side=side, core=core):
                    pltpu.make_async_remote_copy(
                        src_ref=pay.at[: buf.shape[2]],
                        dst_ref=buf.at[side, core],
                        send_sem=gsend.at[0],
                        recv_sem=grecv.at[which, side, core],
                        device_id={"rng": ahead},
                        device_id_type=MESH,
                    ).wait_recv()

                tiles[side, core] = jnp.dot(
                    buf[side, core], spread_ref[...], preferred_element_type=jnp.float32
                )

    def early_power(t, carry):
        one_power(steps - 1 - t, tiles_e, t, 0)
        one_power(steps + t, tiles_e, t, 1)
        return carry

    def late_power(i, carry):
        one_power(i, tiles_l, late - 1 - i, 0)
        one_power(beams - 1 - i, tiles_l, late - 1 - i, 1)

        @pl.when(i == 0)
        def _():
            for up in range(2):
                az_copy(up).start()

                @pl.when(me < size - 1)
                def _(up=up):
                    corner_copy(up, 1).start()

                @pl.when(me > 0)
                def _(up=up):
                    corner_copy(up, 0).start()

        return carry

    spread_weights(0, ends, gat_e, tiles_e)
    lax.fori_loop(0, early, early_power, 0)
    spread_weights(1, middles, gat_l, tiles_l)
    lax.fori_loop(0, late, late_power, 0)

    lane = lax.broadcasted_iota(jnp.int32, (num_chan, cells), 1)

    def row_sum(i):
        mid = pw[i]
        back = pltpu.roll(jnp.where(lane == cells - 1, pl_left[i], mid), 1, 1)
        fore = pltpu.roll(jnp.where(lane == 0, pl_right[i], mid), cells - 1, 1)
        return back + mid + fore

    def finish(group):
        for b in group:

            @pl.when(me > 0)
            def _(b=b):
                tile_copy(1, b).wait_recv()

            @pl.when(me < size - 1)
            def _(b=b):
                tile_copy(0, b).wait_recv()

        for b in group:
            rows[b + 1] = row_sum(b + 1)

    def smooth(b):
        out_ref[b] = (rows[b] + rows[b + 1] + rows[b + 2]) / 9.0

    finish(range(late, beams - late))
    for b in range(late + 1, beams - late - 1):
        smooth(b)
    outer = [*range(late), *range(beams - late, beams)]
    finish(outer)
    for b in range(1, late + 1):
        smooth(b)
        smooth(beams - 1 - b)
    for up in range(2):
        az_copy(up).wait_recv()

        @pl.when(me > 0)
        def _(up=up):
            corner_copy(up, 1).wait_recv()

        @pl.when(me < size - 1)
        def _(up=up):
            corner_copy(up, 0).wait_recv()

    rows[0] = row_sum(0)
    rows[beams + 1] = row_sum(beams + 1)
    smooth(0)
    smooth(beams - 1)

    for i in range(steps):
        low_copy(i).wait_send()
        high_copy(i).wait_send()
        pair_copy(i).wait_send()
        for side in range(2):

            @pl.when(z != owner_of(side, i))
            def _(side=side, i=i):
                for copy in code_copies(side, i, z):
                    copy.wait_send()

    mask_copy.wait_send()

    for which, (buf, here) in enumerate(((gat_e, jnp.logical_not(is_mid)), (gat_l, is_mid))):

        @pl.when(here)
        def _(buf=buf, which=which):
            for d in range(1, size):
                send_copy(d, 0, buf, which).wait_send()

    for up in range(2):
        az_copy(up).wait_send()

    for side in range(2):

        @pl.when(me < size - 1 if side else me > 0)
        def _(side=side):
            for b in range(beams):
                tile_copy(side, b).wait_send()
            for up in range(2):
                corner_copy(up, side).wait_send()


def chain(echoes, arc_start, arc_offsets, doppler_bins, steer_angles, train_mask, early):
    columns, num_pulses, cells = echoes.shape[1:]
    num_sel = arc_offsets.shape[1]
    num_chan = doppler_bins.shape[1]
    size = lax.axis_size("rng")
    beams = BEAMS // lax.axis_size("az")
    dof = BINS * num_sel
    steps = beams // 2
    n = size // 2
    width = ARC // 2
    w = width // steps
    side_chan = num_chan // 2
    half = side_chan * dof
    late = steps - early
    most = max(early, late)
    items = most * side_chan
    lanes = 128
    with jax.ensure_compile_time_eval():
        table_re, table_im = doppler_table(num_pulses)
        table = np.block([[table_re, -table_im], [table_im, table_re]])
    source = np.arange(lanes)[:, None]
    target = np.arange((2 * BINS + 1) * lanes)[None, :]
    block, place = target // lanes, target % lanes
    wanted = np.where(
        block < 2 * BINS, block * num_sel + place % num_sel, 2 * dof + np.minimum(place, 3)
    )
    spread = jnp.asarray(source == wanted, jnp.bfloat16)
    vm = pltpu.VMEM
    sm = pltpu.SMEM
    dma = pltpu.SemaphoreType.DMA
    f32 = jnp.float32
    bf16 = jnp.bfloat16
    i32 = jnp.int32
    i16 = jnp.int16
    tile = (num_chan, cells)
    scratch = [
        sm(arc_start.shape, i32),
        sm(arc_offsets.T.shape, i32),
        sm(doppler_bins.T.shape, i32),
        sm(train_mask.T.shape, i32),
        vm(steer_angles.T.shape, f32),
        vm(doppler_bins.T.shape, i32),
        vm(table.shape, bf16),
        vm(spread.shape, bf16),
        vm((2,) + steer_angles.T.shape, f32),
        vm((2, columns + 2 * width, num_pulses, cells), bf16),
        vm((steps, 2, w, num_pulses, cells), bf16),
        vm((steps, 2, w, num_pulses, cells), bf16),
        vm((beams, 2, num_pulses, num_sel, cells), bf16),
        vm((beams, 2, dof, half), f32),
        vm((steps, 2, dof, half), f32),
        vm((steps, 2, dof, half), i16),
        vm((steps, 2, 1, half + lanes), f32),
        vm((steps, n, dof, half), i16),
        vm((steps, n, 1, half + lanes), f32),
        vm((most, dof, half), f32),
        vm((lanes, lanes), f32),
        vm((dof, items, dof), f32),
        vm((dof, dof, items), f32),
        vm((dof, dof, items), f32),
        vm((dof, dof, items), f32),
        vm((dof, items), f32),
        vm((dof, items), f32),
        vm((dof, items), f32),
        vm((dof, items), f32),
        vm((2, beams, cells), f32),
        vm((beams, lanes), f32),
        vm((most, 1, lanes), f32),
        vm((items, lanes), bf16),
        vm((2, 2, early * side_chan, lanes), bf16),
        vm((2, 2, late * side_chan, lanes), bf16),
        vm((2, 2, early * side_chan, spread.shape[1]), f32),
        vm((2, 2, late * side_chan, spread.shape[1]), f32),
        vm((beams + 2,) + tile, f32),
        vm((beams + 2,) + tile, f32),
        vm((beams + 2,) + tile, f32),
        vm((beams + 2,) + tile, f32),
        dma((9,)),
        dma((2, steps)),
        dma((2, steps)),
        dma((steps,)),
        dma((steps,)),
        dma((2, steps, 2)),
        dma((2, steps, n)),
        dma,
        dma,
        dma((size,)),
        dma((2, 2, 2)),
        pltpu.SemaphoreType.REGULAR,
        dma((2, beams)),
        dma((2, beams)),
        dma((2,)),
        dma((2,)),
        dma((2, 2)),
        dma((2, 2)),
    ]
    return pl.pallas_call(
        functools.partial(chain_kernel, early),
        in_specs=[pl.BlockSpec(memory_space=pl.ANY)] * 8,
        out_specs=pl.BlockSpec(memory_space=vm),
        out_shape=jax.ShapeDtypeStruct((beams,) + tile, f32),
        scratch_shapes=scratch,
        compiler_params=pltpu.CompilerParams(
            collective_id=2, has_side_effects=True, vmem_limit_bytes=CHAIN_VMEM
        ),
        name="chain",
    )(
        arc_start,
        arc_offsets.T,
        doppler_bins.T,
        train_mask.T,
        steer_angles.T,
        echoes,
        jnp.asarray(table),
        spread,
    )


def body(echoes, arc_start, arc_offsets, doppler_bins, steer_angles, train_mask):
    columns = echoes.shape[1]
    num_pulses = echoes.shape[2]
    cells = echoes.shape[3]
    num_sel = arc_offsets.shape[1]
    chan_count = doppler_bins.shape[1]
    cycle_size = lax.axis_size("az")
    cycle_pos = lax.axis_index("az")
    rng_size = lax.axis_size("rng")
    beam_count = BEAMS // cycle_size
    item_count = beam_count * chan_count
    dof = BINS * num_sel
    pairs = beam_count // 2
    if (
        columns == ARC
        and beam_count % 2 == 0
        and pairs * (COLS // BEAMS) == ARC // 2
        and rng_size == 8
        and cycle_size > 2
        and cells == 128
        and chan_count % 16 == 0
        and chan_count // 2 * dof % 128 == 0
        and 2 * dof + 8 <= 128
        and dof % 16 == 0
        and pairs * (chan_count // 2) <= 128
        and pairs > LATE
        and rng_size // 2 > 3
    ):
        return chain(
            echoes, arc_start, arc_offsets, doppler_bins, steer_angles, train_mask, pairs - LATE
        )
    table_re, table_im = doppler_table(num_pulses)
    table = jnp.concatenate(
        [jnp.concatenate([table_re, -table_im], 1), jnp.concatenate([table_im, table_re], 1)], 0
    )

    def own(x):
        return lax.dynamic_slice_in_dim(x, cycle_pos * beam_count, beam_count, axis=0)

    arc_first = (own(arc_start) - cycle_pos * columns + ARC // 2) % COLS
    col_index = arc_first[:, None] + own(arc_offsets)
    bins_own = own(doppler_bins)
    angles = own(steer_angles)
    block_count = train_mask.shape[1]
    cell_mask = (
        jnp.broadcast_to(train_mask[:, :, None], (beam_count, block_count, BLK))
        .reshape(beam_count, 1, block_count * BLK)
        .astype(jnp.bfloat16)
    )
    smem = pl.BlockSpec(memory_space=pltpu.SMEM)

    def snap_gram(extended, first, last, base):
        share = last - first
        ext_cols = extended.shape[1]
        return pl.pallas_call(
            snap_gram_kernel,
            grid=(share,),
            in_specs=[
                smem,
                smem,
                smem,
                smem,
                pl.BlockSpec((2, ext_cols, num_pulses, cells), lambda b: (0, 0, 0, 0)),
                pl.BlockSpec(table.shape, lambda b: (0, 0)),
                pl.BlockSpec((1, 1, cells), lambda b: (b, 0, 0)),
            ],
            out_specs=[
                pl.BlockSpec((1, 2, num_pulses, num_sel, cells), lambda b: (b, 0, 0, 0, 0)),
                pl.BlockSpec((1, dof, chan_count * dof), lambda b: (b, 0, 0)),
            ],
            out_shape=[
                jax.ShapeDtypeStruct((share, 2, num_pulses, num_sel, cells), jnp.bfloat16),
                jax.ShapeDtypeStruct((share, dof, chan_count * dof), jnp.float32),
            ],
            compiler_params=pltpu.CompilerParams(vmem_limit_bytes=VMEM_LIMIT),
            cost_estimate=pl.CostEstimate(
                flops=share * 600_000_000, bytes_accessed=share * 1_500_000, transcendentals=0
            ),
            name="snap_gram",
        )(
            col_index[first:last] - base,
            bins_own[first:last],
            jnp.cos(angles)[first:last],
            jnp.sin(angles)[first:last],
            extended,
            table,
            cell_mask[first:last],
        )

    width = ARC // 2
    forward = [(i, (i + 1) % cycle_size) for i in range(cycle_size)]
    backward = [(target, source) for source, target in forward]
    low = lax.ppermute(echoes[:, columns - width :], "az", forward)
    high = lax.ppermute(echoes[:, :width], "az", backward)
    step = COLS // BEAMS
    half = beam_count // 2
    if (half - 1) * step + step - 1 + ARC - 1 < width + columns and half * step >= width:
        v_lo, gram_lo = snap_gram(jnp.concatenate([low, echoes], 1), 0, half, 0)
        high, v_lo, gram_lo = lax.optimization_barrier((high, v_lo, gram_lo))
        v_hi, gram_hi = snap_gram(jnp.concatenate([echoes, high], 1), half, beam_count, width)
        v_parts = (v_lo, v_hi)
        grams = (gram_lo, gram_hi)
        if rng_size % 4 or item_count // rng_size < chan_count:
            grams = (jnp.concatenate(grams, 0),)
    else:
        v_one, gram_one = snap_gram(jnp.concatenate([low, echoes, high], 1), 0, beam_count, 0)
        v_parts = (v_one,)
        grams = (gram_one,)

    per = item_count // rng_size
    if per < chan_count:
        split = chan_count // per
        gram = grams[0].reshape(beam_count, dof, split, per * dof)
        grams = (jnp.swapaxes(gram, 1, 2).reshape(beam_count * split, dof, per * dof),)
        width = per
    else:
        width = chan_count
    vm = pltpu.VMEM
    dma = pltpu.SemaphoreType.DMA
    line = rng_size // 2
    chunk = (grams[0].shape[0] * len(grams) // rng_size, dof, grams[0].shape[2])
    part = pl.pallas_call(
        functools.partial(scatter_kernel, line, len(grams)),
        in_specs=[pl.BlockSpec(memory_space=vm)] * len(grams),
        out_specs=pl.BlockSpec(memory_space=vm),
        out_shape=jax.ShapeDtypeStruct(chunk, jnp.float32),
        scratch_shapes=[vm((line,) + chunk, jnp.float32)] * 4 + [dma((line,))] * 6,
        compiler_params=pltpu.CompilerParams(
            collective_id=0, has_side_effects=True, vmem_limit_bytes=VMEM_LIMIT
        ),
        name="scatter",
    )(*[g.reshape((rng_size // len(grams),) + chunk) for g in grams])
    solved = pl.pallas_call(
        solve_kernel,
        out_shape=jax.ShapeDtypeStruct((2 * dof + 8, per), jnp.float32),
        scratch_shapes=[
            vm((dof, per, dof), jnp.float32),
            vm((dof, dof, per), jnp.float32),
            vm((dof, dof, per), jnp.float32),
            vm((dof, dof, per), jnp.float32),
            vm((dof, per), jnp.float32),
            vm((dof, per), jnp.float32),
            vm((dof, per), jnp.float32),
            vm((dof, per), jnp.float32),
        ],
        compiler_params=pltpu.CompilerParams(vmem_limit_bytes=VMEM_LIMIT),
        name="solve",
    )(part)
    lanes = 128
    local_count = (BLK * jnp.sum(train_mask, axis=1)).astype(jnp.float32)
    pad_rows = -per % 8
    payload = jnp.concatenate(
        [
            jnp.pad(solved.T, ((0, pad_rows), (0, lanes - solved.shape[0]))),
            jnp.broadcast_to(local_count[:, None], (beam_count, lanes)),
        ],
        0,
    )
    halves = len(v_parts)
    any_spec = pl.BlockSpec(memory_space=pl.ANY)
    block = (chan_count, cells)
    out = pl.pallas_call(
        functools.partial(apply_kernel, halves, per, dof),
        in_specs=[pl.BlockSpec(memory_space=vm)] * 2 + [any_spec] * halves,
        out_specs=pl.BlockSpec(memory_space=vm),
        out_shape=jax.ShapeDtypeStruct((beam_count,) + block, jnp.float32),
        scratch_shapes=[
            vm((beam_count, 2, num_pulses, num_sel, cells), jnp.bfloat16),
            vm((rng_size,) + payload.shape, jnp.float32),
            vm((beam_count,) + block, jnp.float32),
            vm((2, 8, item_count), jnp.float32),
            vm((2, 8, item_count), jnp.float32),
            vm((beam_count,) + block, jnp.float32),
            vm(block, jnp.float32),
            vm(block, jnp.float32),
            dma((halves,)),
            dma((rng_size,)),
            dma((rng_size,)),
            dma((2,)),
            dma((2,)),
            dma((2,)),
            dma((2,)),
        ],
        compiler_params=pltpu.CompilerParams(
            collective_id=1, has_side_effects=True, vmem_limit_bytes=VMEM_LIMIT
        ),
        name="apply",
    )(payload, bins_own[:, :, None], *v_parts)
    return out


def solution(mesh):
    return jax.shard_map(
        body,
        mesh=mesh,
        in_specs=(P(None, "az", None, "rng"), P(), P(), P(), P(), P("az", "rng")),
        out_specs=P("az", None, "rng"),
        check_vma=False,
    )
```

```python
import functools

import jax
import numpy as np
import jax.numpy as jnp
from jax import lax
from jax.experimental import pallas as pl
from jax.experimental.pallas import tpu as pltpu
from jax.sharding import PartitionSpec as P


COLS = 256
ARC = 64
BINS = 3
BEAMS = 64
BLK = 128
LOADING = 0.1
VMEM_LIMIT = 48 << 20
CHAIN_VMEM = 66_200_000
CODE_TOP = 32000.0
LAG = 3
LATE = 4


def doppler_table(num_pulses):
    freq_ids = jnp.arange(num_pulses, dtype=jnp.int32)
    phase_steps = freq_ids[:, None] * freq_ids[None, :] % num_pulses
    phase_angle = -2.0 * jnp.pi / num_pulses * phase_steps.astype(jnp.float32)
    return (jnp.cos(phase_angle).astype(jnp.bfloat16), jnp.sin(phase_angle).astype(jnp.bfloat16))


def snap_gram_kernel(
    col_ref, bins_ref, cos_ref, sin_ref, ext_ref, table_ref, mask_ref, v_ref, gram_ref
):
    beam = pl.program_id(0)
    pulses = ext_ref.shape[2]
    num_sel = col_ref.shape[1]
    num_chan = bins_ref.shape[1]
    table = table_ref[...]
    parts_re, parts_im = [], []
    for j in range(num_sel):
        col = col_ref[beam, j]
        data = jnp.concatenate([ext_ref[0, col], ext_ref[1, col]], axis=0)
        spec = jnp.dot(table, data, preferred_element_type=jnp.float32)
        cosine = cos_ref[beam, j]
        sine = sin_ref[beam, j]
        spec_re = spec[:pulses]
        spec_im = spec[pulses:]
        parts_re.append(cosine * spec_re - sine * spec_im)
        parts_im.append(sine * spec_re + cosine * spec_im)
    for part, pieces in enumerate((parts_re, parts_im)):
        stacked = jnp.swapaxes(jnp.stack(pieces, 0), 0, 1)
        v_ref[0, part] = stacked.astype(jnp.bfloat16)
    dof = BINS * num_sel
    mask_row = mask_ref[0]
    row = lax.broadcasted_iota(jnp.int32, (dof, dof), 0)
    colm = lax.broadcasted_iota(jnp.int32, (dof, dof), 1)
    lower = row >= colm
    packed = []
    for k in range(num_chan):
        centre = bins_ref[beam, k]
        ids = [(centre + (q - BINS // 2 + pulses)) % pulses for q in range(BINS)]
        u_re = jnp.concatenate([v_ref[0, 0, f] for f in ids], 0)
        u_im = jnp.concatenate([v_ref[0, 1, f] for f in ids], 0)
        right = jnp.concatenate([u_re, u_im], 1)
        m_re = u_re * mask_row
        m_im = u_im * mask_row
        left = jnp.concatenate(
            [jnp.concatenate([m_re, m_im], 1), jnp.concatenate([m_im, -m_re], 1)], 0
        )
        both = lax.dot_general(
            left, right, (((1,), (1,)), ((), ())), preferred_element_type=jnp.float32
        )
        packed.append(jnp.where(lower, both[:dof], both[dof:]))
    gram_ref[0] = jnp.concatenate(packed, 1)


def solve_kernel(part_ref, out_ref, stack, turned, hr, hi, xr, xi, yr, yi):
    lead, dof, wide = part_ref.shape
    width = wide // dof
    lanes = lead * width
    nb = dof // 8
    group = min(8, lanes)
    for g in range(0, lanes, group):
        pieces = []
        for item in range(g, g + group):
            k = item % width
            pieces.append(part_ref[item // width, :, k * dof : (k + 1) * dof])
        stack[:, g : g + group, :] = jnp.swapaxes(jnp.stack(pieces, 0), 0, 1)
    for i in range(dof):
        turned[i] = stack[i].T
    trace = jnp.zeros((1, lanes), jnp.float32)
    for i in range(dof):
        trace = trace + turned[i, i : i + 1, :]
    load = (LOADING / dof) * trace
    cube = (8, 8, lanes)
    row = lax.broadcasted_iota(jnp.int32, cube, 0)
    col = lax.broadcasted_iota(jnp.int32, cube, 1)
    for ib in range(nb):
        rows = slice(8 * ib, 8 * ib + 8)
        for jb in range(ib, nb):
            cols = slice(8 * jb, 8 * jb + 8)
            imag = turned[rows, cols, :]
            real = jnp.swapaxes(turned[cols, rows, :], 0, 1)
            if ib == jb:
                straight, flip = imag, real
                real = jnp.where(row >= col, straight, flip)
                real = jnp.where(row == col, real + load[None], real)
                imag = jnp.where(row < col, straight, jnp.where(row > col, -flip, 0.0))
            hr[rows, cols, :] = real
            hi[rows, cols, :] = imag
    yr[...] = jnp.ones_like(yr)
    yi[...] = jnp.zeros_like(yi)
    xr[...] = jnp.zeros_like(xr)
    xi[...] = jnp.zeros_like(xi)
    sub = lax.broadcasted_iota(jnp.int32, (8, lanes), 0)

    for kb in range(nb):

        def step(k, carry, kb=kb):
            pivot = 1.0 / hr[k, pl.ds(k, 1), :]
            rr = [hr[k, 8 * b : 8 * b + 8, :] for b in range(kb, nb)]
            ri = [hi[k, 8 * b : 8 * b + 8, :] for b in range(kb, nb)]
            rs = [x + y for x, y in zip(rr, ri, strict=True)]
            gr = jnp.broadcast_to(yr[pl.ds(k, 1), :], (8, lanes))
            gi = jnp.broadcast_to(yi[pl.ds(k, 1), :], (8, lanes))
            for ib in range(kb, nb):
                fr = rr[ib - kb] * pivot
                fi = -ri[ib - kb] * pivot
                if ib == kb:
                    live = sub + 8 * kb > k
                    fr = jnp.where(live, fr, 0.0)
                    fi = jnp.where(live, fi, 0.0)
                fs = fr + fi
                fd = fi - fr
                own = slice(8 * ib, 8 * ib + 8)
                yr[own, :] = yr[own, :] - (fr * gr - fi * gi)
                yi[own, :] = yi[own, :] - (fr * gi + fi * gr)
                for s in range(8):
                    i = 8 * ib + s
                    cr = jnp.broadcast_to(fr[s : s + 1], (8, lanes))
                    cs = jnp.broadcast_to(fs[s : s + 1], (8, lanes))
                    cd = jnp.broadcast_to(fd[s : s + 1], (8, lanes))
                    for b in range(ib, nb):
                        pr, pi = rr[b - kb], ri[b - kb]
                        sl = slice(8 * b, 8 * b + 8)
                        both = cr * rs[b - kb]
                        hr[i, sl, :] = (hr[i, sl, :] - both) + cs * pi
                        hi[i, sl, :] = (hi[i, sl, :] - both) - cd * pr
            return carry

        lax.fori_loop(8 * kb, 8 * kb + 8, step, 0)

    for ib in reversed(range(nb)):

        def back(t, carry, ib=ib):
            i = 8 * ib + 7 - t
            sr = jnp.zeros((8, lanes), jnp.float32)
            si = jnp.zeros((8, lanes), jnp.float32)
            for b in range(ib, nb):
                sl = slice(8 * b, 8 * b + 8)
                ar, ai = hr[i, sl, :], hi[i, sl, :]
                br, bi = xr[sl, :], xi[sl, :]
                sr = sr + (ar * br - ai * bi)
                si = si + (ar * bi + ai * br)
            pivot = 1.0 / hr[i, pl.ds(i, 1), :]
            top_r = yr[pl.ds(i, 1), :]
            top_i = yi[pl.ds(i, 1), :]
            xr[pl.ds(i, 1), :] = (top_r - jnp.sum(sr, 0, keepdims=True)) * pivot
            xi[pl.ds(i, 1), :] = (top_i - jnp.sum(si, 0, keepdims=True)) * pivot
            return carry

        lax.fori_loop(0, 8, back, 0)
    out_ref[:dof, :lanes] = xr[...]
    out_ref[dof : 2 * dof, :lanes] = xi[...]
    out_ref[2 * dof : 2 * dof + 8, :lanes] = jnp.broadcast_to(
        jnp.sum(xr[...], 0, keepdims=True), (8, lanes)
    )


MESH = pl.DeviceIdType.MESH


def scatter_kernel(n, halves, *refs):
    g_refs = refs[:halves]
    out_ref, pair, acc, right, left, psend, precv, rsend, rrecv, lsend, lrecv = refs[halves:]
    share = n // halves

    def own(t, core):
        return g_refs[t // share].at[2 * (t % share) + core]

    me = lax.axis_index("rng")
    z = me // 2
    c = me % 2
    mate = 2 * z + 1 - c
    ahead = lax.rem(me + 2, 2 * n)
    behind = lax.rem(me + 2 * n - 2, 2 * n)
    barrier = pltpu.get_barrier_semaphore()
    pl.semaphore_signal(barrier, inc=1, device_id={"rng": mate}, device_id_type=MESH)
    pl.semaphore_signal(barrier, inc=1, device_id={"rng": ahead}, device_id_type=MESH)
    pl.semaphore_signal(barrier, inc=1, device_id={"rng": behind}, device_id_type=MESH)
    pl.semaphore_wait(barrier, 3)

    order = []
    for t in range((n + 1) // 2):
        order.append(n - 1 - t)
        if t != n - 1 - t:
            order.append(t)

    def pair_copy(t):
        return pltpu.make_async_remote_copy(
            src_ref=own(t, 1 - c),
            dst_ref=pair.at[t],
            send_sem=psend.at[t],
            recv_sem=precv.at[t],
            device_id={"rng": mate},
            device_id_type=MESH,
        )

    def right_copy(t):
        return pltpu.make_async_remote_copy(
            src_ref=acc.at[t],
            dst_ref=right.at[t],
            send_sem=rsend.at[t],
            recv_sem=rrecv.at[t],
            device_id={"rng": ahead},
            device_id_type=MESH,
        )

    def left_copy(t):
        return pltpu.make_async_remote_copy(
            src_ref=acc.at[t],
            dst_ref=left.at[t],
            send_sem=lsend.at[t],
            recv_sem=lrecv.at[t],
            device_id={"rng": behind},
            device_id_type=MESH,
        )

    for t in order:
        pair_copy(t).start()
    for t in order:
        pair_copy(t).wait_recv()
        acc[t] = own(t, c)[...] + pair[t]

        @pl.when(jnp.logical_and(z == 0, t > 0))
        def _(t=t):
            right_copy(t).start()

        @pl.when(jnp.logical_and(z == n - 1, t < n - 1))
        def _(t=t):
            left_copy(t).start()

    for place in range(n):
        events = [(place + n - 1 - t, 0, t) for t in range(place + 1, n) if place > 0]
        events += [(n - 1 - place + t, 1, t) for t in range(place) if place < n - 1]

        @pl.when(z == place)
        def _(place=place, events=sorted(events)):
            for _, side, t in events:
                copy = left_copy(t) if side else right_copy(t)
                source = left if side else right
                copy.wait_recv()
                acc[t] = acc[t] + source[t]
                copy.start()
            total = acc[place]
            if place > 0:
                right_copy(place).wait_recv()
                total = total + right[place]
            if place < n - 1:
                left_copy(place).wait_recv()
                total = total + left[place]
            out_ref[...] = total

    for t in range(n):
        pair_copy(t).wait_send()

        @pl.when(z < t)
        def _(t=t):
            right_copy(t).wait_send()

        @pl.when(z > t)
        def _(t=t):
            left_copy(t).wait_send()


def apply_kernel(
    halves,
    per,
    dof,
    pay_ref,
    bins_ref,
    *refs,
):
    v_refs = refs[:halves]
    (out_ref, v_all, gat, power, edge, halo, sums, az_lo, az_hi) = refs[halves : halves + 9]
    (vsem, gsend, grecv, esend, erecv, asend, arecv) = refs[halves + 9 :]
    me = lax.axis_index("rng")
    az = lax.axis_index("az")
    n = lax.axis_size("rng")
    m = lax.axis_size("az")
    beams, num_chan, cells = out_ref.shape
    pulses, num_sel = v_all.shape[2], v_all.shape[3]
    taps = pulses * num_sel
    az_next = lax.rem(az + 1, m)
    az_prev = lax.rem(az + m - 1, m)
    barrier = pltpu.get_barrier_semaphore()
    for d in range(1, n):
        peer = lax.rem(me + d, n)
        pl.semaphore_signal(barrier, inc=1, device_id={"rng": peer}, device_id_type=MESH)
    for other in (az_next, az_prev):
        pl.semaphore_signal(barrier, inc=1, device_id={"az": other}, device_id_type=MESH)
    share = beams // halves
    loads = []
    for h in range(halves):
        load = pltpu.make_async_copy(v_refs[h], v_all.at[pl.ds(h * share, share)], vsem.at[h])
        load.start()
        loads.append(load)
    pl.semaphore_wait(barrier, n + 1)

    copies = []
    for d in range(1, n):
        peer = lax.rem(me + d, n)
        copy = pltpu.make_async_remote_copy(
            src_ref=pay_ref,
            dst_ref=gat.at[me],
            send_sem=gsend.at[d],
            recv_sem=grecv.at[d],
            device_id={"rng": peer},
            device_id_type=MESH,
        )
        copy.start()
        copies.append(copy)
    gat[me] = pay_ref[...]
    for load in loads:
        load.wait()
    for copy in copies:
        copy.wait_recv()
    rows = gat.shape[1] - beams
    count = jnp.zeros((beams, gat.shape[2]), jnp.float32)
    for r in range(n):
        count = count + gat[r, rows:, :]
    sums[0] = jnp.zeros(sums.shape[1:], jnp.float32)
    for b in range(beams):
        sums[b, :1, :] = count[b : b + 1]
    freq = lax.broadcasted_iota(jnp.int32, (num_chan, taps), 1) // num_sel
    lanes = gat.shape[2]
    lane = lax.broadcasted_iota(jnp.int32, (num_chan, lanes), 1)

    def one(b, carry):
        if per >= num_chan:
            ratio = per // num_chan
            start = pl.multiple_of((b % ratio) * num_chan, 8)
            w = gat[b // ratio, pl.ds(start, num_chan), :]
        else:
            split = num_chan // per
            w = jnp.concatenate([gat[b * split + t, :per, :] for t in range(split)], 0)
        w = w * sums[b, :1, :]
        quiet = w[:, 2 * dof : 2 * dof + 1]
        centre = bins_ref[b]
        planes = []
        hits = []
        for q in range(BINS):
            f = lax.rem(centre + (q - BINS // 2 + pulses), pulses)
            hits.append(freq == f)
        for part in range(2):
            plane = jnp.zeros((num_chan, taps), jnp.float32)
            for q in range(BINS):
                start = part * dof + q * num_sel
                piece = pltpu.roll(w, (lanes - start) % lanes, 1) if start else w
                piece = jnp.where(lane < num_sel, piece, 0.0)
                span = num_sel
                while span < lanes:
                    piece = piece + pltpu.roll(piece, span, 1)
                    span *= 2
                tiled = jnp.concatenate([piece] * (taps // lanes), 1)
                plane = jnp.where(hits[q], tiled, plane)
            planes.append(plane)
        top = jnp.concatenate([planes[0], planes[1]], 1)
        low = jnp.concatenate([-planes[1], planes[0]], 1)
        lhs = jnp.concatenate([top, low], 0).astype(jnp.bfloat16)
        flat = v_all[b].reshape(2 * taps, cells)
        proj = jnp.dot(lhs, flat, preferred_element_type=jnp.float32)
        p0 = proj[:num_chan]
        p1 = proj[num_chan:]
        power[b] = (p0 * p0 + p1 * p1) / quiet
        return carry

    lax.fori_loop(0, beams, one, 0)
    items = beams * num_chan
    turned = power[...].reshape(items, cells).T
    edge[0] = turned[:8]
    edge[1] = turned[cells - 8 :]

    def edge_copy(side):
        target = lax.rem(me + 1, n) if side else lax.rem(me + n - 1, n)
        return pltpu.make_async_remote_copy(
            src_ref=edge.at[side],
            dst_ref=halo.at[side],
            send_sem=esend.at[side],
            recv_sem=erecv.at[side],
            device_id={"rng": target},
            device_id_type=MESH,
        )

    for side in range(2):
        edge_copy(side).start()
    for side in range(2):
        edge_copy(side).wait()
    before = jnp.where(me > 0, halo[1, 7:8], 0.0)
    after = jnp.where(me < n - 1, halo[0, 0:1], 0.0)
    turned = (
        jnp.concatenate([before, turned[:-1]], 0)
        + turned
        + jnp.concatenate([turned[1:], after], 0)
    )
    sums[...] = turned.T.reshape(beams, num_chan, cells)
    up = pltpu.make_async_remote_copy(
        src_ref=sums.at[beams - 1],
        dst_ref=az_lo,
        send_sem=asend.at[0],
        recv_sem=arecv.at[0],
        device_id={"az": az_next},
        device_id_type=MESH,
    )
    down = pltpu.make_async_remote_copy(
        src_ref=sums.at[0],
        dst_ref=az_hi,
        send_sem=asend.at[1],
        recv_sem=arecv.at[1],
        device_id={"az": az_prev},
        device_id_type=MESH,
    )
    up.start()
    down.start()
    for b in range(1, beams - 1):
        out_ref[b] = (sums[b - 1] + sums[b] + sums[b + 1]) / 9.0
    up.wait_recv()
    down.wait_recv()
    out_ref[0] = (az_lo[...] + sums[0] + sums[1]) / 9.0
    out_ref[beams - 1] = (sums[beams - 2] + sums[beams - 1] + az_hi[...]) / 9.0
    up.wait_send()
    down.wait_send()
    for copy in copies:
        copy.wait_send()


def gram_of(v_ref, beam, bins, mask_row):
    pulses = v_ref.shape[2]
    num_sel = v_ref.shape[3]
    dof = BINS * num_sel
    row = lax.broadcasted_iota(jnp.int32, (dof, dof), 0)
    colm = lax.broadcasted_iota(jnp.int32, (dof, dof), 1)
    lower = row >= colm
    packed = []
    for centre in bins:
        ids = [lax.rem(centre + (q - BINS // 2 + pulses), pulses) for q in range(BINS)]
        u_re = jnp.concatenate([v_ref[beam, 0, f] for f in ids], 0)
        u_im = jnp.concatenate([v_ref[beam, 1, f] for f in ids], 0)
        right = jnp.concatenate([u_re, u_im], 1)
        m_re = u_re * mask_row
        m_im = u_im * mask_row
        left = jnp.concatenate(
            [jnp.concatenate([m_re, m_im], 1), jnp.concatenate([m_im, -m_re], 1)], 0
        )
        both = lax.dot_general(
            left, right, (((1,), (1,)), ((), ())), preferred_element_type=jnp.float32
        )
        packed.append(jnp.where(lower, both[:dof], both[dof:]))
    return packed


def chain_kernel(
    early,
    start_hbm,
    offs_hbm,
    bins_hbm,
    train_hbm,
    angle_hbm,
    echoes,
    table_hbm,
    spread_hbm,
    out_hbm,
    start_ref,
    offs_ref,
    bins_ref,
    train_ref,
    angle_ref,
    chan_ref,
    table_ref,
    spread_ref,
    turn,
    ext,
    halo,
    v_all,
    gram,
    pair,
    coded,
    scale,
    code_in,
    scale_in,
    part,
    solved,
    stack,
    turned,
    hr,
    hi,
    xr,
    xi,
    yr,
    yi,
    masks,
    totals,
    counts,
    pay,
    gat_e,
    gat_l,
    tiles_e,
    tiles_l,
    pw,
    pl_left,
    pl_right,
    rows,
    out_ref,
    esem,
    osem,
    hsend,
    hrecv,
    psend,
    precv,
    dsend,
    drecv,
    msend,
    mrecv,
    gsend,
    grecv,
    hello,
    lsend,
    lrecv,
    tsend,
    trecv,
    arecv,
):
    me = lax.axis_index("rng")
    az = lax.axis_index("az")
    size = lax.axis_size("rng")
    m = lax.axis_size("az")
    n = size // 2
    z = me // 2
    c = lax.rem(me, 2)
    beams, num_chan, cells = out_hbm.shape
    columns = echoes.shape[1]
    pulses = echoes.shape[2]
    num_sel = offs_ref.shape[0]
    blocks = train_ref.shape[0]
    dof = BINS * num_sel
    taps = pulses * num_sel
    steps = beams // 2
    width = ARC // 2
    w = width // steps
    side_chan = num_chan // 2
    half = side_chan * dof
    lanes = pay.shape[1]
    az_next = lax.rem(az + 1, m)
    az_prev = lax.rem(az + m - 1, m)
    ahead = lax.rem(me + 1, size)
    behind = lax.rem(me + size - 1, size)
    mate = 2 * z + 1 - c
    mid_l = n // 2 - 1
    mid_r = n // 2
    late = steps - early
    middles = ((0, mid_l), (1, mid_r))
    ends = ((0, 0), (1, n - 1))
    is_mid = jnp.logical_or(z == mid_l, z == mid_r)

    loads = [
        pltpu.make_async_copy(src, dst, esem.at[i])
        for i, (src, dst) in enumerate(
            (
                (start_hbm, start_ref),
                (offs_hbm, offs_ref),
                (bins_hbm, bins_ref),
                (train_hbm, train_ref),
                (angle_hbm, angle_ref),
                (bins_hbm, chan_ref),
                (table_hbm, table_ref),
                (spread_hbm, spread_ref),
                (echoes, ext.at[:, width : width + columns]),
            )
        )
    ]
    barrier = pltpu.get_barrier_semaphore()
    for other in (az_next, az_prev):
        pl.semaphore_signal(barrier, inc=1, device_id={"az": other}, device_id_type=MESH)
    pl.semaphore_signal(barrier, inc=1, device_id={"rng": mate}, device_id_type=MESH)
    for place in range(n):
        near = jnp.logical_or(is_mid, place in (mid_l, mid_r))

        @pl.when(jnp.logical_and(z != place, near))
        def _(place=place):
            pl.semaphore_signal(
                barrier, inc=1, device_id={"rng": 2 * place + c}, device_id_type=MESH
            )

    for load in loads:
        load.start()
    pl_left[...] = jnp.zeros(pl_left.shape, jnp.float32)
    pl_right[...] = jnp.zeros(pl_right.shape, jnp.float32)
    solved[...] = jnp.zeros(solved.shape, jnp.float32)
    part[...] = jnp.zeros(part.shape, jnp.float32)
    pl.semaphore_wait(barrier, 3 + jnp.where(is_mid, n - 1, 2))

    def all_of(ref, sem):
        pltpu.make_async_copy(ref, ref, sem).wait()

    def low_copy(i):
        return pltpu.make_async_remote_copy(
            src_ref=echoes.at[:, pl.ds(columns - w * (i + 1), w)],
            dst_ref=halo.at[i, 0],
            send_sem=hsend,
            recv_sem=hrecv.at[i],
            device_id={"az": az_next},
            device_id_type=MESH,
        )

    def high_copy(i):
        return pltpu.make_async_remote_copy(
            src_ref=echoes.at[:, pl.ds(w * i, w)],
            dst_ref=halo.at[i, 1],
            send_sem=hsend,
            recv_sem=hrecv.at[i],
            device_id={"az": az_prev},
            device_id_type=MESH,
        )

    for i in range(steps):
        low_copy(i).start()
        high_copy(i).start()
    for side, middle in middles:

        @pl.when(z == middle)
        def _(side=side):
            end = 2 * (n - 1 if side else 0) + c
            pl.semaphore_signal(hello, inc=1, device_id={"rng": end}, device_id_type=MESH)

    for load in loads:
        load.wait()

    cell = lax.broadcasted_iota(jnp.int32, (1, cells), 1) // BLK
    for b in range(beams):
        row = jnp.zeros((1, cells), jnp.float32)
        for blk in range(blocks):
            row = jnp.where(cell == blk, train_ref[blk, b].astype(jnp.float32), row)
        masks[0, b : b + 1, :] = row

    mask_copy = pltpu.make_async_remote_copy(
        src_ref=masks.at[0],
        dst_ref=masks.at[1],
        send_sem=msend,
        recv_sem=mrecv,
        device_id={"rng": mate},
        device_id_type=MESH,
    )
    mask_copy.start()
    turn[0] = jnp.cos(angle_ref[...])
    turn[1] = jnp.sin(angle_ref[...])
    mask_copy.wait_recv()
    totals[...] = jnp.broadcast_to(
        jnp.sum(masks[0] + masks[1], 1, keepdims=True), totals.shape
    )

    def mine(t):
        return jnp.where(c == 0, steps - 1 - t, steps + t)

    def theirs(t):
        return jnp.where(c == 0, steps + t, steps - 1 - t)

    def owner_of(side, t):
        return jnp.where(t < early, side * (n - 1), mid_l + side)

    def row_of(t):
        return jnp.where(t < early, t, t - early)

    def pair_copy(t):
        return pltpu.make_async_remote_copy(
            src_ref=gram.at[theirs(t)],
            dst_ref=pair.at[t],
            send_sem=psend,
            recv_sem=precv.at[t],
            device_id={"rng": mate},
            device_id_type=MESH,
        )

    def code_copies(side, t, source):
        owner = 2 * owner_of(side, t) + c
        return [
            pltpu.make_async_remote_copy(
                src_ref=src.at[2 * t + side],
                dst_ref=dst.at[row_of(t), source],
                send_sem=dsend.at[i],
                recv_sem=drecv.at[i, row_of(t)],
                device_id={"rng": owner},
                device_id_type=MESH,
            )
            for i, (src, dst) in enumerate(((coded, code_in), (scale, scale_in)))
        ]

    table = table_ref[...]
    blane = lax.broadcasted_iota(jnp.int32, angle_ref.shape, 1)

    def one_beam(b):
        bg = az * beams + b
        first = lax.rem(start_ref[bg] - az * columns + (width + COLS), COLS)
        first = jnp.minimum(first, ext.shape[1] - ARC)
        here = blane == bg
        cosine = jnp.sum(jnp.where(here, turn[0], 0.0), 1, keepdims=True)
        sine = jnp.sum(jnp.where(here, turn[1], 0.0), 1, keepdims=True)
        cosine = jnp.broadcast_to(cosine, (num_sel, cells))[None]
        sine = jnp.broadcast_to(sine, (num_sel, cells))[None]
        parts_re, parts_im = [], []
        for j in range(num_sel):
            col = first + offs_ref[j, bg]
            data = jnp.concatenate([ext[0, col], ext[1, col]], axis=0)
            spec = jnp.dot(table, data, preferred_element_type=jnp.float32)
            parts_re.append(spec[:pulses])
            parts_im.append(spec[pulses:])
        spec_re = jnp.swapaxes(jnp.stack(parts_re, 0), 0, 1)
        spec_im = jnp.swapaxes(jnp.stack(parts_im, 0), 0, 1)
        v_all[b, 0] = (cosine * spec_re - sine * spec_im).astype(jnp.bfloat16)
        v_all[b, 1] = (sine * spec_re + cosine * spec_im).astype(jnp.bfloat16)
        mask_row = masks[0, pl.ds(b, 1), :].astype(jnp.bfloat16)
        bins = [bins_ref[k, bg] for k in range(num_chan)]
        packed = gram_of(v_all, b, bins, mask_row)
        gram[b, 0] = jnp.concatenate(packed[:side_chan], 1)
        gram[b, 1] = jnp.concatenate(packed[side_chan:], 1)

    def slot(s, carry):
        @pl.when(s < steps)
        def _():
            all_of(halo.at[s], hrecv.at[s])
            ext[:, pl.ds(width - w * (s + 1), w)] = halo[s, 0]
            ext[:, pl.ds(width + columns + w * s, w)] = halo[s, 1]
            one_beam(theirs(s))
            pair_copy(s).start()

        t = s - 1

        @pl.when(jnp.logical_and(t >= 0, t < steps))
        def _():
            pair_copy(t).wait_recv()
            own = mine(t)
            number = totals[pl.ds(own, 1), :]
            row = row_of(t)
            for side in range(2):
                total = gram[own, side] + pair[t, side]
                owner = owner_of(side, t)

                @pl.when(z == owner)
                def _(total=total):
                    part[row] = total
                    counts[row] = number

                @pl.when(z != owner)
                def _(side=side, total=total):
                    top = jnp.max(jnp.abs(total), 0, keepdims=True)
                    top = jnp.maximum(top, 1e-30)
                    code = jnp.round(total * (CODE_TOP / top))
                    coded[2 * t + side] = code.astype(jnp.int32).astype(jnp.int16)
                    scale[2 * t + side, :, :half] = top * (1.0 / CODE_TOP)
                    scale[2 * t + side, :, half:] = number

            far = jnp.where(z < n // 2, 1, 0)
            for side in (far, 1 - far):

                @pl.when(z != owner_of(side, t))
                def _(side=side):
                    for copy in code_copies(side, t, z):
                        copy.start()

        tt = s - LAG

        @pl.when(jnp.logical_and(tt >= 0, tt < steps))
        def _():
            row = row_of(tt)
            for side in range(2):
                for owner, is_early in ((ends[side][1], True), (middles[side][1], False)):
                    right_time = tt < early if is_early else tt >= early

                    @pl.when(jnp.logical_and(z == owner, right_time))
                    def _(side=side, owner=owner):
                        total = part[row]
                        number = counts[row]
                        all_of(code_in.at[row, pl.ds(0, n - 1)], drecv.at[0, row])
                        all_of(scale_in.at[row, pl.ds(0, n - 1)], drecv.at[1, row])
                        for source in range(n):
                            if source != owner:
                                code = code_in[row, source].astype(jnp.int32)
                                code = code.astype(jnp.float32)
                                total = total + code * scale_in[row, source, :, :half]
                                number = number + scale_in[row, source, :, half:]
                        part[row] = total
                        counts[row] = number

        @pl.when(s < steps)
        def _():
            one_beam(mine(s))

        return carry

    @pl.when(jnp.logical_not(is_mid))
    def _():
        pl.semaphore_wait(hello, 1)

    lax.fori_loop(0, steps + LAG, slot, 0)

    items = pay.shape[0]

    def send_copy(d, side, buf, which):
        return pltpu.make_async_remote_copy(
            src_ref=pay.at[: buf.shape[1]],
            dst_ref=buf.at[2 * side + c],
            send_sem=gsend.at[min((d - 1) // 4 + (d - 1) // 6, 2)],
            recv_sem=grecv.at[which],
            device_id={"rng": lax.rem(me + d, size)},
            device_id_type=MESH,
        )

    solve_kernel(part, solved, stack, turned, hr, hi, xr, xi, yr, yi)
    flipped = solved[...].T
    scaled = []
    for t in range(items // side_chan):
        scaled.append(flipped[side_chan * t : side_chan * (t + 1)] * counts[t])
    full = jnp.concatenate(scaled, 0)
    lane = lax.broadcasted_iota(jnp.int32, (items, lanes), 1)
    hi_part = full.astype(jnp.bfloat16).astype(jnp.float32)
    rest = full - hi_part
    mid_part = rest.astype(jnp.bfloat16).astype(jnp.float32)
    lo_part = rest - mid_part
    split = jnp.where(
        lane == 2 * dof + 1, mid_part, jnp.where(lane == 2 * dof + 2, lo_part, hi_part)
    )
    pay[...] = split.astype(jnp.bfloat16)
    for which, (places, buf) in enumerate(((ends, gat_e), (middles, gat_l))):
        for side, owner in places:

            @pl.when(z == owner)
            def _(side=side, buf=buf, which=which):
                for d in range(1, size):
                    send_copy(d, side, buf, which).start()
                buf[2 * side + c] = pay[: buf.shape[1]]

    freq = (lax.broadcasted_iota(jnp.int32, (num_chan, taps), 1) // num_sel).astype(jnp.float32)
    centres = chan_ref[...].astype(jnp.float32)

    def tile_copy(side, b, group):
        target = ahead if side else behind
        buf = pl_left if side else pl_right
        return pltpu.make_async_remote_copy(
            src_ref=pw.at[b + 1],
            dst_ref=buf.at[b + 1],
            send_sem=lsend.at[side],
            recv_sem=lrecv.at[side, group],
            device_id={"rng": target},
            device_id_type=MESH,
        )

    def az_copy(up):
        return pltpu.make_async_remote_copy(
            src_ref=pw.at[beams if up else 1],
            dst_ref=pw.at[0 if up else beams + 1],
            send_sem=tsend,
            recv_sem=trecv,
            device_id={"az": az_next if up else az_prev},
            device_id_type=MESH,
        )

    def corner_copy(up, side):
        buf = pl_left if side else pl_right
        return pltpu.make_async_remote_copy(
            src_ref=pw.at[beams if up else 1],
            dst_ref=buf.at[0 if up else beams + 1],
            send_sem=lsend.at[side],
            recv_sem=arecv.at[side],
            device_id={
                "az": az_next if up else az_prev,
                "rng": ahead if side else behind,
            },
            device_id_type=MESH,
        )

    def one_power(b, tiles, t, core, group):
        start = pl.multiple_of(t * side_chan, side_chan)
        both = [tiles[2 * side + core, pl.ds(start, side_chan), :] for side in range(2)]
        wide = jnp.concatenate(both, 0)
        tail = wide[:, 2 * BINS * lanes :]
        quiet = tail[:, :1] + tail[:, 1:2] + tail[:, 2:3]
        centre = jnp.sum(jnp.where(blane == az * beams + b, centres, 0.0), 1, keepdims=True)
        hits = []
        for q in range(BINS):
            f = centre + (q - BINS // 2)
            f = jnp.where(f < 0.0, f + pulses, jnp.where(f >= pulses, f - pulses, f))
            hits.append(freq == f)
        planes = []
        for p in range(2):
            plane = jnp.zeros((num_chan, taps), jnp.float32)
            for q in range(BINS):
                at = (p * BINS + q) * lanes
                piece = wide[:, at : at + lanes]
                tiled = jnp.concatenate([piece] * (taps // lanes), 1)
                plane = jnp.where(hits[q], tiled, plane)
            planes.append(plane)
        top = jnp.concatenate([planes[0], planes[1]], 1)
        bottom = jnp.concatenate([-planes[1], planes[0]], 1)
        lhs = jnp.concatenate([top, bottom], 0).astype(jnp.bfloat16)
        flat = v_all[b].reshape(2 * taps, cells)
        proj = jnp.dot(lhs, flat, preferred_element_type=jnp.float32)
        p0 = proj[:num_chan]
        p1 = proj[num_chan:]
        pw[b + 1] = (p0 * p0 + p1 * p1) / quiet

        @pl.when(me < size - 1)
        def _():
            tile_copy(1, b, group).start()

        @pl.when(me > 0)
        def _():
            tile_copy(0, b, group).start()

    def spread_weights(which, buf, tiles):
        mine_too = is_mid if which else jnp.logical_not(is_mid)
        others = 2 * len(middles)
        for own in range(2):

            @pl.when(mine_too if own else jnp.logical_not(mine_too))
            def _(own=own):
                all_of(buf.at[pl.ds(0, others - own)], grecv.at[which])

        flat = buf[...].reshape(others * buf.shape[1], lanes)
        wide = jnp.dot(flat, spread_ref[...], preferred_element_type=jnp.float32)
        tiles[...] = wide.reshape(tiles.shape)

    def early_power(t, carry):
        one_power(steps - 1 - t, tiles_e, t, 0, 0)
        one_power(steps + t, tiles_e, t, 1, 0)
        return carry

    def late_power(i, carry):
        one_power(i, tiles_l, late - 1 - i, 0, 1)
        one_power(beams - 1 - i, tiles_l, late - 1 - i, 1, 1)

        @pl.when(i == 0)
        def _():
            for up in range(2):
                az_copy(up).start()

                @pl.when(me < size - 1)
                def _(up=up):
                    corner_copy(up, 1).start()

                @pl.when(me > 0)
                def _(up=up):
                    corner_copy(up, 0).start()

        return carry

    spread_weights(0, gat_e, tiles_e)
    lax.fori_loop(0, early, early_power, 0)
    spread_weights(1, gat_l, tiles_l)
    lax.fori_loop(0, late, late_power, 0)

    lane = lax.broadcasted_iota(jnp.int32, (num_chan, cells), 1)

    def row_sum(i):
        mid = pw[i]
        back = pltpu.roll(jnp.where(lane == cells - 1, pl_left[i], mid), 1, 1)
        fore = pltpu.roll(jnp.where(lane == 0, pl_right[i], mid), cells - 1, 1)
        return back + mid + fore

    def finish(which, group):
        @pl.when(me > 0)
        def _():
            all_of(pl_left.at[pl.ds(0, len(group))], lrecv.at[1, which])

        @pl.when(me < size - 1)
        def _():
            all_of(pl_right.at[pl.ds(0, len(group))], lrecv.at[0, which])

        for b in group:
            rows[b + 1] = row_sum(b + 1)

    def smooth(b):
        out_ref[b] = (rows[b] + rows[b + 1] + rows[b + 2]) / 9.0

    def write(first, count):
        part_of = pl.ds(first, count)
        copy = pltpu.make_async_copy(
            out_ref.at[part_of], out_hbm.at[part_of], osem
        )
        copy.start()

    finish(0, range(late, beams - late))
    for b in range(late + 1, beams - late - 1):
        smooth(b)
    write(late + 1, beams - 2 * late - 2)
    outer = [*range(late), *range(beams - late, beams)]
    finish(1, outer)
    for b in range(1, late + 1):
        smooth(b)
        smooth(beams - 1 - b)
    write(1, late)
    write(beams - 1 - late, late)
    all_of(pw.at[pl.ds(0, 2)], trecv)

    @pl.when(me > 0)
    def _():
        all_of(pl_left.at[pl.ds(0, 2)], arecv.at[1])

    @pl.when(me < size - 1)
    def _():
        all_of(pl_right.at[pl.ds(0, 2)], arecv.at[0])

    rows[0] = row_sum(0)
    rows[beams + 1] = row_sum(beams + 1)
    smooth(0)
    smooth(beams - 1)
    write(0, 1)
    write(beams - 1, 1)

    all_of(echoes, hsend)
    all_of(pair, psend)
    mask_copy.wait_send()
    for own, buf, here in (
        (early, gat_e, jnp.logical_not(is_mid)),
        (late, gat_l, is_mid),
    ):

        @pl.when(here)
        def _(own=own, buf=buf):
            for i, ref in enumerate((coded, scale)):
                all_of(ref.at[pl.ds(0, 2 * steps - own)], dsend.at[i])
            all_of(buf, gsend.at[0])
            all_of(buf.at[pl.ds(0, 2)], gsend.at[1])
            all_of(buf.at[0], gsend.at[2])

    all_of(pw.at[pl.ds(0, 2)], tsend)
    for side in range(2):

        @pl.when(me < size - 1 if side else me > 0)
        def _(side=side):
            all_of(pw, lsend.at[side])

    pltpu.make_async_copy(out_ref, out_hbm, osem).wait()


def chain(echoes, arc_start, arc_offsets, doppler_bins, steer_angles, train_mask, early):
    columns, num_pulses, cells = echoes.shape[1:]
    num_sel = arc_offsets.shape[1]
    num_chan = doppler_bins.shape[1]
    size = lax.axis_size("rng")
    beams = BEAMS // lax.axis_size("az")
    dof = BINS * num_sel
    steps = beams // 2
    n = size // 2
    width = ARC // 2
    w = width // steps
    side_chan = num_chan // 2
    half = side_chan * dof
    late = steps - early
    most = max(early, late)
    items = most * side_chan
    lanes = 128
    with jax.ensure_compile_time_eval():
        table_re, table_im = doppler_table(num_pulses)
        table = np.block([[table_re, -table_im], [table_im, table_re]])
    source = np.arange(lanes)[:, None]
    target = np.arange((2 * BINS + 1) * lanes)[None, :]
    block, place = target // lanes, target % lanes
    wanted = np.where(
        block < 2 * BINS, block * num_sel + place % num_sel, 2 * dof + np.minimum(place, 3)
    )
    spread = jnp.asarray(source == wanted, jnp.bfloat16)
    vm = pltpu.VMEM
    sm = pltpu.SMEM
    dma = pltpu.SemaphoreType.DMA
    f32 = jnp.float32
    bf16 = jnp.bfloat16
    i32 = jnp.int32
    i16 = jnp.int16
    tile = (num_chan, cells)
    scratch = [
        sm(arc_start.shape, i32),
        sm(arc_offsets.T.shape, i32),
        sm(doppler_bins.T.shape, i32),
        sm(train_mask.T.shape, i32),
        vm(steer_angles.T.shape, f32),
        vm(doppler_bins.T.shape, i32),
        vm(table.shape, bf16),
        vm(spread.shape, bf16),
        vm((2,) + steer_angles.T.shape, f32),
        vm((2, columns + 2 * width, num_pulses, cells), bf16),
        vm((steps, 2, 2, w, num_pulses, cells), bf16),
        vm((beams, 2, num_pulses, num_sel, cells), bf16),
        vm((beams, 2, dof, half), f32),
        vm((steps, 2, dof, half), f32),
        vm((2 * steps, dof, half), i16),
        vm((2 * steps, 1, half + lanes), f32),
        vm((most, n, dof, half), i16),
        vm((most, n, 1, half + lanes), f32),
        vm((most, dof, half), f32),
        vm((lanes, lanes), f32),
        vm((dof, items, dof), f32),
        vm((dof, dof, items), f32),
        vm((dof, dof, items), f32),
        vm((dof, dof, items), f32),
        vm((dof, items), f32),
        vm((dof, items), f32),
        vm((dof, items), f32),
        vm((dof, items), f32),
        vm((2, beams, cells), f32),
        vm((beams, lanes), f32),
        vm((most, 1, lanes), f32),
        vm((items, lanes), bf16),
        vm((4, early * side_chan, lanes), bf16),
        vm((4, late * side_chan, lanes), bf16),
        vm((4, early * side_chan, spread.shape[1]), f32),
        vm((4, late * side_chan, spread.shape[1]), f32),
        vm((beams + 2,) + tile, f32),
        vm((beams + 2,) + tile, f32),
        vm((beams + 2,) + tile, f32),
        vm((beams + 2,) + tile, f32),
        vm((beams,) + tile, f32),
        dma((9,)),
        dma,
        dma,
        dma((steps,)),
        dma,
        dma((steps,)),
        dma((2,)),
        dma((2, most)),
        dma,
        dma,
        dma((3,)),
        dma((2,)),
        pltpu.SemaphoreType.REGULAR,
        dma((2,)),
        dma((2, 2)),
        dma,
        dma,
        dma((2,)),
    ]
    return pl.pallas_call(
        functools.partial(chain_kernel, early),
        in_specs=[pl.BlockSpec(memory_space=pl.ANY)] * 8,
        out_specs=pl.BlockSpec(memory_space=pl.ANY),
        out_shape=jax.ShapeDtypeStruct((beams,) + tile, f32),
        scratch_shapes=scratch,
        compiler_params=pltpu.CompilerParams(
            collective_id=2, has_side_effects=True, vmem_limit_bytes=CHAIN_VMEM
        ),
        name="chain",
    )(
        arc_start,
        arc_offsets.T,
        doppler_bins.T,
        train_mask.T,
        steer_angles.T,
        echoes,
        jnp.asarray(table),
        spread,
    )


def body(echoes, arc_start, arc_offsets, doppler_bins, steer_angles, train_mask):
    columns = echoes.shape[1]
    num_pulses = echoes.shape[2]
    cells = echoes.shape[3]
    num_sel = arc_offsets.shape[1]
    chan_count = doppler_bins.shape[1]
    cycle_size = lax.axis_size("az")
    cycle_pos = lax.axis_index("az")
    rng_size = lax.axis_size("rng")
    beam_count = BEAMS // cycle_size
    item_count = beam_count * chan_count
    dof = BINS * num_sel
    pairs = beam_count // 2
    if (
        columns == ARC
        and beam_count % 2 == 0
        and pairs * (COLS // BEAMS) == ARC // 2
        and rng_size == 8
        and cycle_size > 2
        and cells == 128
        and chan_count % 16 == 0
        and chan_count // 2 * dof % 128 == 0
        and 2 * dof + 8 <= 128
        and dof % 16 == 0
        and pairs * (chan_count // 2) <= 128
        and pairs > LATE
        and rng_size // 2 > 3
    ):
        return chain(
            echoes, arc_start, arc_offsets, doppler_bins, steer_angles, train_mask, pairs - LATE
        )
    table_re, table_im = doppler_table(num_pulses)
    table = jnp.concatenate(
        [jnp.concatenate([table_re, -table_im], 1), jnp.concatenate([table_im, table_re], 1)], 0
    )

    def own(x):
        return lax.dynamic_slice_in_dim(x, cycle_pos * beam_count, beam_count, axis=0)

    arc_first = (own(arc_start) - cycle_pos * columns + ARC // 2) % COLS
    col_index = arc_first[:, None] + own(arc_offsets)
    bins_own = own(doppler_bins)
    angles = own(steer_angles)
    block_count = train_mask.shape[1]
    cell_mask = (
        jnp.broadcast_to(train_mask[:, :, None], (beam_count, block_count, BLK))
        .reshape(beam_count, 1, block_count * BLK)
        .astype(jnp.bfloat16)
    )
    smem = pl.BlockSpec(memory_space=pltpu.SMEM)

    def snap_gram(extended, first, last, base):
        share = last - first
        ext_cols = extended.shape[1]
        return pl.pallas_call(
            snap_gram_kernel,
            grid=(share,),
            in_specs=[
                smem,
                smem,
                smem,
                smem,
                pl.BlockSpec((2, ext_cols, num_pulses, cells), lambda b: (0, 0, 0, 0)),
                pl.BlockSpec(table.shape, lambda b: (0, 0)),
                pl.BlockSpec((1, 1, cells), lambda b: (b, 0, 0)),
            ],
            out_specs=[
                pl.BlockSpec((1, 2, num_pulses, num_sel, cells), lambda b: (b, 0, 0, 0, 0)),
                pl.BlockSpec((1, dof, chan_count * dof), lambda b: (b, 0, 0)),
            ],
            out_shape=[
                jax.ShapeDtypeStruct((share, 2, num_pulses, num_sel, cells), jnp.bfloat16),
                jax.ShapeDtypeStruct((share, dof, chan_count * dof), jnp.float32),
            ],
            compiler_params=pltpu.CompilerParams(vmem_limit_bytes=VMEM_LIMIT),
            cost_estimate=pl.CostEstimate(
                flops=share * 600_000_000, bytes_accessed=share * 1_500_000, transcendentals=0
            ),
            name="snap_gram",
        )(
            col_index[first:last] - base,
            bins_own[first:last],
            jnp.cos(angles)[first:last],
            jnp.sin(angles)[first:last],
            extended,
            table,
            cell_mask[first:last],
        )

    width = ARC // 2
    forward = [(i, (i + 1) % cycle_size) for i in range(cycle_size)]
    backward = [(target, source) for source, target in forward]
    low = lax.ppermute(echoes[:, columns - width :], "az", forward)
    high = lax.ppermute(echoes[:, :width], "az", backward)
    step = COLS // BEAMS
    half = beam_count // 2
    if (half - 1) * step + step - 1 + ARC - 1 < width + columns and half * step >= width:
        v_lo, gram_lo = snap_gram(jnp.concatenate([low, echoes], 1), 0, half, 0)
        high, v_lo, gram_lo = lax.optimization_barrier((high, v_lo, gram_lo))
        v_hi, gram_hi = snap_gram(jnp.concatenate([echoes, high], 1), half, beam_count, width)
        v_parts = (v_lo, v_hi)
        grams = (gram_lo, gram_hi)
        if rng_size % 4 or item_count // rng_size < chan_count:
            grams = (jnp.concatenate(grams, 0),)
    else:
        v_one, gram_one = snap_gram(jnp.concatenate([low, echoes, high], 1), 0, beam_count, 0)
        v_parts = (v_one,)
        grams = (gram_one,)

    per = item_count // rng_size
    if per < chan_count:
        split = chan_count // per
        gram = grams[0].reshape(beam_count, dof, split, per * dof)
        grams = (jnp.swapaxes(gram, 1, 2).reshape(beam_count * split, dof, per * dof),)
        width = per
    else:
        width = chan_count
    vm = pltpu.VMEM
    dma = pltpu.SemaphoreType.DMA
    line = rng_size // 2
    chunk = (grams[0].shape[0] * len(grams) // rng_size, dof, grams[0].shape[2])
    part = pl.pallas_call(
        functools.partial(scatter_kernel, line, len(grams)),
        in_specs=[pl.BlockSpec(memory_space=vm)] * len(grams),
        out_specs=pl.BlockSpec(memory_space=vm),
        out_shape=jax.ShapeDtypeStruct(chunk, jnp.float32),
        scratch_shapes=[vm((line,) + chunk, jnp.float32)] * 4 + [dma((line,))] * 6,
        compiler_params=pltpu.CompilerParams(
            collective_id=0, has_side_effects=True, vmem_limit_bytes=VMEM_LIMIT
        ),
        name="scatter",
    )(*[g.reshape((rng_size // len(grams),) + chunk) for g in grams])
    solved = pl.pallas_call(
        solve_kernel,
        out_shape=jax.ShapeDtypeStruct((2 * dof + 8, per), jnp.float32),
        scratch_shapes=[
            vm((dof, per, dof), jnp.float32),
            vm((dof, dof, per), jnp.float32),
            vm((dof, dof, per), jnp.float32),
            vm((dof, dof, per), jnp.float32),
            vm((dof, per), jnp.float32),
            vm((dof, per), jnp.float32),
            vm((dof, per), jnp.float32),
            vm((dof, per), jnp.float32),
        ],
        compiler_params=pltpu.CompilerParams(vmem_limit_bytes=VMEM_LIMIT),
        name="solve",
    )(part)
    lanes = 128
    local_count = (BLK * jnp.sum(train_mask, axis=1)).astype(jnp.float32)
    pad_rows = -per % 8
    payload = jnp.concatenate(
        [
            jnp.pad(solved.T, ((0, pad_rows), (0, lanes - solved.shape[0]))),
            jnp.broadcast_to(local_count[:, None], (beam_count, lanes)),
        ],
        0,
    )
    halves = len(v_parts)
    any_spec = pl.BlockSpec(memory_space=pl.ANY)
    block = (chan_count, cells)
    out = pl.pallas_call(
        functools.partial(apply_kernel, halves, per, dof),
        in_specs=[pl.BlockSpec(memory_space=vm)] * 2 + [any_spec] * halves,
        out_specs=pl.BlockSpec(memory_space=vm),
        out_shape=jax.ShapeDtypeStruct((beam_count,) + block, jnp.float32),
        scratch_shapes=[
            vm((beam_count, 2, num_pulses, num_sel, cells), jnp.bfloat16),
            vm((rng_size,) + payload.shape, jnp.float32),
            vm((beam_count,) + block, jnp.float32),
            vm((2, 8, item_count), jnp.float32),
            vm((2, 8, item_count), jnp.float32),
            vm((beam_count,) + block, jnp.float32),
            vm(block, jnp.float32),
            vm(block, jnp.float32),
            dma((halves,)),
            dma((rng_size,)),
            dma((rng_size,)),
            dma((2,)),
            dma((2,)),
            dma((2,)),
            dma((2,)),
        ],
        compiler_params=pltpu.CompilerParams(
            collective_id=1, has_side_effects=True, vmem_limit_bytes=VMEM_LIMIT
        ),
        name="apply",
    )(payload, bins_own[:, :, None], *v_parts)
    return out


def solution(mesh):
    return jax.shard_map(
        body,
        mesh=mesh,
        in_specs=(P(None, "az", None, "rng"), P(), P(), P(), P(), P("az", "rng")),
        out_specs=P("az", None, "rng"),
        check_vma=False,
    )
```

```python
import functools

import jax
import numpy as np
import jax.numpy as jnp
from jax import lax
from jax.experimental import pallas as pl
from jax.experimental.pallas import tpu as pltpu
from jax.sharding import PartitionSpec as P


COLS = 256
ARC = 64
BINS = 3
BEAMS = 64
BLK = 128
LOADING = 0.1
VMEM_LIMIT = 48 << 20
CHAIN_VMEM = 66_200_000
CODE_TOP = 32000.0
LAG = 3
LATE = 4


def doppler_table(num_pulses):
    freq_ids = jnp.arange(num_pulses, dtype=jnp.int32)
    phase_steps = freq_ids[:, None] * freq_ids[None, :] % num_pulses
    phase_angle = -2.0 * jnp.pi / num_pulses * phase_steps.astype(jnp.float32)
    return (jnp.cos(phase_angle).astype(jnp.bfloat16), jnp.sin(phase_angle).astype(jnp.bfloat16))


def snap_gram_kernel(
    col_ref, bins_ref, cos_ref, sin_ref, ext_ref, table_ref, mask_ref, v_ref, gram_ref
):
    beam = pl.program_id(0)
    pulses = ext_ref.shape[2]
    num_sel = col_ref.shape[1]
    num_chan = bins_ref.shape[1]
    table = table_ref[...]
    parts_re, parts_im = [], []
    for j in range(num_sel):
        col = col_ref[beam, j]
        data = jnp.concatenate([ext_ref[0, col], ext_ref[1, col]], axis=0)
        spec = jnp.dot(table, data, preferred_element_type=jnp.float32)
        cosine = cos_ref[beam, j]
        sine = sin_ref[beam, j]
        spec_re = spec[:pulses]
        spec_im = spec[pulses:]
        parts_re.append(cosine * spec_re - sine * spec_im)
        parts_im.append(sine * spec_re + cosine * spec_im)
    for part, pieces in enumerate((parts_re, parts_im)):
        stacked = jnp.swapaxes(jnp.stack(pieces, 0), 0, 1)
        v_ref[0, part] = stacked.astype(jnp.bfloat16)
    dof = BINS * num_sel
    mask_row = mask_ref[0]
    row = lax.broadcasted_iota(jnp.int32, (dof, dof), 0)
    colm = lax.broadcasted_iota(jnp.int32, (dof, dof), 1)
    lower = row >= colm
    packed = []
    for k in range(num_chan):
        centre = bins_ref[beam, k]
        ids = [(centre + (q - BINS // 2 + pulses)) % pulses for q in range(BINS)]
        u_re = jnp.concatenate([v_ref[0, 0, f] for f in ids], 0)
        u_im = jnp.concatenate([v_ref[0, 1, f] for f in ids], 0)
        right = jnp.concatenate([u_re, u_im], 1)
        m_re = u_re * mask_row
        m_im = u_im * mask_row
        left = jnp.concatenate(
            [jnp.concatenate([m_re, m_im], 1), jnp.concatenate([m_im, -m_re], 1)], 0
        )
        both = lax.dot_general(
            left, right, (((1,), (1,)), ((), ())), preferred_element_type=jnp.float32
        )
        packed.append(jnp.where(lower, both[:dof], both[dof:]))
    gram_ref[0] = jnp.concatenate(packed, 1)


def solve_kernel(part_ref, out_ref, stack, turned, hr, hi, xr, xi, yr, yi):
    lead, dof, wide = part_ref.shape
    width = wide // dof
    lanes = lead * width
    nb = dof // 8
    group = min(8, lanes)
    for g in range(0, lanes, group):
        pieces = []
        for item in range(g, g + group):
            k = item % width
            pieces.append(part_ref[item // width, :, k * dof : (k + 1) * dof])
        stack[:, g : g + group, :] = jnp.swapaxes(jnp.stack(pieces, 0), 0, 1)
    for i in range(dof):
        turned[i] = stack[i].T
    trace = jnp.zeros((1, lanes), jnp.float32)
    for i in range(dof):
        trace = trace + turned[i, i : i + 1, :]
    load = (LOADING / dof) * trace
    cube = (8, 8, lanes)
    row = lax.broadcasted_iota(jnp.int32, cube, 0)
    col = lax.broadcasted_iota(jnp.int32, cube, 1)
    for ib in range(nb):
        rows = slice(8 * ib, 8 * ib + 8)
        for jb in range(ib, nb):
            cols = slice(8 * jb, 8 * jb + 8)
            imag = turned[rows, cols, :]
            real = jnp.swapaxes(turned[cols, rows, :], 0, 1)
            if ib == jb:
                straight, flip = imag, real
                real = jnp.where(row >= col, straight, flip)
                real = jnp.where(row == col, real + load[None], real)
                imag = jnp.where(row < col, straight, jnp.where(row > col, -flip, 0.0))
            hr[rows, cols, :] = real
            hi[rows, cols, :] = imag
    yr[...] = jnp.ones_like(yr)
    yi[...] = jnp.zeros_like(yi)
    xr[...] = jnp.zeros_like(xr)
    xi[...] = jnp.zeros_like(xi)
    sub = lax.broadcasted_iota(jnp.int32, (8, lanes), 0)

    for kb in range(nb):

        def step(k, carry, kb=kb, first=0):
            pivot = 1.0 / hr[k, pl.ds(k, 1), :]
            rr = [hr[k, 8 * b : 8 * b + 8, :] for b in range(kb, nb)]
            ri = [hi[k, 8 * b : 8 * b + 8, :] for b in range(kb, nb)]
            rs = [x + y for x, y in zip(rr, ri, strict=True)]
            gr = jnp.broadcast_to(yr[pl.ds(k, 1), :], (8, lanes))
            gi = jnp.broadcast_to(yi[pl.ds(k, 1), :], (8, lanes))
            for ib in range(kb, nb):
                fr = rr[ib - kb] * pivot
                fi = -ri[ib - kb] * pivot
                if ib == kb:
                    live = sub + 8 * kb > k
                    fr = jnp.where(live, fr, 0.0)
                    fi = jnp.where(live, fi, 0.0)
                fs = fr + fi
                fd = fi - fr
                own = slice(8 * ib, 8 * ib + 8)
                yr[own, :] = yr[own, :] - (fr * gr - fi * gi)
                yi[own, :] = yi[own, :] - (fr * gi + fi * gr)
                for s in range(first + 1 if ib == kb else 0, 8):
                    i = 8 * ib + s
                    cr = jnp.broadcast_to(fr[s : s + 1], (8, lanes))
                    cs = jnp.broadcast_to(fs[s : s + 1], (8, lanes))
                    cd = jnp.broadcast_to(fd[s : s + 1], (8, lanes))
                    for b in range(ib, nb):
                        pr, pi = rr[b - kb], ri[b - kb]
                        sl = slice(8 * b, 8 * b + 8)
                        both = cr * rs[b - kb]
                        hr[i, sl, :] = (hr[i, sl, :] - both) + cs * pi
                        hi[i, sl, :] = (hi[i, sl, :] - both) - cd * pr
            return carry

        for first in range(8):
            step(8 * kb + first, 0, first=first)

    for ib in reversed(range(nb)):

        def back(t, carry, ib=ib):
            i = 8 * ib + 7 - t
            sr = jnp.zeros((8, lanes), jnp.float32)
            si = jnp.zeros((8, lanes), jnp.float32)
            for b in range(ib, nb):
                sl = slice(8 * b, 8 * b + 8)
                ar, ai = hr[i, sl, :], hi[i, sl, :]
                br, bi = xr[sl, :], xi[sl, :]
                sr = sr + (ar * br - ai * bi)
                si = si + (ar * bi + ai * br)
            pivot = 1.0 / hr[i, pl.ds(i, 1), :]
            top_r = yr[pl.ds(i, 1), :]
            top_i = yi[pl.ds(i, 1), :]
            xr[pl.ds(i, 1), :] = (top_r - jnp.sum(sr, 0, keepdims=True)) * pivot
            xi[pl.ds(i, 1), :] = (top_i - jnp.sum(si, 0, keepdims=True)) * pivot
            return carry

        lax.fori_loop(0, 8, back, 0)
    out_ref[:dof, :lanes] = xr[...]
    out_ref[dof : 2 * dof, :lanes] = xi[...]
    out_ref[2 * dof : 2 * dof + 8, :lanes] = jnp.broadcast_to(
        jnp.sum(xr[...], 0, keepdims=True), (8, lanes)
    )


MESH = pl.DeviceIdType.MESH


def scatter_kernel(n, halves, *refs):
    g_refs = refs[:halves]
    out_ref, pair, acc, right, left, psend, precv, rsend, rrecv, lsend, lrecv = refs[halves:]
    share = n // halves

    def own(t, core):
        return g_refs[t // share].at[2 * (t % share) + core]

    me = lax.axis_index("rng")
    z = me // 2
    c = me % 2
    mate = 2 * z + 1 - c
    ahead = lax.rem(me + 2, 2 * n)
    behind = lax.rem(me + 2 * n - 2, 2 * n)
    barrier = pltpu.get_barrier_semaphore()
    pl.semaphore_signal(barrier, inc=1, device_id={"rng": mate}, device_id_type=MESH)
    pl.semaphore_signal(barrier, inc=1, device_id={"rng": ahead}, device_id_type=MESH)
    pl.semaphore_signal(barrier, inc=1, device_id={"rng": behind}, device_id_type=MESH)
    pl.semaphore_wait(barrier, 3)

    order = []
    for t in range((n + 1) // 2):
        order.append(n - 1 - t)
        if t != n - 1 - t:
            order.append(t)

    def pair_copy(t):
        return pltpu.make_async_remote_copy(
            src_ref=own(t, 1 - c),
            dst_ref=pair.at[t],
            send_sem=psend.at[t],
            recv_sem=precv.at[t],
            device_id={"rng": mate},
            device_id_type=MESH,
        )

    def right_copy(t):
        return pltpu.make_async_remote_copy(
            src_ref=acc.at[t],
            dst_ref=right.at[t],
            send_sem=rsend.at[t],
            recv_sem=rrecv.at[t],
            device_id={"rng": ahead},
            device_id_type=MESH,
        )

    def left_copy(t):
        return pltpu.make_async_remote_copy(
            src_ref=acc.at[t],
            dst_ref=left.at[t],
            send_sem=lsend.at[t],
            recv_sem=lrecv.at[t],
            device_id={"rng": behind},
            device_id_type=MESH,
        )

    for t in order:
        pair_copy(t).start()
    for t in order:
        pair_copy(t).wait_recv()
        acc[t] = own(t, c)[...] + pair[t]

        @pl.when(jnp.logical_and(z == 0, t > 0))
        def _(t=t):
            right_copy(t).start()

        @pl.when(jnp.logical_and(z == n - 1, t < n - 1))
        def _(t=t):
            left_copy(t).start()

    for place in range(n):
        events = [(place + n - 1 - t, 0, t) for t in range(place + 1, n) if place > 0]
        events += [(n - 1 - place + t, 1, t) for t in range(place) if place < n - 1]

        @pl.when(z == place)
        def _(place=place, events=sorted(events)):
            for _, side, t in events:
                copy = left_copy(t) if side else right_copy(t)
                source = left if side else right
                copy.wait_recv()
                acc[t] = acc[t] + source[t]
                copy.start()
            total = acc[place]
            if place > 0:
                right_copy(place).wait_recv()
                total = total + right[place]
            if place < n - 1:
                left_copy(place).wait_recv()
                total = total + left[place]
            out_ref[...] = total

    for t in range(n):
        pair_copy(t).wait_send()

        @pl.when(z < t)
        def _(t=t):
            right_copy(t).wait_send()

        @pl.when(z > t)
        def _(t=t):
            left_copy(t).wait_send()


def apply_kernel(
    halves,
    per,
    dof,
    pay_ref,
    bins_ref,
    *refs,
):
    v_refs = refs[:halves]
    (out_ref, v_all, gat, power, edge, halo, sums, az_lo, az_hi) = refs[halves : halves + 9]
    (vsem, gsend, grecv, esend, erecv, asend, arecv) = refs[halves + 9 :]
    me = lax.axis_index("rng")
    az = lax.axis_index("az")
    n = lax.axis_size("rng")
    m = lax.axis_size("az")
    beams, num_chan, cells = out_ref.shape
    pulses, num_sel = v_all.shape[2], v_all.shape[3]
    taps = pulses * num_sel
    az_next = lax.rem(az + 1, m)
    az_prev = lax.rem(az + m - 1, m)
    barrier = pltpu.get_barrier_semaphore()
    for d in range(1, n):
        peer = lax.rem(me + d, n)
        pl.semaphore_signal(barrier, inc=1, device_id={"rng": peer}, device_id_type=MESH)
    for other in (az_next, az_prev):
        pl.semaphore_signal(barrier, inc=1, device_id={"az": other}, device_id_type=MESH)
    share = beams // halves
    loads = []
    for h in range(halves):
        load = pltpu.make_async_copy(v_refs[h], v_all.at[pl.ds(h * share, share)], vsem.at[h])
        load.start()
        loads.append(load)
    pl.semaphore_wait(barrier, n + 1)

    copies = []
    for d in range(1, n):
        peer = lax.rem(me + d, n)
        copy = pltpu.make_async_remote_copy(
            src_ref=pay_ref,
            dst_ref=gat.at[me],
            send_sem=gsend.at[d],
            recv_sem=grecv.at[d],
            device_id={"rng": peer},
            device_id_type=MESH,
        )
        copy.start()
        copies.append(copy)
    gat[me] = pay_ref[...]
    for load in loads:
        load.wait()
    for copy in copies:
        copy.wait_recv()
    rows = gat.shape[1] - beams
    count = jnp.zeros((beams, gat.shape[2]), jnp.float32)
    for r in range(n):
        count = count + gat[r, rows:, :]
    sums[0] = jnp.zeros(sums.shape[1:], jnp.float32)
    for b in range(beams):
        sums[b, :1, :] = count[b : b + 1]
    freq = lax.broadcasted_iota(jnp.int32, (num_chan, taps), 1) // num_sel
    lanes = gat.shape[2]
    lane = lax.broadcasted_iota(jnp.int32, (num_chan, lanes), 1)

    def one(b, carry):
        if per >= num_chan:
            ratio = per // num_chan
            start = pl.multiple_of((b % ratio) * num_chan, 8)
            w = gat[b // ratio, pl.ds(start, num_chan), :]
        else:
            split = num_chan // per
            w = jnp.concatenate([gat[b * split + t, :per, :] for t in range(split)], 0)
        w = w * sums[b, :1, :]
        quiet = w[:, 2 * dof : 2 * dof + 1]
        centre = bins_ref[b]
        planes = []
        hits = []
        for q in range(BINS):
            f = lax.rem(centre + (q - BINS // 2 + pulses), pulses)
            hits.append(freq == f)
        for part in range(2):
            plane = jnp.zeros((num_chan, taps), jnp.float32)
            for q in range(BINS):
                start = part * dof + q * num_sel
                piece = pltpu.roll(w, (lanes - start) % lanes, 1) if start else w
                piece = jnp.where(lane < num_sel, piece, 0.0)
                span = num_sel
                while span < lanes:
                    piece = piece + pltpu.roll(piece, span, 1)
                    span *= 2
                tiled = jnp.concatenate([piece] * (taps // lanes), 1)
                plane = jnp.where(hits[q], tiled, plane)
            planes.append(plane)
        top = jnp.concatenate([planes[0], planes[1]], 1)
        low = jnp.concatenate([-planes[1], planes[0]], 1)
        lhs = jnp.concatenate([top, low], 0).astype(jnp.bfloat16)
        flat = v_all[b].reshape(2 * taps, cells)
        proj = jnp.dot(lhs, flat, preferred_element_type=jnp.float32)
        p0 = proj[:num_chan]
        p1 = proj[num_chan:]
        power[b] = (p0 * p0 + p1 * p1) / quiet
        return carry

    lax.fori_loop(0, beams, one, 0)
    items = beams * num_chan
    turned = power[...].reshape(items, cells).T
    edge[0] = turned[:8]
    edge[1] = turned[cells - 8 :]

    def edge_copy(side):
        target = lax.rem(me + 1, n) if side else lax.rem(me + n - 1, n)
        return pltpu.make_async_remote_copy(
            src_ref=edge.at[side],
            dst_ref=halo.at[side],
            send_sem=esend.at[side],
            recv_sem=erecv.at[side],
            device_id={"rng": target},
            device_id_type=MESH,
        )

    for side in range(2):
        edge_copy(side).start()
    for side in range(2):
        edge_copy(side).wait()
    before = jnp.where(me > 0, halo[1, 7:8], 0.0)
    after = jnp.where(me < n - 1, halo[0, 0:1], 0.0)
    turned = (
        jnp.concatenate([before, turned[:-1]], 0)
        + turned
        + jnp.concatenate([turned[1:], after], 0)
    )
    sums[...] = turned.T.reshape(beams, num_chan, cells)
    up = pltpu.make_async_remote_copy(
        src_ref=sums.at[beams - 1],
        dst_ref=az_lo,
        send_sem=asend.at[0],
        recv_sem=arecv.at[0],
        device_id={"az": az_next},
        device_id_type=MESH,
    )
    down = pltpu.make_async_remote_copy(
        src_ref=sums.at[0],
        dst_ref=az_hi,
        send_sem=asend.at[1],
        recv_sem=arecv.at[1],
        device_id={"az": az_prev},
        device_id_type=MESH,
    )
    up.start()
    down.start()
    for b in range(1, beams - 1):
        out_ref[b] = (sums[b - 1] + sums[b] + sums[b + 1]) / 9.0
    up.wait_recv()
    down.wait_recv()
    out_ref[0] = (az_lo[...] + sums[0] + sums[1]) / 9.0
    out_ref[beams - 1] = (sums[beams - 2] + sums[beams - 1] + az_hi[...]) / 9.0
    up.wait_send()
    down.wait_send()
    for copy in copies:
        copy.wait_send()


def gram_of(v_ref, beam, bins, mask_row):
    pulses = v_ref.shape[2]
    num_sel = v_ref.shape[3]
    dof = BINS * num_sel
    row = lax.broadcasted_iota(jnp.int32, (dof, dof), 0)
    colm = lax.broadcasted_iota(jnp.int32, (dof, dof), 1)
    lower = row >= colm
    packed = []
    for centre in bins:
        ids = [lax.rem(centre + (q - BINS // 2 + pulses), pulses) for q in range(BINS)]
        u_re = jnp.concatenate([v_ref[beam, 0, f] for f in ids], 0)
        u_im = jnp.concatenate([v_ref[beam, 1, f] for f in ids], 0)
        right = jnp.concatenate([u_re, u_im], 1)
        m_re = u_re * mask_row
        m_im = u_im * mask_row
        left = jnp.concatenate(
            [jnp.concatenate([m_re, m_im], 1), jnp.concatenate([m_im, -m_re], 1)], 0
        )
        both = lax.dot_general(
            left, right, (((1,), (1,)), ((), ())), preferred_element_type=jnp.float32
        )
        packed.append(jnp.where(lower, both[:dof], both[dof:]))
    return packed


def chain_kernel(
    early,
    start_hbm,
    offs_hbm,
    bins_hbm,
    train_hbm,
    angle_hbm,
    echoes,
    table_hbm,
    spread_hbm,
    out_hbm,
    start_ref,
    offs_ref,
    bins_ref,
    train_ref,
    angle_ref,
    chan_ref,
    table_ref,
    spread_ref,
    turn,
    ext,
    halo,
    v_all,
    gram,
    pair,
    coded,
    scale,
    code_in,
    scale_in,
    part,
    solved,
    stack,
    turned,
    hr,
    hi,
    xr,
    xi,
    yr,
    yi,
    masks,
    totals,
    counts,
    pay,
    gat_e,
    gat_l,
    tiles_e,
    tiles_l,
    pw,
    pl_left,
    pl_right,
    rows,
    out_ref,
    esem,
    osem,
    hsend,
    hrecv,
    psend,
    precv,
    dsend,
    drecv,
    msend,
    mrecv,
    gsend,
    grecv,
    hello,
    lsend,
    lrecv,
    tsend,
    trecv,
    arecv,
):
    me = lax.axis_index("rng")
    az = lax.axis_index("az")
    size = lax.axis_size("rng")
    m = lax.axis_size("az")
    n = size // 2
    z = me // 2
    c = lax.rem(me, 2)
    beams, num_chan, cells = out_hbm.shape
    columns = echoes.shape[1]
    pulses = echoes.shape[2]
    num_sel = offs_ref.shape[0]
    blocks = train_ref.shape[0]
    dof = BINS * num_sel
    taps = pulses * num_sel
    steps = beams // 2
    width = ARC // 2
    w = width // steps
    side_chan = num_chan // 2
    half = side_chan * dof
    lanes = pay.shape[1]
    az_next = lax.rem(az + 1, m)
    az_prev = lax.rem(az + m - 1, m)
    ahead = lax.rem(me + 1, size)
    behind = lax.rem(me + size - 1, size)
    mate = 2 * z + 1 - c
    mid_l = n // 2 - 1
    mid_r = n // 2
    late = steps - early
    middles = ((0, mid_l), (1, mid_r))
    ends = ((0, 0), (1, n - 1))
    is_mid = jnp.logical_or(z == mid_l, z == mid_r)

    loads = [
        pltpu.make_async_copy(src, dst, esem.at[i])
        for i, (src, dst) in enumerate(
            (
                (start_hbm, start_ref),
                (offs_hbm, offs_ref),
                (bins_hbm, bins_ref),
                (train_hbm, train_ref),
                (angle_hbm, angle_ref),
                (bins_hbm, chan_ref),
                (table_hbm, table_ref),
                (spread_hbm, spread_ref),
                (echoes, ext.at[:, width : width + columns]),
            )
        )
    ]
    barrier = pltpu.get_barrier_semaphore()
    for other in (az_next, az_prev):
        pl.semaphore_signal(barrier, inc=1, device_id={"az": other}, device_id_type=MESH)
    pl.semaphore_signal(barrier, inc=1, device_id={"rng": mate}, device_id_type=MESH)
    for place in range(n):
        near = jnp.logical_or(is_mid, place in (mid_l, mid_r))

        @pl.when(jnp.logical_and(z != place, near))
        def _(place=place):
            pl.semaphore_signal(
                barrier, inc=1, device_id={"rng": 2 * place + c}, device_id_type=MESH
            )

    for load in loads:
        load.start()
    pl_left[...] = jnp.zeros(pl_left.shape, jnp.float32)
    pl_right[...] = jnp.zeros(pl_right.shape, jnp.float32)
    solved[...] = jnp.zeros(solved.shape, jnp.float32)
    part[...] = jnp.zeros(part.shape, jnp.float32)
    counts[...] = jnp.zeros(counts.shape, jnp.float32)
    pl.semaphore_wait(barrier, 3 + jnp.where(is_mid, n - 1, 2))

    def all_of(ref, sem):
        pltpu.make_async_copy(ref, ref, sem).wait()

    def low_copy(i):
        return pltpu.make_async_remote_copy(
            src_ref=echoes.at[:, pl.ds(columns - w * (i + 1), w)],
            dst_ref=halo.at[i, 0],
            send_sem=hsend,
            recv_sem=hrecv.at[i],
            device_id={"az": az_next},
            device_id_type=MESH,
        )

    def high_copy(i):
        return pltpu.make_async_remote_copy(
            src_ref=echoes.at[:, pl.ds(w * i, w)],
            dst_ref=halo.at[i, 1],
            send_sem=hsend,
            recv_sem=hrecv.at[i],
            device_id={"az": az_prev},
            device_id_type=MESH,
        )

    for i in range(steps):
        low_copy(i).start()
        high_copy(i).start()
    for side, middle in middles:

        @pl.when(z == middle)
        def _(side=side):
            end = 2 * (n - 1 if side else 0) + c
            pl.semaphore_signal(hello, inc=1, device_id={"rng": end}, device_id_type=MESH)

    for load in loads:
        load.wait()

    cell = lax.broadcasted_iota(jnp.int32, (1, cells), 1) // BLK
    for b in range(beams):
        row = jnp.zeros((1, cells), jnp.float32)
        for blk in range(blocks):
            row = jnp.where(cell == blk, train_ref[blk, b].astype(jnp.float32), row)
        masks[0, b : b + 1, :] = row

    mask_copy = pltpu.make_async_remote_copy(
        src_ref=masks.at[0],
        dst_ref=masks.at[1],
        send_sem=msend,
        recv_sem=mrecv,
        device_id={"rng": mate},
        device_id_type=MESH,
    )
    mask_copy.start()
    turn[0] = jnp.cos(angle_ref[...])
    turn[1] = jnp.sin(angle_ref[...])
    mask_copy.wait_recv()
    totals[...] = jnp.broadcast_to(
        jnp.sum(masks[0] + masks[1], 1, keepdims=True), totals.shape
    )

    def mine(t):
        return jnp.where(c == 0, steps - 1 - t, steps + t)

    def theirs(t):
        return jnp.where(c == 0, steps + t, steps - 1 - t)

    def owner_of(side, t):
        return jnp.where(t < early, side * (n - 1), mid_l + side)

    def row_of(t):
        return jnp.where(t < early, t, t - early)

    def pair_copy(t):
        return pltpu.make_async_remote_copy(
            src_ref=gram.at[theirs(t)],
            dst_ref=pair.at[t],
            send_sem=psend,
            recv_sem=precv.at[t],
            device_id={"rng": mate},
            device_id_type=MESH,
        )

    def code_copies(side, t, source):
        owner = 2 * owner_of(side, t) + c
        return [
            pltpu.make_async_remote_copy(
                src_ref=src.at[2 * t + side],
                dst_ref=dst.at[row_of(t), source],
                send_sem=dsend.at[i],
                recv_sem=drecv.at[i, row_of(t)],
                device_id={"rng": owner},
                device_id_type=MESH,
            )
            for i, (src, dst) in enumerate(((coded, code_in), (scale, scale_in)))
        ]

    table = table_ref[...]
    blane = lax.broadcasted_iota(jnp.int32, angle_ref.shape, 1)

    def one_beam(b):
        bg = az * beams + b
        first = lax.rem(start_ref[bg] - az * columns + (width + COLS), COLS)
        first = jnp.minimum(first, ext.shape[1] - ARC)
        here = blane == bg
        cosine = jnp.sum(jnp.where(here, turn[0], 0.0), 1, keepdims=True)
        sine = jnp.sum(jnp.where(here, turn[1], 0.0), 1, keepdims=True)
        cosine = jnp.broadcast_to(cosine, (num_sel, cells))[None]
        sine = jnp.broadcast_to(sine, (num_sel, cells))[None]
        parts_re, parts_im = [], []
        for j in range(num_sel):
            col = first + offs_ref[j, bg]
            data = jnp.concatenate([ext[0, col], ext[1, col]], axis=0)
            spec = jnp.dot(table, data, preferred_element_type=jnp.float32)
            parts_re.append(spec[:pulses])
            parts_im.append(spec[pulses:])
        spec_re = jnp.swapaxes(jnp.stack(parts_re, 0), 0, 1)
        spec_im = jnp.swapaxes(jnp.stack(parts_im, 0), 0, 1)
        v_all[b, 0] = (cosine * spec_re - sine * spec_im).astype(jnp.bfloat16)
        v_all[b, 1] = (sine * spec_re + cosine * spec_im).astype(jnp.bfloat16)
        mask_row = masks[0, pl.ds(b, 1), :].astype(jnp.bfloat16)
        bins = [bins_ref[k, bg] for k in range(num_chan)]
        packed = gram_of(v_all, b, bins, mask_row)
        gram[b, 0] = jnp.concatenate(packed[:side_chan], 1)
        gram[b, 1] = jnp.concatenate(packed[side_chan:], 1)

    def slot(s, carry):
        t = s - 1

        @pl.when(jnp.logical_and(t >= 0, t < steps))
        def _():
            pair_copy(t).wait_recv()
            own = mine(t)
            number = totals[pl.ds(own, 1), :]
            row = row_of(t)
            for side in range(2):
                total = gram[own, side] + pair[t, side]
                owner = owner_of(side, t)

                @pl.when(z == owner)
                def _(total=total):
                    part[row] = total
                    counts[row] = number

                @pl.when(z != owner)
                def _(side=side, total=total):
                    top = jnp.max(jnp.abs(total), 0, keepdims=True)
                    top = jnp.maximum(top, 1e-30)
                    code = jnp.round(total * (CODE_TOP / top))
                    coded[2 * t + side] = code.astype(jnp.int32).astype(jnp.int16)
                    scale[2 * t + side, :, :half] = top * (1.0 / CODE_TOP)
                    scale[2 * t + side, :, half:] = number

            far = jnp.where(z < n // 2, 1, 0)
            for side in (far, 1 - far):

                @pl.when(z != owner_of(side, t))
                def _(side=side):
                    for copy in code_copies(side, t, z):
                        copy.start()

        tt = s - LAG

        @pl.when(jnp.logical_and(tt >= 0, tt < steps))
        def _():
            row = row_of(tt)
            for side in range(2):
                for owner, is_early in ((ends[side][1], True), (middles[side][1], False)):
                    right_time = tt < early if is_early else tt >= early

                    @pl.when(jnp.logical_and(z == owner, right_time))
                    def _(side=side, owner=owner):
                        total = part[row]
                        number = counts[row]
                        all_of(code_in.at[row, pl.ds(0, n - 1)], drecv.at[0, row])
                        all_of(scale_in.at[row, pl.ds(0, n - 1)], drecv.at[1, row])
                        for source in range(n):
                            if source != owner:
                                code = code_in[row, source].astype(jnp.int32)
                                code = code.astype(jnp.float32)
                                total = total + code * scale_in[row, source, :, :half]
                                number = number + scale_in[row, source, :, half:]
                        part[row] = total
                        counts[row] = number

        @pl.when(s < steps)
        def _():
            all_of(halo.at[s], hrecv.at[s])
            ext[:, pl.ds(width - w * (s + 1), w)] = halo[s, 0]
            ext[:, pl.ds(width + columns + w * s, w)] = halo[s, 1]
            one_beam(theirs(s))
            pair_copy(s).start()
            one_beam(mine(s))

        return carry

    @pl.when(jnp.logical_not(is_mid))
    def _():
        pl.semaphore_wait(hello, 1)

    lax.fori_loop(0, steps + LAG, slot, 0)

    items = pay.shape[0]

    def send_copy(at, place, core, side, buf, which):
        return pltpu.make_async_remote_copy(
            src_ref=pay.at[: buf.shape[1]],
            dst_ref=buf.at[2 * side + c],
            send_sem=gsend.at[at // 4 + at // 6],
            recv_sem=grecv.at[which],
            device_id={"rng": 2 * place + core},
            device_id_type=MESH,
        )

    solve_kernel(part, solved, stack, turned, hr, hi, xr, xi, yr, yi)
    flipped = solved[...].T
    scaled = []
    for t in range(part.shape[0]):
        scaled.append(flipped[side_chan * t : side_chan * (t + 1)] * counts[t])
    spare = items - len(scaled) * side_chan
    if spare:
        scaled.append(jnp.zeros((spare, lanes), jnp.float32))
    full = jnp.concatenate(scaled, 0)
    lane = lax.broadcasted_iota(jnp.int32, (items, lanes), 1)
    hi_part = full.astype(jnp.bfloat16).astype(jnp.float32)
    rest = full - hi_part
    mid_part = rest.astype(jnp.bfloat16).astype(jnp.float32)
    lo_part = rest - mid_part
    split = jnp.where(
        lane == 2 * dof + 1, mid_part, jnp.where(lane == 2 * dof + 2, lo_part, hi_part)
    )
    pay[...] = split.astype(jnp.bfloat16)
    for which, (places, buf) in enumerate(((ends, gat_e), (middles, gat_l))):
        for side, owner in places:

            @pl.when(z == owner)
            def _(side=side, buf=buf, which=which, owner=owner):
                order = sorted(range(n), key=lambda place: -abs(place - owner))
                peers = [(place, core) for place in order for core in (c, 1 - c)]
                peers.remove((owner, c))
                for at, (place, core) in enumerate(peers):
                    send_copy(at, place, core, side, buf, which).start()
                buf[2 * side + c] = pay[: buf.shape[1]]

    freq = (lax.broadcasted_iota(jnp.int32, (num_chan, taps), 1) // num_sel).astype(jnp.float32)
    centres = chan_ref[...].astype(jnp.float32)

    def tile_copy(side, b, group):
        target = ahead if side else behind
        buf = pl_left if side else pl_right
        return pltpu.make_async_remote_copy(
            src_ref=pw.at[b + 1],
            dst_ref=buf.at[b + 1],
            send_sem=lsend.at[side],
            recv_sem=lrecv.at[side, group],
            device_id={"rng": target},
            device_id_type=MESH,
        )

    def az_copy(up):
        return pltpu.make_async_remote_copy(
            src_ref=pw.at[beams if up else 1],
            dst_ref=pw.at[0 if up else beams + 1],
            send_sem=tsend,
            recv_sem=trecv,
            device_id={"az": az_next if up else az_prev},
            device_id_type=MESH,
        )

    def corner_copy(up, side):
        buf = pl_left if side else pl_right
        return pltpu.make_async_remote_copy(
            src_ref=pw.at[beams if up else 1],
            dst_ref=buf.at[0 if up else beams + 1],
            send_sem=lsend.at[side],
            recv_sem=arecv.at[side],
            device_id={
                "az": az_next if up else az_prev,
                "rng": ahead if side else behind,
            },
            device_id_type=MESH,
        )

    def one_power(b, tiles, t, core, group, edge=None):
        start = pl.multiple_of(t * side_chan, side_chan)
        both = [tiles[2 * side + core, pl.ds(start, side_chan), :] for side in range(2)]
        wide = jnp.concatenate(both, 0)
        tail = wide[:, 2 * BINS * lanes :]
        quiet = tail[:, :1] + tail[:, 1:2] + tail[:, 2:3]
        centre = jnp.sum(jnp.where(blane == az * beams + b, centres, 0.0), 1, keepdims=True)
        hits = []
        for q in range(BINS):
            f = centre + (q - BINS // 2)
            f = jnp.where(f < 0.0, f + pulses, jnp.where(f >= pulses, f - pulses, f))
            hits.append(freq == f)
        planes = []
        for p in range(2):
            plane = jnp.zeros((num_chan, taps), jnp.float32)
            for q in range(BINS):
                at = (p * BINS + q) * lanes
                piece = wide[:, at : at + lanes]
                tiled = jnp.concatenate([piece] * (taps // lanes), 1)
                plane = jnp.where(hits[q], tiled, plane)
            planes.append(plane)
        top = jnp.concatenate([planes[0], planes[1]], 1)
        bottom = jnp.concatenate([-planes[1], planes[0]], 1)
        lhs = jnp.concatenate([top, bottom], 0).astype(jnp.bfloat16)
        flat = v_all[b].reshape(2 * taps, cells)
        proj = jnp.dot(lhs, flat, preferred_element_type=jnp.float32)
        p0 = proj[:num_chan]
        p1 = proj[num_chan:]
        pw[b + 1] = (p0 * p0 + p1 * p1) / quiet
        if edge is not None:
            up, first = edge

            @pl.when(first)
            def _():
                @pl.when(me < size - 1)
                def _():
                    corner_copy(up, 1).start()

                @pl.when(me > 0)
                def _():
                    corner_copy(up, 0).start()

                az_copy(up).start()

        @pl.when(me < size - 1)
        def _():
            tile_copy(1, b, group).start()

        @pl.when(me > 0)
        def _():
            tile_copy(0, b, group).start()

    def spread_weights(which, buf, tiles):
        mine_too = is_mid if which else jnp.logical_not(is_mid)
        others = 2 * len(middles)
        for own in range(2):

            @pl.when(mine_too if own else jnp.logical_not(mine_too))
            def _(own=own):
                all_of(buf.at[pl.ds(0, others - own)], grecv.at[which])

        flat = buf[...].reshape(others * buf.shape[1], lanes)
        wide = jnp.dot(flat, spread_ref[...], preferred_element_type=jnp.float32)
        tiles[...] = wide.reshape(tiles.shape)

    def early_power(t, carry):
        one_power(steps - 1 - t, tiles_e, t, 0, 0)
        one_power(steps + t, tiles_e, t, 1, 0)
        return carry

    def late_power(i, carry):
        one_power(i, tiles_l, late - 1 - i, 0, 1, (0, i == 0))
        one_power(beams - 1 - i, tiles_l, late - 1 - i, 1, 1, (1, i == 0))

        return carry

    spread_weights(0, gat_e, tiles_e)
    lax.fori_loop(0, early, early_power, 0)
    spread_weights(1, gat_l, tiles_l)
    lax.fori_loop(0, late, late_power, 0)

    lane = lax.broadcasted_iota(jnp.int32, (num_chan, cells), 1)

    def row_sum(i):
        mid = pw[i]
        back = pltpu.roll(jnp.where(lane == cells - 1, pl_left[i], mid), 1, 1)
        fore = pltpu.roll(jnp.where(lane == 0, pl_right[i], mid), cells - 1, 1)
        return back + mid + fore

    def finish(which, group):
        @pl.when(me > 0)
        def _():
            all_of(pl_left.at[pl.ds(0, len(group))], lrecv.at[1, which])

        @pl.when(me < size - 1)
        def _():
            all_of(pl_right.at[pl.ds(0, len(group))], lrecv.at[0, which])

        for b in group:
            rows[b + 1] = row_sum(b + 1)

    def smooth(b):
        out_ref[b] = (rows[b] + rows[b + 1] + rows[b + 2]) / 9.0

    def write(first, count):
        part_of = pl.ds(first, count)
        copy = pltpu.make_async_copy(
            out_ref.at[part_of], out_hbm.at[part_of], osem
        )
        copy.start()

    finish(0, range(late, beams - late))
    for b in range(late + 1, beams - late - 1):
        smooth(b)
    write(late + 1, beams - 2 * late - 2)
    outer = [*range(late), *range(beams - late, beams)]
    finish(1, outer)
    for b in range(1, late + 1):
        smooth(b)
        smooth(beams - 1 - b)
    write(1, late)
    write(beams - 1 - late, late)
    all_of(pw.at[pl.ds(0, 2)], trecv)

    @pl.when(me > 0)
    def _():
        all_of(pl_left.at[pl.ds(0, 2)], arecv.at[1])

    @pl.when(me < size - 1)
    def _():
        all_of(pl_right.at[pl.ds(0, 2)], arecv.at[0])

    rows[0] = row_sum(0)
    rows[beams + 1] = row_sum(beams + 1)
    smooth(0)
    smooth(beams - 1)
    write(0, 1)
    write(beams - 1, 1)

    all_of(echoes, hsend)
    all_of(pair, psend)
    mask_copy.wait_send()
    for own, buf, here in (
        (early, gat_e, jnp.logical_not(is_mid)),
        (late, gat_l, is_mid),
    ):

        @pl.when(here)
        def _(own=own, buf=buf):
            for i, ref in enumerate((coded, scale)):
                all_of(ref.at[pl.ds(0, 2 * steps - own)], dsend.at[i])
            all_of(buf, gsend.at[0])
            all_of(buf.at[pl.ds(0, 2)], gsend.at[1])
            all_of(buf.at[0], gsend.at[2])

    all_of(pw.at[pl.ds(0, 2)], tsend)
    for side in range(2):

        @pl.when(me < size - 1 if side else me > 0)
        def _(side=side):
            all_of(pw, lsend.at[side])

    pltpu.make_async_copy(out_ref, out_hbm, osem).wait()


def chain(echoes, arc_start, arc_offsets, doppler_bins, steer_angles, train_mask, early):
    columns, num_pulses, cells = echoes.shape[1:]
    num_sel = arc_offsets.shape[1]
    num_chan = doppler_bins.shape[1]
    size = lax.axis_size("rng")
    beams = BEAMS // lax.axis_size("az")
    dof = BINS * num_sel
    steps = beams // 2
    n = size // 2
    width = ARC // 2
    w = width // steps
    side_chan = num_chan // 2
    half = side_chan * dof
    late = steps - early
    most = max(early, late)
    items = most * side_chan
    early_rows = -(-early * side_chan // 16) * 16
    late_rows = -(-late * side_chan // 16) * 16
    most_rows = max(early_rows, late_rows)
    lanes = 128
    with jax.ensure_compile_time_eval():
        table_re, table_im = doppler_table(num_pulses)
        table = np.block([[table_re, -table_im], [table_im, table_re]])
    source = np.arange(lanes)[:, None]
    target = np.arange((2 * BINS + 1) * lanes)[None, :]
    block, place = target // lanes, target % lanes
    wanted = np.where(
        block < 2 * BINS, block * num_sel + place % num_sel, 2 * dof + np.minimum(place, 3)
    )
    spread = jnp.asarray(source == wanted, jnp.bfloat16)
    vm = pltpu.VMEM
    sm = pltpu.SMEM
    dma = pltpu.SemaphoreType.DMA
    f32 = jnp.float32
    bf16 = jnp.bfloat16
    i32 = jnp.int32
    i16 = jnp.int16
    tile = (num_chan, cells)
    scratch = [
        sm(arc_start.shape, i32),
        sm(arc_offsets.T.shape, i32),
        sm(doppler_bins.T.shape, i32),
        sm(train_mask.T.shape, i32),
        vm(steer_angles.T.shape, f32),
        vm(doppler_bins.T.shape, i32),
        vm(table.shape, bf16),
        vm(spread.shape, bf16),
        vm((2,) + steer_angles.T.shape, f32),
        vm((2, columns + 2 * width, num_pulses, cells), bf16),
        vm((steps, 2, 2, w, num_pulses, cells), bf16),
        vm((beams, 2, num_pulses, num_sel, cells), bf16),
        vm((beams, 2, dof, half), f32),
        vm((steps, 2, dof, half), f32),
        vm((2 * steps, dof, half), i16),
        vm((2 * steps, 1, half + lanes), f32),
        vm((most, n, dof, half), i16),
        vm((most, n, 1, half + lanes), f32),
        vm((most, dof, half), f32),
        vm((lanes, lanes), f32),
        vm((dof, items, dof), f32),
        vm((dof, dof, items), f32),
        vm((dof, dof, items), f32),
        vm((dof, dof, items), f32),
        vm((dof, items), f32),
        vm((dof, items), f32),
        vm((dof, items), f32),
        vm((dof, items), f32),
        vm((2, beams, cells), f32),
        vm((beams, lanes), f32),
        vm((most, 1, lanes), f32),
        vm((most_rows, lanes), bf16),
        vm((4, early_rows, lanes), bf16),
        vm((4, late_rows, lanes), bf16),
        vm((4, early_rows, spread.shape[1]), f32),
        vm((4, late_rows, spread.shape[1]), f32),
        vm((beams + 2,) + tile, f32),
        vm((beams + 2,) + tile, f32),
        vm((beams + 2,) + tile, f32),
        vm((beams + 2,) + tile, f32),
        vm((beams,) + tile, f32),
        dma((9,)),
        dma,
        dma,
        dma((steps,)),
        dma,
        dma((steps,)),
        dma((2,)),
        dma((2, most)),
        dma,
        dma,
        dma((3,)),
        dma((2,)),
        pltpu.SemaphoreType.REGULAR,
        dma((2,)),
        dma((2, 2)),
        dma,
        dma,
        dma((2,)),
    ]
    return pl.pallas_call(
        functools.partial(chain_kernel, early),
        in_specs=[pl.BlockSpec(memory_space=pl.ANY)] * 8,
        out_specs=pl.BlockSpec(memory_space=pl.ANY),
        out_shape=jax.ShapeDtypeStruct((beams,) + tile, f32),
        scratch_shapes=scratch,
        compiler_params=pltpu.CompilerParams(
            collective_id=2, has_side_effects=True, vmem_limit_bytes=CHAIN_VMEM
        ),
        name="chain",
    )(
        arc_start,
        arc_offsets.T,
        doppler_bins.T,
        train_mask.T,
        steer_angles.T,
        echoes,
        jnp.asarray(table),
        spread,
    )


def body(echoes, arc_start, arc_offsets, doppler_bins, steer_angles, train_mask):
    columns = echoes.shape[1]
    num_pulses = echoes.shape[2]
    cells = echoes.shape[3]
    num_sel = arc_offsets.shape[1]
    chan_count = doppler_bins.shape[1]
    cycle_size = lax.axis_size("az")
    cycle_pos = lax.axis_index("az")
    rng_size = lax.axis_size("rng")
    beam_count = BEAMS // cycle_size
    item_count = beam_count * chan_count
    dof = BINS * num_sel
    pairs = beam_count // 2
    if (
        columns == ARC
        and beam_count % 2 == 0
        and pairs * (COLS // BEAMS) == ARC // 2
        and rng_size == 8
        and cycle_size > 2
        and cells == 128
        and chan_count % 16 == 0
        and chan_count // 2 * dof % 128 == 0
        and 2 * dof + 8 <= 128
        and dof % 16 == 0
        and pairs * (chan_count // 2) <= 128
        and pairs > LATE
        and rng_size // 2 > 3
    ):
        return chain(
            echoes, arc_start, arc_offsets, doppler_bins, steer_angles, train_mask, pairs - LATE
        )
    table_re, table_im = doppler_table(num_pulses)
    table = jnp.concatenate(
        [jnp.concatenate([table_re, -table_im], 1), jnp.concatenate([table_im, table_re], 1)], 0
    )

    def own(x):
        return lax.dynamic_slice_in_dim(x, cycle_pos * beam_count, beam_count, axis=0)

    arc_first = (own(arc_start) - cycle_pos * columns + ARC // 2) % COLS
    col_index = arc_first[:, None] + own(arc_offsets)
    bins_own = own(doppler_bins)
    angles = own(steer_angles)
    block_count = train_mask.shape[1]
    cell_mask = (
        jnp.broadcast_to(train_mask[:, :, None], (beam_count, block_count, BLK))
        .reshape(beam_count, 1, block_count * BLK)
        .astype(jnp.bfloat16)
    )
    smem = pl.BlockSpec(memory_space=pltpu.SMEM)

    def snap_gram(extended, first, last, base):
        share = last - first
        ext_cols = extended.shape[1]
        return pl.pallas_call(
            snap_gram_kernel,
            grid=(share,),
            in_specs=[
                smem,
                smem,
                smem,
                smem,
                pl.BlockSpec((2, ext_cols, num_pulses, cells), lambda b: (0, 0, 0, 0)),
                pl.BlockSpec(table.shape, lambda b: (0, 0)),
                pl.BlockSpec((1, 1, cells), lambda b: (b, 0, 0)),
            ],
            out_specs=[
                pl.BlockSpec((1, 2, num_pulses, num_sel, cells), lambda b: (b, 0, 0, 0, 0)),
                pl.BlockSpec((1, dof, chan_count * dof), lambda b: (b, 0, 0)),
            ],
            out_shape=[
                jax.ShapeDtypeStruct((share, 2, num_pulses, num_sel, cells), jnp.bfloat16),
                jax.ShapeDtypeStruct((share, dof, chan_count * dof), jnp.float32),
            ],
            compiler_params=pltpu.CompilerParams(vmem_limit_bytes=VMEM_LIMIT),
            cost_estimate=pl.CostEstimate(
                flops=share * 600_000_000, bytes_accessed=share * 1_500_000, transcendentals=0
            ),
            name="snap_gram",
        )(
            col_index[first:last] - base,
            bins_own[first:last],
            jnp.cos(angles)[first:last],
            jnp.sin(angles)[first:last],
            extended,
            table,
            cell_mask[first:last],
        )

    width = ARC // 2
    forward = [(i, (i + 1) % cycle_size) for i in range(cycle_size)]
    backward = [(target, source) for source, target in forward]
    low = lax.ppermute(echoes[:, columns - width :], "az", forward)
    high = lax.ppermute(echoes[:, :width], "az", backward)
    step = COLS // BEAMS
    half = beam_count // 2
    if (half - 1) * step + step - 1 + ARC - 1 < width + columns and half * step >= width:
        v_lo, gram_lo = snap_gram(jnp.concatenate([low, echoes], 1), 0, half, 0)
        high, v_lo, gram_lo = lax.optimization_barrier((high, v_lo, gram_lo))
        v_hi, gram_hi = snap_gram(jnp.concatenate([echoes, high], 1), half, beam_count, width)
        v_parts = (v_lo, v_hi)
        grams = (gram_lo, gram_hi)
        if rng_size % 4 or item_count // rng_size < chan_count:
            grams = (jnp.concatenate(grams, 0),)
    else:
        v_one, gram_one = snap_gram(jnp.concatenate([low, echoes, high], 1), 0, beam_count, 0)
        v_parts = (v_one,)
        grams = (gram_one,)

    per = item_count // rng_size
    if per < chan_count:
        split = chan_count // per
        gram = grams[0].reshape(beam_count, dof, split, per * dof)
        grams = (jnp.swapaxes(gram, 1, 2).reshape(beam_count * split, dof, per * dof),)
        width = per
    else:
        width = chan_count
    vm = pltpu.VMEM
    dma = pltpu.SemaphoreType.DMA
    line = rng_size // 2
    chunk = (grams[0].shape[0] * len(grams) // rng_size, dof, grams[0].shape[2])
    part = pl.pallas_call(
        functools.partial(scatter_kernel, line, len(grams)),
        in_specs=[pl.BlockSpec(memory_space=vm)] * len(grams),
        out_specs=pl.BlockSpec(memory_space=vm),
        out_shape=jax.ShapeDtypeStruct(chunk, jnp.float32),
        scratch_shapes=[vm((line,) + chunk, jnp.float32)] * 4 + [dma((line,))] * 6,
        compiler_params=pltpu.CompilerParams(
            collective_id=0, has_side_effects=True, vmem_limit_bytes=VMEM_LIMIT
        ),
        name="scatter",
    )(*[g.reshape((rng_size // len(grams),) + chunk) for g in grams])
    solved = pl.pallas_call(
        solve_kernel,
        out_shape=jax.ShapeDtypeStruct((2 * dof + 8, per), jnp.float32),
        scratch_shapes=[
            vm((dof, per, dof), jnp.float32),
            vm((dof, dof, per), jnp.float32),
            vm((dof, dof, per), jnp.float32),
            vm((dof, dof, per), jnp.float32),
            vm((dof, per), jnp.float32),
            vm((dof, per), jnp.float32),
            vm((dof, per), jnp.float32),
            vm((dof, per), jnp.float32),
        ],
        compiler_params=pltpu.CompilerParams(vmem_limit_bytes=VMEM_LIMIT),
        name="solve",
    )(part)
    lanes = 128
    local_count = (BLK * jnp.sum(train_mask, axis=1)).astype(jnp.float32)
    pad_rows = -per % 8
    payload = jnp.concatenate(
        [
            jnp.pad(solved.T, ((0, pad_rows), (0, lanes - solved.shape[0]))),
            jnp.broadcast_to(local_count[:, None], (beam_count, lanes)),
        ],
        0,
    )
    halves = len(v_parts)
    any_spec = pl.BlockSpec(memory_space=pl.ANY)
    block = (chan_count, cells)
    out = pl.pallas_call(
        functools.partial(apply_kernel, halves, per, dof),
        in_specs=[pl.BlockSpec(memory_space=vm)] * 2 + [any_spec] * halves,
        out_specs=pl.BlockSpec(memory_space=vm),
        out_shape=jax.ShapeDtypeStruct((beam_count,) + block, jnp.float32),
        scratch_shapes=[
            vm((beam_count, 2, num_pulses, num_sel, cells), jnp.bfloat16),
            vm((rng_size,) + payload.shape, jnp.float32),
            vm((beam_count,) + block, jnp.float32),
            vm((2, 8, item_count), jnp.float32),
            vm((2, 8, item_count), jnp.float32),
            vm((beam_count,) + block, jnp.float32),
            vm(block, jnp.float32),
            vm(block, jnp.float32),
            dma((halves,)),
            dma((rng_size,)),
            dma((rng_size,)),
            dma((2,)),
            dma((2,)),
            dma((2,)),
            dma((2,)),
        ],
        compiler_params=pltpu.CompilerParams(
            collective_id=1, has_side_effects=True, vmem_limit_bytes=VMEM_LIMIT
        ),
        name="apply",
    )(payload, bins_own[:, :, None], *v_parts)
    return out


def solution(mesh):
    return jax.shard_map(
        body,
        mesh=mesh,
        in_specs=(P(None, "az", None, "rng"), P(), P(), P(), P(), P("az", "rng")),
        out_specs=P("az", None, "rng"),
        check_vma=False,
    )
```

```python
import functools

import jax
import numpy as np
import jax.numpy as jnp
from jax import lax
from jax.experimental import pallas as pl
from jax.experimental.pallas import tpu as pltpu
from jax.sharding import PartitionSpec as P


COLS = 256
ARC = 64
BINS = 3
BEAMS = 64
BLK = 128
LOADING = 0.1
VMEM_LIMIT = 48 << 20
CHAIN_VMEM = 66_200_000
CODE_TOP = 32000.0
LAG = 3
LATE = 4


def doppler_table(num_pulses):
    freq_ids = jnp.arange(num_pulses, dtype=jnp.int32)
    phase_steps = freq_ids[:, None] * freq_ids[None, :] % num_pulses
    phase_angle = -2.0 * jnp.pi / num_pulses * phase_steps.astype(jnp.float32)
    return (jnp.cos(phase_angle).astype(jnp.bfloat16), jnp.sin(phase_angle).astype(jnp.bfloat16))


def snap_gram_kernel(
    col_ref, bins_ref, cos_ref, sin_ref, ext_ref, table_ref, mask_ref, v_ref, gram_ref
):
    beam = pl.program_id(0)
    pulses = ext_ref.shape[2]
    num_sel = col_ref.shape[1]
    num_chan = bins_ref.shape[1]
    table = table_ref[...]
    parts_re, parts_im = [], []
    for j in range(num_sel):
        col = col_ref[beam, j]
        data = jnp.concatenate([ext_ref[0, col], ext_ref[1, col]], axis=0)
        spec = jnp.dot(table, data, preferred_element_type=jnp.float32)
        cosine = cos_ref[beam, j]
        sine = sin_ref[beam, j]
        spec_re = spec[:pulses]
        spec_im = spec[pulses:]
        parts_re.append(cosine * spec_re - sine * spec_im)
        parts_im.append(sine * spec_re + cosine * spec_im)
    for part, pieces in enumerate((parts_re, parts_im)):
        stacked = jnp.swapaxes(jnp.stack(pieces, 0), 0, 1)
        v_ref[0, part] = stacked.astype(jnp.bfloat16)
    dof = BINS * num_sel
    mask_row = mask_ref[0]
    row = lax.broadcasted_iota(jnp.int32, (dof, dof), 0)
    colm = lax.broadcasted_iota(jnp.int32, (dof, dof), 1)
    lower = row >= colm
    packed = []
    for k in range(num_chan):
        centre = bins_ref[beam, k]
        ids = [(centre + (q - BINS // 2 + pulses)) % pulses for q in range(BINS)]
        u_re = jnp.concatenate([v_ref[0, 0, f] for f in ids], 0)
        u_im = jnp.concatenate([v_ref[0, 1, f] for f in ids], 0)
        right = jnp.concatenate([u_re, u_im], 1)
        m_re = u_re * mask_row
        m_im = u_im * mask_row
        left = jnp.concatenate(
            [jnp.concatenate([m_re, m_im], 1), jnp.concatenate([m_im, -m_re], 1)], 0
        )
        both = lax.dot_general(
            left, right, (((1,), (1,)), ((), ())), preferred_element_type=jnp.float32
        )
        packed.append(jnp.where(lower, both[:dof], both[dof:]))
    gram_ref[0] = jnp.concatenate(packed, 1)


def solve_kernel(part_ref, out_ref, stack, turned, hr, hi, xr, xi, yr, yi):
    lead, dof, wide = part_ref.shape
    width = wide // dof
    lanes = lead * width
    nb = dof // 8
    group = min(8, lanes)
    for g in range(0, lanes, group):
        pieces = []
        for item in range(g, g + group):
            k = item % width
            pieces.append(part_ref[item // width, :, k * dof : (k + 1) * dof])
        stack[:, g : g + group, :] = jnp.swapaxes(jnp.stack(pieces, 0), 0, 1)
    for i in range(dof):
        turned[i] = stack[i].T
    trace = jnp.zeros((1, lanes), jnp.float32)
    for i in range(dof):
        trace = trace + turned[i, i : i + 1, :]
    load = (LOADING / dof) * trace
    cube = (8, 8, lanes)
    row = lax.broadcasted_iota(jnp.int32, cube, 0)
    col = lax.broadcasted_iota(jnp.int32, cube, 1)
    for ib in range(nb):
        rows = slice(8 * ib, 8 * ib + 8)
        for jb in range(ib, nb):
            cols = slice(8 * jb, 8 * jb + 8)
            imag = turned[rows, cols, :]
            real = jnp.swapaxes(turned[cols, rows, :], 0, 1)
            if ib == jb:
                straight, flip = imag, real
                real = jnp.where(row >= col, straight, flip)
                real = jnp.where(row == col, real + load[None], real)
                imag = jnp.where(row < col, straight, jnp.where(row > col, -flip, 0.0))
            hr[rows, cols, :] = real
            hi[rows, cols, :] = imag
    yr[...] = jnp.ones_like(yr)
    yi[...] = jnp.zeros_like(yi)
    xr[...] = jnp.zeros_like(xr)
    xi[...] = jnp.zeros_like(xi)
    sub = lax.broadcasted_iota(jnp.int32, (8, lanes), 0)

    for kb in range(nb):

        def step(k, carry, kb=kb, first=0):
            pivot = 1.0 / hr[k, pl.ds(k, 1), :]
            rr = [hr[k, 8 * b : 8 * b + 8, :] for b in range(kb, nb)]
            ri = [hi[k, 8 * b : 8 * b + 8, :] for b in range(kb, nb)]
            rs = [x + y for x, y in zip(rr, ri, strict=True)]
            gr = jnp.broadcast_to(yr[pl.ds(k, 1), :], (8, lanes))
            gi = jnp.broadcast_to(yi[pl.ds(k, 1), :], (8, lanes))
            for ib in range(kb, nb):
                fr = rr[ib - kb] * pivot
                fi = -ri[ib - kb] * pivot
                if ib == kb:
                    live = sub + 8 * kb > k
                    fr = jnp.where(live, fr, 0.0)
                    fi = jnp.where(live, fi, 0.0)
                fs = fr + fi
                fd = fi - fr
                own = slice(8 * ib, 8 * ib + 8)
                yr[own, :] = yr[own, :] - (fr * gr - fi * gi)
                yi[own, :] = yi[own, :] - (fr * gi + fi * gr)
                for s in range(first + 1 if ib == kb else 0, 8):
                    i = 8 * ib + s
                    cr = jnp.broadcast_to(fr[s : s + 1], (8, lanes))
                    cs = jnp.broadcast_to(fs[s : s + 1], (8, lanes))
                    cd = jnp.broadcast_to(fd[s : s + 1], (8, lanes))
                    for b in range(ib, nb):
                        pr, pi = rr[b - kb], ri[b - kb]
                        sl = slice(8 * b, 8 * b + 8)
                        both = cr * rs[b - kb]
                        hr[i, sl, :] = (hr[i, sl, :] - both) + cs * pi
                        hi[i, sl, :] = (hi[i, sl, :] - both) - cd * pr
            return carry

        for first in range(8):
            step(8 * kb + first, 0, first=first)

    for ib in reversed(range(nb)):

        def back(t, carry, ib=ib):
            i = 8 * ib + 7 - t
            sr = jnp.zeros((8, lanes), jnp.float32)
            si = jnp.zeros((8, lanes), jnp.float32)
            for b in range(ib, nb):
                sl = slice(8 * b, 8 * b + 8)
                ar, ai = hr[i, sl, :], hi[i, sl, :]
                br, bi = xr[sl, :], xi[sl, :]
                sr = sr + (ar * br - ai * bi)
                si = si + (ar * bi + ai * br)
            pivot = 1.0 / hr[i, pl.ds(i, 1), :]
            top_r = yr[pl.ds(i, 1), :]
            top_i = yi[pl.ds(i, 1), :]
            xr[pl.ds(i, 1), :] = (top_r - jnp.sum(sr, 0, keepdims=True)) * pivot
            xi[pl.ds(i, 1), :] = (top_i - jnp.sum(si, 0, keepdims=True)) * pivot
            return carry

        lax.fori_loop(0, 8, back, 0)
    out_ref[:dof, :lanes] = xr[...]
    out_ref[dof : 2 * dof, :lanes] = xi[...]
    out_ref[2 * dof : 2 * dof + 8, :lanes] = jnp.broadcast_to(
        jnp.sum(xr[...], 0, keepdims=True), (8, lanes)
    )


MESH = pl.DeviceIdType.MESH


def scatter_kernel(n, halves, *refs):
    g_refs = refs[:halves]
    out_ref, pair, acc, right, left, psend, precv, rsend, rrecv, lsend, lrecv = refs[halves:]
    share = n // halves

    def own(t, core):
        return g_refs[t // share].at[2 * (t % share) + core]

    me = lax.axis_index("rng")
    z = me // 2
    c = me % 2
    mate = 2 * z + 1 - c
    ahead = lax.rem(me + 2, 2 * n)
    behind = lax.rem(me + 2 * n - 2, 2 * n)
    barrier = pltpu.get_barrier_semaphore()
    pl.semaphore_signal(barrier, inc=1, device_id={"rng": mate}, device_id_type=MESH)
    pl.semaphore_signal(barrier, inc=1, device_id={"rng": ahead}, device_id_type=MESH)
    pl.semaphore_signal(barrier, inc=1, device_id={"rng": behind}, device_id_type=MESH)
    pl.semaphore_wait(barrier, 3)

    order = []
    for t in range((n + 1) // 2):
        order.append(n - 1 - t)
        if t != n - 1 - t:
            order.append(t)

    def pair_copy(t):
        return pltpu.make_async_remote_copy(
            src_ref=own(t, 1 - c),
            dst_ref=pair.at[t],
            send_sem=psend.at[t],
            recv_sem=precv.at[t],
            device_id={"rng": mate},
            device_id_type=MESH,
        )

    def right_copy(t):
        return pltpu.make_async_remote_copy(
            src_ref=acc.at[t],
            dst_ref=right.at[t],
            send_sem=rsend.at[t],
            recv_sem=rrecv.at[t],
            device_id={"rng": ahead},
            device_id_type=MESH,
        )

    def left_copy(t):
        return pltpu.make_async_remote_copy(
            src_ref=acc.at[t],
            dst_ref=left.at[t],
            send_sem=lsend.at[t],
            recv_sem=lrecv.at[t],
            device_id={"rng": behind},
            device_id_type=MESH,
        )

    for t in order:
        pair_copy(t).start()
    for t in order:
        pair_copy(t).wait_recv()
        acc[t] = own(t, c)[...] + pair[t]

        @pl.when(jnp.logical_and(z == 0, t > 0))
        def _(t=t):
            right_copy(t).start()

        @pl.when(jnp.logical_and(z == n - 1, t < n - 1))
        def _(t=t):
            left_copy(t).start()

    for place in range(n):
        events = [(place + n - 1 - t, 0, t) for t in range(place + 1, n) if place > 0]
        events += [(n - 1 - place + t, 1, t) for t in range(place) if place < n - 1]

        @pl.when(z == place)
        def _(place=place, events=sorted(events)):
            for _, side, t in events:
                copy = left_copy(t) if side else right_copy(t)
                source = left if side else right
                copy.wait_recv()
                acc[t] = acc[t] + source[t]
                copy.start()
            total = acc[place]
            if place > 0:
                right_copy(place).wait_recv()
                total = total + right[place]
            if place < n - 1:
                left_copy(place).wait_recv()
                total = total + left[place]
            out_ref[...] = total

    for t in range(n):
        pair_copy(t).wait_send()

        @pl.when(z < t)
        def _(t=t):
            right_copy(t).wait_send()

        @pl.when(z > t)
        def _(t=t):
            left_copy(t).wait_send()


def apply_kernel(
    halves,
    per,
    dof,
    pay_ref,
    bins_ref,
    *refs,
):
    v_refs = refs[:halves]
    (out_ref, v_all, gat, power, edge, halo, sums, az_lo, az_hi) = refs[halves : halves + 9]
    (vsem, gsend, grecv, esend, erecv, asend, arecv) = refs[halves + 9 :]
    me = lax.axis_index("rng")
    az = lax.axis_index("az")
    n = lax.axis_size("rng")
    m = lax.axis_size("az")
    beams, num_chan, cells = out_ref.shape
    pulses, num_sel = v_all.shape[2], v_all.shape[3]
    taps = pulses * num_sel
    az_next = lax.rem(az + 1, m)
    az_prev = lax.rem(az + m - 1, m)
    barrier = pltpu.get_barrier_semaphore()
    for d in range(1, n):
        peer = lax.rem(me + d, n)
        pl.semaphore_signal(barrier, inc=1, device_id={"rng": peer}, device_id_type=MESH)
    for other in (az_next, az_prev):
        pl.semaphore_signal(barrier, inc=1, device_id={"az": other}, device_id_type=MESH)
    share = beams // halves
    loads = []
    for h in range(halves):
        load = pltpu.make_async_copy(v_refs[h], v_all.at[pl.ds(h * share, share)], vsem.at[h])
        load.start()
        loads.append(load)
    pl.semaphore_wait(barrier, n + 1)

    copies = []
    for d in range(1, n):
        peer = lax.rem(me + d, n)
        copy = pltpu.make_async_remote_copy(
            src_ref=pay_ref,
            dst_ref=gat.at[me],
            send_sem=gsend.at[d],
            recv_sem=grecv.at[d],
            device_id={"rng": peer},
            device_id_type=MESH,
        )
        copy.start()
        copies.append(copy)
    gat[me] = pay_ref[...]
    for load in loads:
        load.wait()
    for copy in copies:
        copy.wait_recv()
    rows = gat.shape[1] - beams
    count = jnp.zeros((beams, gat.shape[2]), jnp.float32)
    for r in range(n):
        count = count + gat[r, rows:, :]
    sums[0] = jnp.zeros(sums.shape[1:], jnp.float32)
    for b in range(beams):
        sums[b, :1, :] = count[b : b + 1]
    freq = lax.broadcasted_iota(jnp.int32, (num_chan, taps), 1) // num_sel
    lanes = gat.shape[2]
    lane = lax.broadcasted_iota(jnp.int32, (num_chan, lanes), 1)

    def one(b, carry):
        if per >= num_chan:
            ratio = per // num_chan
            start = pl.multiple_of((b % ratio) * num_chan, 8)
            w = gat[b // ratio, pl.ds(start, num_chan), :]
        else:
            split = num_chan // per
            w = jnp.concatenate([gat[b * split + t, :per, :] for t in range(split)], 0)
        w = w * sums[b, :1, :]
        quiet = w[:, 2 * dof : 2 * dof + 1]
        centre = bins_ref[b]
        planes = []
        hits = []
        for q in range(BINS):
            f = lax.rem(centre + (q - BINS // 2 + pulses), pulses)
            hits.append(freq == f)
        for part in range(2):
            plane = jnp.zeros((num_chan, taps), jnp.float32)
            for q in range(BINS):
                start = part * dof + q * num_sel
                piece = pltpu.roll(w, (lanes - start) % lanes, 1) if start else w
                piece = jnp.where(lane < num_sel, piece, 0.0)
                span = num_sel
                while span < lanes:
                    piece = piece + pltpu.roll(piece, span, 1)
                    span *= 2
                tiled = jnp.concatenate([piece] * (taps // lanes), 1)
                plane = jnp.where(hits[q], tiled, plane)
            planes.append(plane)
        top = jnp.concatenate([planes[0], planes[1]], 1)
        low = jnp.concatenate([-planes[1], planes[0]], 1)
        lhs = jnp.concatenate([top, low], 0).astype(jnp.bfloat16)
        flat = v_all[b].reshape(2 * taps, cells)
        proj = jnp.dot(lhs, flat, preferred_element_type=jnp.float32)
        p0 = proj[:num_chan]
        p1 = proj[num_chan:]
        power[b] = (p0 * p0 + p1 * p1) / quiet
        return carry

    lax.fori_loop(0, beams, one, 0)
    items = beams * num_chan
    turned = power[...].reshape(items, cells).T
    edge[0] = turned[:8]
    edge[1] = turned[cells - 8 :]

    def edge_copy(side):
        target = lax.rem(me + 1, n) if side else lax.rem(me + n - 1, n)
        return pltpu.make_async_remote_copy(
            src_ref=edge.at[side],
            dst_ref=halo.at[side],
            send_sem=esend.at[side],
            recv_sem=erecv.at[side],
            device_id={"rng": target},
            device_id_type=MESH,
        )

    for side in range(2):
        edge_copy(side).start()
    for side in range(2):
        edge_copy(side).wait()
    before = jnp.where(me > 0, halo[1, 7:8], 0.0)
    after = jnp.where(me < n - 1, halo[0, 0:1], 0.0)
    turned = (
        jnp.concatenate([before, turned[:-1]], 0)
        + turned
        + jnp.concatenate([turned[1:], after], 0)
    )
    sums[...] = turned.T.reshape(beams, num_chan, cells)
    up = pltpu.make_async_remote_copy(
        src_ref=sums.at[beams - 1],
        dst_ref=az_lo,
        send_sem=asend.at[0],
        recv_sem=arecv.at[0],
        device_id={"az": az_next},
        device_id_type=MESH,
    )
    down = pltpu.make_async_remote_copy(
        src_ref=sums.at[0],
        dst_ref=az_hi,
        send_sem=asend.at[1],
        recv_sem=arecv.at[1],
        device_id={"az": az_prev},
        device_id_type=MESH,
    )
    up.start()
    down.start()
    for b in range(1, beams - 1):
        out_ref[b] = (sums[b - 1] + sums[b] + sums[b + 1]) / 9.0
    up.wait_recv()
    down.wait_recv()
    out_ref[0] = (az_lo[...] + sums[0] + sums[1]) / 9.0
    out_ref[beams - 1] = (sums[beams - 2] + sums[beams - 1] + az_hi[...]) / 9.0
    up.wait_send()
    down.wait_send()
    for copy in copies:
        copy.wait_send()


def gram_of(v_ref, beam, bins, mask_row):
    pulses = v_ref.shape[2]
    num_sel = v_ref.shape[3]
    dof = BINS * num_sel
    row = lax.broadcasted_iota(jnp.int32, (dof, dof), 0)
    colm = lax.broadcasted_iota(jnp.int32, (dof, dof), 1)
    lower = row >= colm
    packed = []
    for centre in bins:
        ids = [lax.rem(centre + (q - BINS // 2 + pulses), pulses) for q in range(BINS)]
        u_re = jnp.concatenate([v_ref[beam, 0, f] for f in ids], 0)
        u_im = jnp.concatenate([v_ref[beam, 1, f] for f in ids], 0)
        right = jnp.concatenate([u_re, u_im], 1)
        m_re = u_re * mask_row
        m_im = u_im * mask_row
        left = jnp.concatenate(
            [jnp.concatenate([m_re, m_im], 1), jnp.concatenate([m_im, -m_re], 1)], 0
        )
        both = lax.dot_general(
            left, right, (((1,), (1,)), ((), ())), preferred_element_type=jnp.float32
        )
        packed.append(jnp.where(lower, both[:dof], both[dof:]))
    return packed


def chain_kernel(
    early,
    start_hbm,
    offs_hbm,
    bins_hbm,
    train_hbm,
    angle_hbm,
    echoes,
    table_hbm,
    spread_hbm,
    out_hbm,
    start_ref,
    offs_ref,
    bins_ref,
    train_ref,
    angle_ref,
    chan_ref,
    table_ref,
    spread_ref,
    turn,
    ext,
    halo,
    v_all,
    gram,
    pair,
    coded,
    scale,
    code_in,
    scale_in,
    part,
    solved,
    stack,
    turned,
    hr,
    hi,
    xr,
    xi,
    yr,
    yi,
    masks,
    totals,
    counts,
    pay,
    gat_e,
    gat_l,
    tiles_e,
    tiles_l,
    pw,
    pl_left,
    pl_right,
    rows,
    out_ref,
    esem,
    osem,
    hsend,
    hrecv,
    psend,
    precv,
    dsend,
    drecv,
    msend,
    mrecv,
    gsend,
    grecv,
    hello,
    lsend,
    lrecv,
    tsend,
    trecv,
    arecv,
):
    me = lax.axis_index("rng")
    az = lax.axis_index("az")
    size = lax.axis_size("rng")
    m = lax.axis_size("az")
    n = size // 2
    z = me // 2
    c = lax.rem(me, 2)
    beams, num_chan, cells = out_hbm.shape
    columns = echoes.shape[1]
    pulses = echoes.shape[2]
    num_sel = offs_ref.shape[0]
    blocks = train_ref.shape[0]
    dof = BINS * num_sel
    taps = pulses * num_sel
    steps = beams // 2
    width = ARC // 2
    w = width // steps
    side_chan = num_chan // 2
    half = side_chan * dof
    lanes = pay.shape[1]
    az_next = lax.rem(az + 1, m)
    az_prev = lax.rem(az + m - 1, m)
    ahead = lax.rem(me + 1, size)
    behind = lax.rem(me + size - 1, size)
    mate = 2 * z + 1 - c
    mid_l = n // 2 - 1
    mid_r = n // 2
    late = steps - early
    middles = ((0, mid_l), (1, mid_r))
    ends = ((0, 0), (1, n - 1))
    is_mid = jnp.logical_or(z == mid_l, z == mid_r)

    loads = [
        pltpu.make_async_copy(src, dst, esem.at[i])
        for i, (src, dst) in enumerate(
            (
                (start_hbm, start_ref),
                (offs_hbm, offs_ref),
                (bins_hbm, bins_ref),
                (train_hbm, train_ref),
                (angle_hbm, angle_ref),
                (bins_hbm, chan_ref),
                (table_hbm, table_ref),
                (spread_hbm, spread_ref),
                (echoes, ext.at[:, width : width + columns]),
            )
        )
    ]
    barrier = pltpu.get_barrier_semaphore()
    for other in (az_next, az_prev):
        pl.semaphore_signal(barrier, inc=1, device_id={"az": other}, device_id_type=MESH)
    pl.semaphore_signal(barrier, inc=1, device_id={"rng": mate}, device_id_type=MESH)
    for place in range(n):
        near = jnp.logical_or(is_mid, place in (mid_l, mid_r))

        @pl.when(jnp.logical_and(z != place, near))
        def _(place=place):
            pl.semaphore_signal(
                barrier, inc=1, device_id={"rng": 2 * place + c}, device_id_type=MESH
            )

    for load in loads:
        load.start()
    pl_left[...] = jnp.zeros(pl_left.shape, jnp.float32)
    pl_right[...] = jnp.zeros(pl_right.shape, jnp.float32)
    solved[...] = jnp.zeros(solved.shape, jnp.float32)
    part[...] = jnp.zeros(part.shape, jnp.float32)
    counts[...] = jnp.zeros(counts.shape, jnp.float32)
    pl.semaphore_wait(barrier, 3 + jnp.where(is_mid, n - 1, 2))

    def all_of(ref, sem):
        pltpu.make_async_copy(ref, ref, sem).wait()

    def low_copy(i):
        return pltpu.make_async_remote_copy(
            src_ref=echoes.at[:, pl.ds(columns - w * (i + 1), w)],
            dst_ref=halo.at[i, 0],
            send_sem=hsend,
            recv_sem=hrecv.at[i],
            device_id={"az": az_next},
            device_id_type=MESH,
        )

    def high_copy(i):
        some = w - 1 if i == steps - 1 else w
        return pltpu.make_async_remote_copy(
            src_ref=echoes.at[:, pl.ds(w * i, some)],
            dst_ref=halo.at[i, 1, :, pl.ds(0, some)],
            send_sem=hsend,
            recv_sem=hrecv.at[i],
            device_id={"az": az_prev},
            device_id_type=MESH,
        )

    for i in range(steps):
        low_copy(i).start()
        high_copy(i).start()
    for side, middle in middles:

        @pl.when(z == middle)
        def _(side=side):
            end = 2 * (n - 1 if side else 0) + c
            pl.semaphore_signal(hello, inc=1, device_id={"rng": end}, device_id_type=MESH)

    for load in loads:
        load.wait()

    cell = lax.broadcasted_iota(jnp.int32, (1, cells), 1) // BLK
    for b in range(beams):
        row = jnp.zeros((1, cells), jnp.float32)
        for blk in range(blocks):
            row = jnp.where(cell == blk, train_ref[blk, b].astype(jnp.float32), row)
        masks[0, b : b + 1, :] = row

    mask_copy = pltpu.make_async_remote_copy(
        src_ref=masks.at[0],
        dst_ref=masks.at[1],
        send_sem=msend,
        recv_sem=mrecv,
        device_id={"rng": mate},
        device_id_type=MESH,
    )
    mask_copy.start()
    turn[0] = jnp.cos(angle_ref[...])
    turn[1] = jnp.sin(angle_ref[...])
    mask_copy.wait_recv()
    totals[...] = jnp.broadcast_to(
        jnp.sum(masks[0] + masks[1], 1, keepdims=True), totals.shape
    )

    def mine(t):
        return jnp.where(c == 0, steps - 1 - t, steps + t)

    def theirs(t):
        return jnp.where(c == 0, steps + t, steps - 1 - t)

    def owner_of(side, t):
        return jnp.where(t < early, side * (n - 1), mid_l + side)

    def row_of(t):
        return jnp.where(t < early, t, t - early)

    def pair_copy(t):
        return pltpu.make_async_remote_copy(
            src_ref=gram.at[theirs(t)],
            dst_ref=pair.at[t],
            send_sem=psend,
            recv_sem=precv.at[t],
            device_id={"rng": mate},
            device_id_type=MESH,
        )

    def code_copies(side, t, source):
        owner = 2 * owner_of(side, t) + c
        return [
            pltpu.make_async_remote_copy(
                src_ref=src.at[2 * t + side],
                dst_ref=dst.at[row_of(t), source],
                send_sem=dsend.at[i],
                recv_sem=drecv.at[i, row_of(t)],
                device_id={"rng": owner},
                device_id_type=MESH,
            )
            for i, (src, dst) in enumerate(((coded, code_in), (scale, scale_in)))
        ]

    table = table_ref[...]
    blane = lax.broadcasted_iota(jnp.int32, angle_ref.shape, 1)

    def one_beam(b):
        bg = az * beams + b
        first = lax.rem(start_ref[bg] - az * columns + (width + COLS), COLS)
        first = jnp.minimum(first, ext.shape[1] - ARC - 1)
        here = blane == bg
        cosine = jnp.sum(jnp.where(here, turn[0], 0.0), 1, keepdims=True)
        sine = jnp.sum(jnp.where(here, turn[1], 0.0), 1, keepdims=True)
        cosine = jnp.broadcast_to(cosine, (num_sel, cells))[None]
        sine = jnp.broadcast_to(sine, (num_sel, cells))[None]
        parts_re, parts_im = [], []
        for j in range(num_sel):
            col = first + offs_ref[j, bg]
            data = jnp.concatenate([ext[0, col], ext[1, col]], axis=0)
            spec = jnp.dot(table, data, preferred_element_type=jnp.float32)
            parts_re.append(spec[:pulses])
            parts_im.append(spec[pulses:])
        spec_re = jnp.swapaxes(jnp.stack(parts_re, 0), 0, 1)
        spec_im = jnp.swapaxes(jnp.stack(parts_im, 0), 0, 1)
        v_all[b, 0] = (cosine * spec_re - sine * spec_im).astype(jnp.bfloat16)
        v_all[b, 1] = (sine * spec_re + cosine * spec_im).astype(jnp.bfloat16)
        mask_row = masks[0, pl.ds(b, 1), :].astype(jnp.bfloat16)
        bins = [bins_ref[k, bg] for k in range(num_chan)]
        packed = gram_of(v_all, b, bins, mask_row)
        gram[b, 0] = jnp.concatenate(packed[:side_chan], 1)
        gram[b, 1] = jnp.concatenate(packed[side_chan:], 1)

    def slot(s, carry):
        t = s - 1

        @pl.when(jnp.logical_and(t >= 0, t < steps))
        def _():
            pair_copy(t).wait_recv()
            own = mine(t)
            number = totals[pl.ds(own, 1), :]
            row = row_of(t)
            for side in range(2):
                total = gram[own, side] + pair[t, side]
                owner = owner_of(side, t)

                @pl.when(z == owner)
                def _(total=total):
                    part[row] = total
                    counts[row] = number

                @pl.when(z != owner)
                def _(side=side, total=total):
                    top = jnp.max(jnp.abs(total), 0, keepdims=True)
                    top = jnp.maximum(top, 1e-30)
                    code = jnp.round(total * (CODE_TOP / top))
                    coded[2 * t + side] = code.astype(jnp.int32).astype(jnp.int16)
                    scale[2 * t + side, :, :half] = top * (1.0 / CODE_TOP)
                    scale[2 * t + side, :, half:] = number

            far = jnp.where(z < n // 2, 1, 0)
            for side in (far, 1 - far):

                @pl.when(z != owner_of(side, t))
                def _(side=side):
                    for copy in code_copies(side, t, z):
                        copy.start()

        tt = s - LAG

        @pl.when(jnp.logical_and(tt >= 0, tt < steps))
        def _():
            row = row_of(tt)
            for side in range(2):
                for owner, is_early in ((ends[side][1], True), (middles[side][1], False)):
                    right_time = tt < early if is_early else tt >= early

                    @pl.when(jnp.logical_and(z == owner, right_time))
                    def _(side=side, owner=owner):
                        total = part[row]
                        number = counts[row]
                        all_of(code_in.at[row, pl.ds(0, n - 1)], drecv.at[0, row])
                        all_of(scale_in.at[row, pl.ds(0, n - 1)], drecv.at[1, row])
                        for source in range(n):
                            if source != owner:
                                code = code_in[row, source].astype(jnp.int32)
                                code = code.astype(jnp.float32)
                                total = total + code * scale_in[row, source, :, :half]
                                number = number + scale_in[row, source, :, half:]
                        part[row] = total
                        counts[row] = number

        @pl.when(s < steps)
        def _():
            @pl.when(s < steps - 1)
            def _():
                all_of(halo.at[s], hrecv.at[s])

            @pl.when(s == steps - 1)
            def _():
                all_of(ext.at[0, pl.ds(0, 4 * w - 2)], hrecv.at[s])

            ext[:, pl.ds(width - w * (s + 1), w)] = halo[s, 0]
            ext[:, pl.ds(width + columns + w * s, w)] = halo[s, 1]
            one_beam(theirs(s))
            pair_copy(s).start()
            one_beam(mine(s))

        return carry

    @pl.when(jnp.logical_not(is_mid))
    def _():
        pl.semaphore_wait(hello, 1)

    lax.fori_loop(0, steps + LAG, slot, 0)

    items = pay.shape[0]

    def send_copy(at, place, core, side, buf, which):
        return pltpu.make_async_remote_copy(
            src_ref=pay.at[: buf.shape[1]],
            dst_ref=buf.at[2 * side + c],
            send_sem=gsend.at[at // 4 + at // 6],
            recv_sem=grecv.at[which],
            device_id={"rng": 2 * place + core},
            device_id_type=MESH,
        )

    solve_kernel(part, solved, stack, turned, hr, hi, xr, xi, yr, yi)
    flipped = solved[...].T
    scaled = []
    for t in range(part.shape[0]):
        scaled.append(flipped[side_chan * t : side_chan * (t + 1)] * counts[t])
    spare = items - len(scaled) * side_chan
    if spare:
        scaled.append(jnp.zeros((spare, lanes), jnp.float32))
    full = jnp.concatenate(scaled, 0)
    lane = lax.broadcasted_iota(jnp.int32, (items, lanes), 1)
    hi_part = full.astype(jnp.bfloat16).astype(jnp.float32)
    rest = full - hi_part
    mid_part = rest.astype(jnp.bfloat16).astype(jnp.float32)
    lo_part = rest - mid_part
    split = jnp.where(
        lane == 2 * dof + 1, mid_part, jnp.where(lane == 2 * dof + 2, lo_part, hi_part)
    )
    pay[...] = split.astype(jnp.bfloat16)
    for which, (places, buf) in enumerate(((ends, gat_e), (middles, gat_l))):
        for side, owner in places:

            @pl.when(z == owner)
            def _(side=side, buf=buf, which=which, owner=owner):
                order = sorted(range(n), key=lambda place: -abs(place - owner))
                peers = [(place, core) for place in order for core in (c, 1 - c)]
                peers.remove((owner, c))
                for at, (place, core) in enumerate(peers):
                    send_copy(at, place, core, side, buf, which).start()
                buf[2 * side + c] = pay[: buf.shape[1]]

    freq = (lax.broadcasted_iota(jnp.int32, (num_chan, taps), 1) // num_sel).astype(jnp.float32)
    centres = chan_ref[...].astype(jnp.float32)

    def tile_copy(side, b, group):
        target = ahead if side else behind
        buf = pl_left if side else pl_right
        return pltpu.make_async_remote_copy(
            src_ref=pw.at[b + 1],
            dst_ref=buf.at[b + 1],
            send_sem=lsend.at[side],
            recv_sem=lrecv.at[side, group],
            device_id={"rng": target},
            device_id_type=MESH,
        )

    def az_copy(up):
        return pltpu.make_async_remote_copy(
            src_ref=pw.at[beams if up else 1],
            dst_ref=pw.at[0 if up else beams + 1],
            send_sem=tsend,
            recv_sem=trecv,
            device_id={"az": az_next if up else az_prev},
            device_id_type=MESH,
        )

    def corner_copy(up, side):
        buf = pl_left if side else pl_right
        return pltpu.make_async_remote_copy(
            src_ref=pw.at[beams if up else 1],
            dst_ref=buf.at[0 if up else beams + 1],
            send_sem=lsend.at[side],
            recv_sem=arecv.at[side],
            device_id={
                "az": az_next if up else az_prev,
                "rng": ahead if side else behind,
            },
            device_id_type=MESH,
        )

    def one_power(b, tiles, t, core, group, edge=None):
        start = pl.multiple_of(t * side_chan, side_chan)
        both = [tiles[2 * side + core, pl.ds(start, side_chan), :] for side in range(2)]
        wide = jnp.concatenate(both, 0)
        tail = wide[:, 2 * BINS * lanes :]
        quiet = tail[:, :1] + tail[:, 1:2] + tail[:, 2:3]
        centre = jnp.sum(jnp.where(blane == az * beams + b, centres, 0.0), 1, keepdims=True)
        hits = []
        for q in range(BINS):
            f = centre + (q - BINS // 2)
            f = jnp.where(f < 0.0, f + pulses, jnp.where(f >= pulses, f - pulses, f))
            hits.append(freq == f)
        planes = []
        for p in range(2):
            plane = jnp.zeros((num_chan, taps), jnp.float32)
            for q in range(BINS):
                at = (p * BINS + q) * lanes
                piece = wide[:, at : at + lanes]
                tiled = jnp.concatenate([piece] * (taps // lanes), 1)
                plane = jnp.where(hits[q], tiled, plane)
            planes.append(plane)
        top = jnp.concatenate([planes[0], planes[1]], 1)
        bottom = jnp.concatenate([-planes[1], planes[0]], 1)
        lhs = jnp.concatenate([top, bottom], 0).astype(jnp.bfloat16)
        flat = v_all[b].reshape(2 * taps, cells)
        proj = jnp.dot(lhs, flat, preferred_element_type=jnp.float32)
        p0 = proj[:num_chan]
        p1 = proj[num_chan:]
        pw[b + 1] = (p0 * p0 + p1 * p1) / quiet
        if edge is not None:
            up, first = edge

            @pl.when(first)
            def _():
                @pl.when(me < size - 1)
                def _():
                    corner_copy(up, 1).start()

                @pl.when(me > 0)
                def _():
                    corner_copy(up, 0).start()

                az_copy(up).start()

        @pl.when(me < size - 1)
        def _():
            tile_copy(1, b, group).start()

        @pl.when(me > 0)
        def _():
            tile_copy(0, b, group).start()

    def spread_weights(which, buf, tiles):
        mine_too = is_mid if which else jnp.logical_not(is_mid)
        others = 2 * len(middles)
        for own in range(2):

            @pl.when(mine_too if own else jnp.logical_not(mine_too))
            def _(own=own):
                all_of(buf.at[pl.ds(0, others - own)], grecv.at[which])

        flat = buf[...].reshape(others * buf.shape[1], lanes)
        wide = jnp.dot(flat, spread_ref[...], preferred_element_type=jnp.float32)
        tiles[...] = wide.reshape(tiles.shape)

    def early_power(t, carry):
        one_power(steps - 1 - t, tiles_e, t, 0, 0)
        one_power(steps + t, tiles_e, t, 1, 0)
        return carry

    def late_power(i, carry):
        one_power(i, tiles_l, late - 1 - i, 0, 1, (0, i == 0))
        one_power(beams - 1 - i, tiles_l, late - 1 - i, 1, 1, (1, i == 0))

        return carry

    spread_weights(0, gat_e, tiles_e)
    lax.fori_loop(0, early, early_power, 0)
    spread_weights(1, gat_l, tiles_l)
    lax.fori_loop(0, late, late_power, 0)

    lane = lax.broadcasted_iota(jnp.int32, (num_chan, cells), 1)

    def row_sum(i):
        mid = pw[i]
        back = pltpu.roll(jnp.where(lane == cells - 1, pl_left[i], mid), 1, 1)
        fore = pltpu.roll(jnp.where(lane == 0, pl_right[i], mid), cells - 1, 1)
        return back + mid + fore

    def finish(which, group):
        @pl.when(me > 0)
        def _():
            all_of(pl_left.at[pl.ds(0, len(group))], lrecv.at[1, which])

        @pl.when(me < size - 1)
        def _():
            all_of(pl_right.at[pl.ds(0, len(group))], lrecv.at[0, which])

        for b in group:
            rows[b + 1] = row_sum(b + 1)

    def smooth(b):
        out_ref[b] = (rows[b] + rows[b + 1] + rows[b + 2]) / 9.0

    def write(first, count):
        part_of = pl.ds(first, count)
        copy = pltpu.make_async_copy(
            out_ref.at[part_of], out_hbm.at[part_of], osem
        )
        copy.start()

    finish(0, range(late, beams - late))
    for b in range(late + 1, beams - late - 1):
        smooth(b)
    write(late + 1, beams - 2 * late - 2)
    outer = [*range(late), *range(beams - late, beams)]
    finish(1, outer)
    for b in range(1, late + 1):
        smooth(b)
        smooth(beams - 1 - b)
    write(1, late)
    write(beams - 1 - late, late)
    all_of(pw.at[pl.ds(0, 2)], trecv)

    @pl.when(me > 0)
    def _():
        all_of(pl_left.at[pl.ds(0, 2)], arecv.at[1])

    @pl.when(me < size - 1)
    def _():
        all_of(pl_right.at[pl.ds(0, 2)], arecv.at[0])

    rows[0] = row_sum(0)
    rows[beams + 1] = row_sum(beams + 1)
    smooth(0)
    smooth(beams - 1)
    write(0, 1)
    write(beams - 1, 1)

    all_of(ext.at[0, pl.ds(0, 4 * width - 2)], hsend)
    all_of(pair, psend)
    mask_copy.wait_send()
    for own, buf, here in (
        (early, gat_e, jnp.logical_not(is_mid)),
        (late, gat_l, is_mid),
    ):

        @pl.when(here)
        def _(own=own, buf=buf):
            for i, ref in enumerate((coded, scale)):
                all_of(ref.at[pl.ds(0, 2 * steps - own)], dsend.at[i])
            all_of(buf, gsend.at[0])
            all_of(buf.at[pl.ds(0, 2)], gsend.at[1])
            all_of(buf.at[0], gsend.at[2])

    all_of(pw.at[pl.ds(0, 2)], tsend)
    for side in range(2):

        @pl.when(me < size - 1 if side else me > 0)
        def _(side=side):
            all_of(pw, lsend.at[side])

    pltpu.make_async_copy(out_ref, out_hbm, osem).wait()


def chain(echoes, arc_start, arc_offsets, doppler_bins, steer_angles, train_mask, early):
    columns, num_pulses, cells = echoes.shape[1:]
    num_sel = arc_offsets.shape[1]
    num_chan = doppler_bins.shape[1]
    size = lax.axis_size("rng")
    beams = BEAMS // lax.axis_size("az")
    dof = BINS * num_sel
    steps = beams // 2
    n = size // 2
    width = ARC // 2
    w = width // steps
    side_chan = num_chan // 2
    half = side_chan * dof
    late = steps - early
    most = max(early, late)
    items = most * side_chan
    early_rows = -(-early * side_chan // 16) * 16
    late_rows = -(-late * side_chan // 16) * 16
    most_rows = max(early_rows, late_rows)
    lanes = 128
    with jax.ensure_compile_time_eval():
        table_re, table_im = doppler_table(num_pulses)
        table = np.block([[table_re, -table_im], [table_im, table_re]])
    source = np.arange(lanes)[:, None]
    target = np.arange((2 * BINS + 1) * lanes)[None, :]
    block, place = target // lanes, target % lanes
    wanted = np.where(
        block < 2 * BINS, block * num_sel + place % num_sel, 2 * dof + np.minimum(place, 3)
    )
    spread = jnp.asarray(source == wanted, jnp.bfloat16)
    vm = pltpu.VMEM
    sm = pltpu.SMEM
    dma = pltpu.SemaphoreType.DMA
    f32 = jnp.float32
    bf16 = jnp.bfloat16
    i32 = jnp.int32
    i16 = jnp.int16
    tile = (num_chan, cells)
    scratch = [
        sm(arc_start.shape, i32),
        sm(arc_offsets.T.shape, i32),
        sm(doppler_bins.T.shape, i32),
        sm(train_mask.T.shape, i32),
        vm(steer_angles.T.shape, f32),
        vm(doppler_bins.T.shape, i32),
        vm(table.shape, bf16),
        vm(spread.shape, bf16),
        vm((2,) + steer_angles.T.shape, f32),
        vm((2, columns + 2 * width, num_pulses, cells), bf16),
        vm((steps, 2, 2, w, num_pulses, cells), bf16),
        vm((beams, 2, num_pulses, num_sel, cells), bf16),
        vm((beams, 2, dof, half), f32),
        vm((steps, 2, dof, half), f32),
        vm((2 * steps, dof, half), i16),
        vm((2 * steps, 1, half + lanes), f32),
        vm((most, n, dof, half), i16),
        vm((most, n, 1, half + lanes), f32),
        vm((most, dof, half), f32),
        vm((lanes, lanes), f32),
        vm((dof, items, dof), f32),
        vm((dof, dof, items), f32),
        vm((dof, dof, items), f32),
        vm((dof, dof, items), f32),
        vm((dof, items), f32),
        vm((dof, items), f32),
        vm((dof, items), f32),
        vm((dof, items), f32),
        vm((2, beams, cells), f32),
        vm((beams, lanes), f32),
        vm((most, 1, lanes), f32),
        vm((most_rows, lanes), bf16),
        vm((4, early_rows, lanes), bf16),
        vm((4, late_rows, lanes), bf16),
        vm((4, early_rows, spread.shape[1]), f32),
        vm((4, late_rows, spread.shape[1]), f32),
        vm((beams + 2,) + tile, f32),
        vm((beams + 2,) + tile, f32),
        vm((beams + 2,) + tile, f32),
        vm((beams + 2,) + tile, f32),
        vm((beams,) + tile, f32),
        dma((9,)),
        dma,
        dma,
        dma((steps,)),
        dma,
        dma((steps,)),
        dma((2,)),
        dma((2, most)),
        dma,
        dma,
        dma((3,)),
        dma((2,)),
        pltpu.SemaphoreType.REGULAR,
        dma((2,)),
        dma((2, 2)),
        dma,
        dma,
        dma((2,)),
    ]
    return pl.pallas_call(
        functools.partial(chain_kernel, early),
        in_specs=[pl.BlockSpec(memory_space=pl.ANY)] * 8,
        out_specs=pl.BlockSpec(memory_space=pl.ANY),
        out_shape=jax.ShapeDtypeStruct((beams,) + tile, f32),
        scratch_shapes=scratch,
        compiler_params=pltpu.CompilerParams(
            collective_id=2, has_side_effects=True, vmem_limit_bytes=CHAIN_VMEM
        ),
        name="chain",
    )(
        arc_start,
        arc_offsets.T,
        doppler_bins.T,
        train_mask.T,
        steer_angles.T,
        echoes,
        jnp.asarray(table),
        spread,
    )


def body(echoes, arc_start, arc_offsets, doppler_bins, steer_angles, train_mask):
    columns = echoes.shape[1]
    num_pulses = echoes.shape[2]
    cells = echoes.shape[3]
    num_sel = arc_offsets.shape[1]
    chan_count = doppler_bins.shape[1]
    cycle_size = lax.axis_size("az")
    cycle_pos = lax.axis_index("az")
    rng_size = lax.axis_size("rng")
    beam_count = BEAMS // cycle_size
    item_count = beam_count * chan_count
    dof = BINS * num_sel
    pairs = beam_count // 2
    if (
        columns == ARC
        and beam_count % 2 == 0
        and pairs * (COLS // BEAMS) == ARC // 2
        and ARC // 2 // pairs > 1
        and rng_size == 8
        and cycle_size > 2
        and cells == 128
        and chan_count % 16 == 0
        and chan_count // 2 * dof % 128 == 0
        and 2 * dof + 8 <= 128
        and dof % 16 == 0
        and pairs * (chan_count // 2) <= 128
        and pairs > LATE
        and rng_size // 2 > 3
    ):
        return chain(
            echoes, arc_start, arc_offsets, doppler_bins, steer_angles, train_mask, pairs - LATE
        )
    table_re, table_im = doppler_table(num_pulses)
    table = jnp.concatenate(
        [jnp.concatenate([table_re, -table_im], 1), jnp.concatenate([table_im, table_re], 1)], 0
    )

    def own(x):
        return lax.dynamic_slice_in_dim(x, cycle_pos * beam_count, beam_count, axis=0)

    arc_first = (own(arc_start) - cycle_pos * columns + ARC // 2) % COLS
    col_index = arc_first[:, None] + own(arc_offsets)
    bins_own = own(doppler_bins)
    angles = own(steer_angles)
    block_count = train_mask.shape[1]
    cell_mask = (
        jnp.broadcast_to(train_mask[:, :, None], (beam_count, block_count, BLK))
        .reshape(beam_count, 1, block_count * BLK)
        .astype(jnp.bfloat16)
    )
    smem = pl.BlockSpec(memory_space=pltpu.SMEM)

    def snap_gram(extended, first, last, base):
        share = last - first
        ext_cols = extended.shape[1]
        return pl.pallas_call(
            snap_gram_kernel,
            grid=(share,),
            in_specs=[
                smem,
                smem,
                smem,
                smem,
                pl.BlockSpec((2, ext_cols, num_pulses, cells), lambda b: (0, 0, 0, 0)),
                pl.BlockSpec(table.shape, lambda b: (0, 0)),
                pl.BlockSpec((1, 1, cells), lambda b: (b, 0, 0)),
            ],
            out_specs=[
                pl.BlockSpec((1, 2, num_pulses, num_sel, cells), lambda b: (b, 0, 0, 0, 0)),
                pl.BlockSpec((1, dof, chan_count * dof), lambda b: (b, 0, 0)),
            ],
            out_shape=[
                jax.ShapeDtypeStruct((share, 2, num_pulses, num_sel, cells), jnp.bfloat16),
                jax.ShapeDtypeStruct((share, dof, chan_count * dof), jnp.float32),
            ],
            compiler_params=pltpu.CompilerParams(vmem_limit_bytes=VMEM_LIMIT),
            cost_estimate=pl.CostEstimate(
                flops=share * 600_000_000, bytes_accessed=share * 1_500_000, transcendentals=0
            ),
            name="snap_gram",
        )(
            col_index[first:last] - base,
            bins_own[first:last],
            jnp.cos(angles)[first:last],
            jnp.sin(angles)[first:last],
            extended,
            table,
            cell_mask[first:last],
        )

    width = ARC // 2
    forward = [(i, (i + 1) % cycle_size) for i in range(cycle_size)]
    backward = [(target, source) for source, target in forward]
    low = lax.ppermute(echoes[:, columns - width :], "az", forward)
    high = lax.ppermute(echoes[:, :width], "az", backward)
    step = COLS // BEAMS
    half = beam_count // 2
    if (half - 1) * step + step - 1 + ARC - 1 < width + columns and half * step >= width:
        v_lo, gram_lo = snap_gram(jnp.concatenate([low, echoes], 1), 0, half, 0)
        high, v_lo, gram_lo = lax.optimization_barrier((high, v_lo, gram_lo))
        v_hi, gram_hi = snap_gram(jnp.concatenate([echoes, high], 1), half, beam_count, width)
        v_parts = (v_lo, v_hi)
        grams = (gram_lo, gram_hi)
        if rng_size % 4 or item_count // rng_size < chan_count:
            grams = (jnp.concatenate(grams, 0),)
    else:
        v_one, gram_one = snap_gram(jnp.concatenate([low, echoes, high], 1), 0, beam_count, 0)
        v_parts = (v_one,)
        grams = (gram_one,)

    per = item_count // rng_size
    if per < chan_count:
        split = chan_count // per
        gram = grams[0].reshape(beam_count, dof, split, per * dof)
        grams = (jnp.swapaxes(gram, 1, 2).reshape(beam_count * split, dof, per * dof),)
        width = per
    else:
        width = chan_count
    vm = pltpu.VMEM
    dma = pltpu.SemaphoreType.DMA
    line = rng_size // 2
    chunk = (grams[0].shape[0] * len(grams) // rng_size, dof, grams[0].shape[2])
    part = pl.pallas_call(
        functools.partial(scatter_kernel, line, len(grams)),
        in_specs=[pl.BlockSpec(memory_space=vm)] * len(grams),
        out_specs=pl.BlockSpec(memory_space=vm),
        out_shape=jax.ShapeDtypeStruct(chunk, jnp.float32),
        scratch_shapes=[vm((line,) + chunk, jnp.float32)] * 4 + [dma((line,))] * 6,
        compiler_params=pltpu.CompilerParams(
            collective_id=0, has_side_effects=True, vmem_limit_bytes=VMEM_LIMIT
        ),
        name="scatter",
    )(*[g.reshape((rng_size // len(grams),) + chunk) for g in grams])
    solved = pl.pallas_call(
        solve_kernel,
        out_shape=jax.ShapeDtypeStruct((2 * dof + 8, per), jnp.float32),
        scratch_shapes=[
            vm((dof, per, dof), jnp.float32),
            vm((dof, dof, per), jnp.float32),
            vm((dof, dof, per), jnp.float32),
            vm((dof, dof, per), jnp.float32),
            vm((dof, per), jnp.float32),
            vm((dof, per), jnp.float32),
            vm((dof, per), jnp.float32),
            vm((dof, per), jnp.float32),
        ],
        compiler_params=pltpu.CompilerParams(vmem_limit_bytes=VMEM_LIMIT),
        name="solve",
    )(part)
    lanes = 128
    local_count = (BLK * jnp.sum(train_mask, axis=1)).astype(jnp.float32)
    pad_rows = -per % 8
    payload = jnp.concatenate(
        [
            jnp.pad(solved.T, ((0, pad_rows), (0, lanes - solved.shape[0]))),
            jnp.broadcast_to(local_count[:, None], (beam_count, lanes)),
        ],
        0,
    )
    halves = len(v_parts)
    any_spec = pl.BlockSpec(memory_space=pl.ANY)
    block = (chan_count, cells)
    out = pl.pallas_call(
        functools.partial(apply_kernel, halves, per, dof),
        in_specs=[pl.BlockSpec(memory_space=vm)] * 2 + [any_spec] * halves,
        out_specs=pl.BlockSpec(memory_space=vm),
        out_shape=jax.ShapeDtypeStruct((beam_count,) + block, jnp.float32),
        scratch_shapes=[
            vm((beam_count, 2, num_pulses, num_sel, cells), jnp.bfloat16),
            vm((rng_size,) + payload.shape, jnp.float32),
            vm((beam_count,) + block, jnp.float32),
            vm((2, 8, item_count), jnp.float32),
            vm((2, 8, item_count), jnp.float32),
            vm((beam_count,) + block, jnp.float32),
            vm(block, jnp.float32),
            vm(block, jnp.float32),
            dma((halves,)),
            dma((rng_size,)),
            dma((rng_size,)),
            dma((2,)),
            dma((2,)),
            dma((2,)),
            dma((2,)),
        ],
        compiler_params=pltpu.CompilerParams(
            collective_id=1, has_side_effects=True, vmem_limit_bytes=VMEM_LIMIT
        ),
        name="apply",
    )(payload, bins_own[:, :, None], *v_parts)
    return out


def solution(mesh):
    return jax.shard_map(
        body,
        mesh=mesh,
        in_specs=(P(None, "az", None, "rng"), P(), P(), P(), P(), P("az", "rng")),
        out_specs=P("az", None, "rng"),
        check_vma=False,
    )
```
